32 devices in a mesh: view: 8 (over y, x, core), band: 4 (over z).
Axes of the slice: x: 2, y: 2, z: 4, core: 2. Of those that a mesh axis runs over, the one named last changes fastest.
Arguments:
- gaussians: float32 [512, 62, 256], P(('view', 'band')), may hold values from -8 to 128, as said below
- first_moment: float32 [512, 62, 256], P(('view', 'band')), may hold values from -0.6 to 0.6
- second_moment: float32 [512, 62, 256], P(('view', 'band')), may hold values from 0.0001 to 0.1
- camera: float32 [8, 9], P('view'), may hold values from -352 to 352, as said below
- target: float32 [8, 3, 64, 128], P('view', None, 'band'), may hold values from 0 to 1
- block_list: int32 [8, 4, 16], P('view', 'band'), may hold values from -1 to 511, as said below
- block_count: int32 [8, 4], P('view', 'band'), may hold values from 12 to 16, as said below
- tile_start: int32 [8, 4, 8], P('view', 'band'), may hold values from 0 to 15, as said below
- tile_end: int32 [8, 4, 8], P('view', 'band'), may hold values from 1 to 16, as said below
Outputs:
- new_gaussians: float32 [512, 62, 256], P(('view', 'band'))
- new_first_moment: float32 [512, 62, 256], P(('view', 'band'))
- new_second_moment: float32 [512, 62, 256], P(('view', 'band'))
- mean_loss: float32 [], replicated
- grads: float32 [512, 62, 256], P(('view', 'band'))
The draws below stay inside these ranges and needn't reach their ends.
Inputs may be any that keep to these rules, and one draw needn't show every extreme that they name: Block k is held by device k // 16, devices counted with view slowest. Entry i of block_list[v, b] is a block for i < block_count[v, b] and -1 after; the live entries of one band are distinct, at most 1 of them are held by one device, and in every band some device holds exactly 1 of them. `block_count`: some band has exactly 16. tile_start < tile_end <= block_count of the band; tile_end - tile_start is at most 2, and exactly 2 for some tile of every band; the tiles of a band together cover every live position. `tile_end`: see tile_start. `gaussians`: component 9 of every Gaussian lies in [1, 2]; components 6 to 8 lie in [0, 2]. `camera`: A0 x A1 has a third entry of 0.6 or more.
All inputs are finite; a program needn't handle non-finite values.
Results may differ from the reference program's by a relative error of at most 0.0003.
Values sent between devices are 32-bit elements; how exact they have to be, the bound alone decides.
A program may use at most 128 MiB of HBM per device.

```python
import math
import jax
import jax.numpy as jnp
import numpy as np
from jax import lax

PARAMS = 62
BLOCK = 256
TILE = 16
ROWS = 16
COLS = 128
BLK_DEV = 16
LIST = 16
TILE_MOST = 2
VIEWS = 8
BANDS = 4
IMG_ROWS = 64
NBLK = 512
TILES = 8
CAP = 1
DEVICES = 32


def lists_helper(key):
    base_key = jax.random.fold_in(key, 7311)
    key_full, key_count, key_device = jax.random.split(base_key, 3)
    dev_total = VIEWS * BANDS
    slot_total = DEVICES * CAP
    counts = jax.random.randint(key_count, (dev_total,), 3 * LIST // 4, LIST + 1)
    full_device = jax.random.randint(key_full, (), 0, dev_total)
    counts = jnp.where(jnp.arange(dev_total) == full_device, LIST, counts)

    def draw_device(device_key, live_count):
        key_list = jax.random.split(device_key, 8)
        full_owner = jax.random.randint(key_list[0], (), 0, DEVICES)
        scores = jax.random.permutation(key_list[1], slot_total)
        slot_ids = jnp.arange(slot_total)
        scores = jnp.where(slot_ids // CAP == full_owner, scores - slot_total, scores)
        ranking = jnp.argsort(scores, stable=True)
        chosen = ranking[:LIST]
        half_list = LIST // 2
        front_half = chosen[:half_list][jax.random.permutation(key_list[2], half_list)]
        back_half = chosen[half_list:][jax.random.permutation(key_list[3], LIST - half_list)]
        chosen = jnp.concatenate([front_half, back_half])
        owners = chosen // CAP
        slot_rank = chosen % CAP
        local_perm = jax.vmap(lambda subkey: jax.random.permutation(subkey, BLK_DEV))(jax.random.split(key_list[4], DEVICES))
        local_ids = local_perm[owners, slot_rank]
        block_ids = owners * BLK_DEV + local_ids
        block_ids = jnp.where(jnp.arange(LIST) < live_count, block_ids, -1)
        tile_index = jnp.arange(TILES)
        low_end = tile_index * live_count // TILES
        high_end = (tile_index + 1) * live_count // TILES
        length = jax.random.randint(key_list[5], (TILES,), jnp.maximum(high_end - low_end, 1), TILE_MOST + 1)
        forced = jax.random.randint(key_list[6], (), 0, TILES)
        length = jnp.where(tile_index == forced, TILE_MOST, length)
        first_ok = jnp.maximum(0, high_end - length)
        last_ok = jnp.minimum(low_end, live_count - length)
        starts = jax.random.randint(key_list[7], (TILES,), first_ok, last_ok + 1)
        return (block_ids, starts, starts + length)
    block_ids, starts, endings = jax.vmap(draw_device)(jax.random.split(key_device, dev_total), counts)
    return (block_ids.reshape(VIEWS, BANDS, LIST).astype(jnp.int32), counts.reshape(VIEWS, BANDS).astype(jnp.int32), starts.reshape(VIEWS, BANDS, TILES).astype(jnp.int32), endings.reshape(VIEWS, BANDS, TILES).astype(jnp.int32))


def draw_block_list(key, part):
    return lists_helper(key)[0]


def draw_block_count(key, part):
    return lists_helper(key)[1]


def draw_tile_start(key, part):
    return lists_helper(key)[2]


def draw_tile_end(key, part):
    return lists_helper(key)[3]


def draw_gaussians(key, part):
    key_list = jax.random.split(jax.random.fold_in(key, 23), 8)
    grid_shape = (NBLK, BLOCK)
    extent = jnp.array([COLS * 1.0, IMG_ROWS * 1.0, 64.0], jnp.float32)[:, None, None]
    centre = jax.random.uniform(key_list[0], (3,) + grid_shape) * extent
    velocity = jnp.clip(2.0 * jax.random.normal(key_list[1], (3,) + grid_shape), -8.0, 8.0)
    log_scale = jax.random.uniform(key_list[2], (3,) + grid_shape, minval=math.log(1.2), maxval=math.log(4.0))
    quat_real = jax.random.uniform(key_list[3], (1,) + grid_shape, minval=1.0, maxval=2.0)
    quat_vec = jnp.clip(0.5 * jax.random.normal(key_list[4], (3,) + grid_shape), -2.0, 2.0)
    opacity = jax.random.uniform(key_list[5], (1,) + grid_shape, minval=-4.5, maxval=-2.5)
    sh_base = jnp.clip(0.6 * jax.random.normal(key_list[6], (3,) + grid_shape), -3.0, 3.0)
    sh_rest = jnp.clip(0.25 * jax.random.normal(key_list[7], (45,) + grid_shape), -1.5, 1.5)
    stacked = jnp.concatenate([centre, velocity, log_scale, quat_real, quat_vec, opacity, sh_base, sh_rest], axis=0)
    return stacked.transpose(1, 0, 2).astype(jnp.float32)


def draw_camera(key, part):
    key_list = jax.random.split(jax.random.fold_in(key, 41), 5)
    tilt_range = 0.3
    spin_angle = jax.random.uniform(key_list[0], (VIEWS,), minval=-0.15, maxval=0.15)
    tilt_a = jax.random.uniform(key_list[1], (VIEWS,), minval=-tilt_range, maxval=tilt_range)
    tilt_b = jax.random.uniform(key_list[2], (VIEWS,), minval=-tilt_range, maxval=tilt_range)
    zoom_factor = jax.random.uniform(key_list[3], (VIEWS,), minval=0.9, maxval=1.1)
    view_time = jax.random.uniform(key_list[4], (VIEWS,))
    row_top = zoom_factor[:, None] * jnp.stack([jnp.cos(spin_angle), -jnp.sin(spin_angle), tilt_a], axis=1)
    row_low = zoom_factor[:, None] * jnp.stack([jnp.sin(spin_angle), jnp.cos(spin_angle), tilt_b], axis=1)
    centre = jnp.array([COLS * 0.5, IMG_ROWS * 0.5, 32.0], jnp.float32)
    off_top = COLS * 0.5 - jnp.sum(row_top * centre[None, :], axis=1)
    off_low = IMG_ROWS * 0.5 - jnp.sum(row_low * centre[None, :], axis=1)
    return jnp.concatenate([row_top, row_low, off_top[:, None], off_low[:, None], view_time[:, None]], axis=1).astype(jnp.float32)


def block_scale(key, shape, pieces, low, top_value):
    loudness = 1.0
    for axis_at, blocks in pieces:
        heights = jax.random.uniform(jax.random.fold_in(jax.random.fold_in(key, 6), axis_at), (blocks,), jnp.float32, low / len(pieces), top_value / len(pieces))
        loudness = loudness * jnp.repeat(jnp.exp(heights), shape[axis_at] // blocks).reshape((-1,) + (1,) * (len(shape) - 1 - axis_at))
    return loudness


def noise(rng, shape, scale, reach, shards=(), held_as=jnp.bfloat16):
    entries = jax.random.normal(rng, shape, jnp.float32) * scale
    if len(shards) > 0:
        entries = block_scale(rng, shape, shards, -0.22, 0.18) * entries
    return jnp.clip(entries, min=-reach, max=reach).astype(held_as)


def setup_inputs(seed: int = 0) -> dict:
    key_of = jax.random.split(jax.random.key(seed), 10)
    return {
        "gaussians": draw_gaussians(jax.random.fold_in(key_of[9], 71), 0),
        "first_moment": noise(key_of[1], (NBLK, PARAMS, BLOCK), 0.1, 0.6, ((0, 32),), jnp.float32),
        "second_moment": jnp.clip(jnp.exp(math.log(0.1) - 6.9077553 * jax.random.uniform(key_of[2], (NBLK, PARAMS, BLOCK), jnp.float32) ** block_scale(key_of[2], (NBLK, PARAMS, BLOCK), ((0, 32),), -0.2, 0.2)), 0.0001, 0.1),
        "camera": draw_camera(jax.random.fold_in(key_of[9], 71), 0),
        "target": jnp.clip(1.0 * jax.random.uniform(key_of[4], (VIEWS, 3, IMG_ROWS, COLS), jnp.float32) ** block_scale(key_of[4], (VIEWS, 3, IMG_ROWS, COLS), ((0, 8), (2, 4)), -0.2, 0.2), 0.0, 1.0),
        "block_list": draw_block_list(jax.random.fold_in(key_of[9], 71), 0),
        "block_count": draw_block_count(jax.random.fold_in(key_of[9], 71), 0),
        "tile_start": draw_tile_start(jax.random.fold_in(key_of[9], 71), 0),
        "tile_end": draw_tile_end(jax.random.fold_in(key_of[9], 71), 0),
    }


HIGHEST_MODE = lax.Precision.HIGHEST
SSIM_WEIGHT = 0.2
ABS_WEIGHT = 0.8
STAB_MEAN = 0.0001
STAB_VAR = 0.0009
BIAS_FIRST = 1.0 - math.exp(100.0 * math.log(0.9))
BIAS_SECOND = 1.0 - math.exp(100.0 * math.log(0.999))
SH_ZERO = 0.28209479177387814
SH_ONE = 0.4886025119029199
SH_TWO = [1.0925484305920792, -1.0925484305920792, 0.31539156525252005, -1.0925484305920792, 0.5462742152960396]
SH_THREE = [-0.5900435899266435, 2.890611442640554, -0.4570457994644658, 0.3731763325901154, -0.4570457994644658, 1.445305721320277, -0.5900435899266435]

def learning_rates():
    return np.concatenate([np.full(6, 0.016), np.full(3, 0.005), np.full(4, 0.001), np.full(1, 0.05), np.full(3, 0.0025), np.full(45, 0.000125)]).astype(np.float32)

def kernel_taps():
    raw_taps = [math.exp(-(offset * offset) / 4.5) for offset in range(-5, 6)]
    tap_total = sum(raw_taps)
    return [raw_tap / tap_total for raw_tap in raw_taps]

def smooth(source, rows_out):
    kernel = kernel_taps()
    rows_done = kernel[0] * source[..., 0:rows_out, :]
    for offset in range(1, 11):
        rows_done = rows_done + kernel[offset] * source[..., offset:offset + rows_out, :]
    cols_n = source.shape[-1]
    padded = jnp.pad(rows_done, [(0, 0)] * (source.ndim - 1) + [(5, 5)])
    result = kernel[0] * padded[..., 0:cols_n]
    for offset in range(1, 11):
        result = result + kernel[offset] * padded[..., offset:offset + cols_n]
    return result

def ssim_value(mean_x, mean_y, square_x, square_y, cross_xy):
    var_x = square_x - mean_x * mean_x
    var_y = square_y - mean_y * mean_y
    covar = cross_xy - mean_x * mean_y
    upper = (2.0 * mean_x * mean_y + STAB_MEAN) * (2.0 * covar + STAB_VAR)
    lower = (mean_x * mean_x + mean_y * mean_y + STAB_MEAN) * (var_x + var_y + STAB_VAR)
    return upper / lower

def ssim_terms(pred_ext, target_ext, rows_out):
    mean_x = smooth(pred_ext, rows_out)
    mean_y = smooth(target_ext, rows_out)
    square_x = smooth(pred_ext * pred_ext, rows_out)
    square_y = smooth(target_ext * target_ext, rows_out)
    cross_xy = smooth(pred_ext * target_ext, rows_out)
    ssim_map, pullback = jax.vjp(ssim_value, mean_x, mean_y, square_x, square_y, cross_xy)
    partials = pullback(jnp.full_like(ssim_map, -SSIM_WEIGHT / 3.0))
    return (ssim_map, partials[0], partials[2], partials[4])

def harmonics(facing):
    dir_x, dir_y, dir_z = (facing[0], facing[1], facing[2])
    sq_x, sq_y, sq_z = (dir_x * dir_x, dir_y * dir_y, dir_z * dir_z)
    return jnp.stack([SH_ZERO + 0.0 * dir_x, -SH_ONE * dir_y, SH_ONE * dir_z, -SH_ONE * dir_x, SH_TWO[0] * dir_x * dir_y, SH_TWO[1] * dir_y * dir_z, SH_TWO[2] * (2.0 * sq_z - sq_x - sq_y), SH_TWO[3] * dir_x * dir_z, SH_TWO[4] * (sq_x - sq_y), SH_THREE[0] * dir_y * (3.0 * sq_x - sq_y), SH_THREE[1] * dir_x * dir_y * dir_z, SH_THREE[2] * dir_y * (4.0 * sq_z - sq_x - sq_y), SH_THREE[3] * dir_z * (2.0 * sq_z - 3.0 * sq_x - 3.0 * sq_y), SH_THREE[4] * dir_x * (4.0 * sq_z - sq_x - sq_y), SH_THREE[5] * dir_z * (sq_x - sq_y), SH_THREE[6] * dir_x * (sq_x - 3.0 * sq_y)])

def project(window, cam_row):
    affine = cam_row[0:6].reshape(2, 3)
    cam_time = cam_row[8]
    centre = [window[:, axis_k, :] + cam_time * window[:, 3 + axis_k, :] for axis_k in range(3)]
    col_pos = affine[0, 0] * centre[0] + affine[0, 1] * centre[1] + affine[0, 2] * centre[2] + cam_row[6]
    row_pos = affine[1, 0] * centre[0] + affine[1, 1] * centre[1] + affine[1, 2] * centre[2] + cam_row[7]
    scales = [jnp.exp(window[:, 6 + axis_k, :]) for axis_k in range(3)]
    quat_len = jnp.sqrt(window[:, 9, :] * window[:, 9, :] + window[:, 10, :] * window[:, 10, :] + window[:, 11, :] * window[:, 11, :] + window[:, 12, :] * window[:, 12, :])
    quat_r = window[:, 9, :] / quat_len
    quat_i = window[:, 10, :] / quat_len
    quat_j = window[:, 11, :] / quat_len
    quat_k = window[:, 12, :] / quat_len
    rotation = [[1.0 - 2.0 * (quat_j * quat_j + quat_k * quat_k), 2.0 * (quat_i * quat_j - quat_r * quat_k), 2.0 * (quat_i * quat_k + quat_r * quat_j)], [2.0 * (quat_i * quat_j + quat_r * quat_k), 1.0 - 2.0 * (quat_i * quat_i + quat_k * quat_k), 2.0 * (quat_j * quat_k - quat_r * quat_i)], [2.0 * (quat_i * quat_k - quat_r * quat_j), 2.0 * (quat_j * quat_k + quat_r * quat_i), 1.0 - 2.0 * (quat_i * quat_i + quat_j * quat_j)]]
    spread_rows = [[(affine[out_row, 0] * rotation[0][in_col] + affine[out_row, 1] * rotation[1][in_col] + affine[out_row, 2] * rotation[2][in_col]) * scales[in_col] for in_col in range(3)] for out_row in range(2)]
    conic_a = spread_rows[0][0] * spread_rows[0][0] + spread_rows[0][1] * spread_rows[0][1] + spread_rows[0][2] * spread_rows[0][2] + 0.3
    conic_b = spread_rows[0][0] * spread_rows[1][0] + spread_rows[0][1] * spread_rows[1][1] + spread_rows[0][2] * spread_rows[1][2]
    conic_c = spread_rows[1][0] * spread_rows[1][0] + spread_rows[1][1] * spread_rows[1][1] + spread_rows[1][2] * spread_rows[1][2] + 0.3
    determinant = conic_a * conic_c - conic_b * conic_b
    opacity = jax.nn.sigmoid(window[:, 13, :])
    normal = jnp.cross(affine[0], affine[1])
    facing = normal / jnp.sqrt(jnp.sum(normal * normal))
    sh_basis = harmonics(facing)
    sh_coef = window[:, 14:, :].reshape(window.shape[0], 16, 3, window.shape[2])
    colour = 0.5 + jnp.einsum('k,tkcb->ctb', sh_basis, sh_coef, precision=HIGHEST_MODE)
    return (col_pos, row_pos, conic_a, conic_b, conic_c, determinant, opacity, colour)

def render_tile(window, cam_row, first_pos, live_low, live_high, row_start, col_start):
    window_len = window.shape[0]
    block_len = window.shape[2]
    col_pos, row_pos, conic_a, conic_b, conic_c, determinant, opacity, colour = project(window, cam_row)
    positions = first_pos + jnp.arange(window_len, dtype=jnp.int32)
    is_live = (positions >= live_low) & (positions < live_high)
    live_flat = jnp.repeat(is_live, block_len)
    pixels = jnp.arange(TILE * TILE, dtype=jnp.int32)
    pix_row = (row_start + pixels // TILE).astype(jnp.float32) + 0.5
    pix_col = (col_start + pixels % TILE).astype(jnp.float32) + 0.5
    delta_col = pix_col[None, :] - col_pos.reshape(-1)[:, None]
    delta_row = pix_row[None, :] - row_pos.reshape(-1)[:, None]
    exponent = -0.5 * (conic_c.reshape(-1)[:, None] * delta_col * delta_col - 2.0 * conic_b.reshape(-1)[:, None] * delta_col * delta_row + conic_a.reshape(-1)[:, None] * delta_row * delta_row) / determinant.reshape(-1)[:, None]
    alphas = jnp.where(live_flat[:, None], opacity.reshape(-1)[:, None] * jnp.exp(exponent), 0.0)
    keep_log = jnp.log1p(-alphas).reshape(window_len, block_len, -1)
    inner_sum = jnp.cumsum(keep_log, axis=1)
    block_total = inner_sum[:, -1, :]
    outer_sum = jnp.cumsum(block_total, axis=0) - block_total
    log_trans = inner_sum - keep_log + outer_sum[:, None, :]
    weight = alphas * jnp.exp(log_trans.reshape(window_len * block_len, -1))
    return jnp.dot(colour.reshape(3, -1), weight, precision=HIGHEST_MODE)

def tile_frame(tile_index, starts, list_len, row_base):
    tile_cols = COLS // TILE
    first_pos = jnp.minimum(starts[tile_index], list_len - TILE_MOST).astype(jnp.int32)
    row_start = row_base + tile_index // tile_cols * TILE
    col_start = tile_index % tile_cols * TILE
    return (first_pos, row_start, col_start)

def from_tiles(tiles_out):
    tile_rows = ROWS // TILE
    tile_cols = COLS // TILE
    return tiles_out.reshape(tile_rows, tile_cols, 3, TILE, TILE).transpose(2, 0, 3, 1, 4).reshape(3, ROWS, COLS)

def to_tiles(image):
    tile_rows = ROWS // TILE
    tile_cols = COLS // TILE
    return image.reshape(3, tile_rows, TILE, tile_cols, TILE).transpose(1, 3, 0, 2, 4).reshape(tile_rows * tile_cols, 3, TILE * TILE)

def render_band(listed, cam_row, starts, endings, row_base):
    list_len = listed.shape[0]

    def draw_tile(tile_index):
        first_pos, row_start, col_start = tile_frame(tile_index, starts, list_len, row_base)
        window = lax.dynamic_slice_in_dim(listed, first_pos, TILE_MOST, 0)
        return render_tile(window, cam_row, first_pos, starts[tile_index], endings[tile_index], row_start, col_start)
    tiles_out = lax.map(draw_tile, jnp.arange(starts.shape[0], dtype=jnp.int32))
    return from_tiles(tiles_out)

def backward_band(listed, cam_row, starts, endings, row_base, grad_pred):
    list_len = listed.shape[0]
    cot_tiles = to_tiles(grad_pred)

    def tile_back(summed, tile_index):
        first_pos, row_start, col_start = tile_frame(tile_index, starts, list_len, row_base)
        window = lax.dynamic_slice_in_dim(listed, first_pos, TILE_MOST, 0)

        def draw_window(chosen):
            return render_tile(chosen, cam_row, first_pos, starts[tile_index], endings[tile_index], row_start, col_start)
        unused, pullback = jax.vjp(draw_window, window)
        grad_window = pullback(cot_tiles[tile_index])[0]
        current = lax.dynamic_slice_in_dim(summed, first_pos, TILE_MOST, 0)
        summed = lax.dynamic_update_slice_in_dim(summed, current + grad_window, first_pos, 0)
        return (summed, None)
    summed, unused = lax.scan(tile_back, jnp.zeros_like(listed), jnp.arange(starts.shape[0], dtype=jnp.int32))
    return summed

def image_loss(pred_img, target_img):
    pad_rows = [(0, 0), (5, 5), (0, 0)]
    ssim_map, part_mean, part_square, part_cross = ssim_terms(jnp.pad(pred_img, pad_rows), jnp.pad(target_img, pad_rows), IMG_ROWS)
    adjoint = jnp.pad(jnp.stack([part_mean, part_square, part_cross]), [(0, 0), (0, 0), (5, 5), (0, 0)])
    spread = smooth(adjoint, IMG_ROWS)
    error_map = pred_img - target_img
    grad_pred = ABS_WEIGHT / 3.0 * jnp.sign(error_map) + spread[0] + 2.0 * pred_img * spread[1] + target_img * spread[2]
    summed = jnp.sum(ABS_WEIGHT / 3.0 * jnp.abs(error_map) + SSIM_WEIGHT / 3.0 * (1.0 - ssim_map))
    return (summed, grad_pred)

def adam_update(params, moment_one, moment_two, gradient):
    learn_rates = jnp.asarray(learning_rates())[None, :, None]
    new_one = 0.9 * moment_one + 0.1 * gradient
    new_two = 0.999 * moment_two + 0.001 * gradient * gradient
    change = learn_rates * (new_one / BIAS_FIRST) / (jnp.sqrt(new_two / BIAS_SECOND) + 1e-08)
    return (params - change, new_one, new_two)

def reference(gaussians, first_moment, second_moment, camera, target, block_list, block_count, tile_start, tile_end):
    nblk_total = gaussians.shape[0]
    list_len = block_list.shape[2]
    dev_total = VIEWS * BANDS
    list_rows = block_list.reshape(dev_total, list_len)
    counts = block_count.reshape(dev_total)
    starts = tile_start.reshape(dev_total, -1)
    endings = tile_end.reshape(dev_total, -1)
    position = jnp.arange(list_len, dtype=jnp.int32)

    def fetch(device):
        safe_ids = jnp.where(position < counts[device], list_rows[device], 0).astype(jnp.int32)
        return jnp.take(gaussians, safe_ids, axis=0)

    def render_device(device):
        view_index = device // BANDS
        band_index = device % BANDS
        return render_band(fetch(device), camera[view_index], starts[device], endings[device], band_index * ROWS)
    rendered = lax.map(render_device, jnp.arange(dev_total, dtype=jnp.int32))
    images = rendered.reshape(VIEWS, BANDS, 3, ROWS, COLS).transpose(0, 2, 1, 3, 4).reshape(VIEWS, 3, IMG_ROWS, COLS)
    totals, grad_images = jax.vmap(image_loss)(images, target)
    mean_loss = jnp.sum(totals) / (VIEWS * IMG_ROWS * COLS)
    grad_bands = grad_images.reshape(VIEWS, 3, BANDS, ROWS, COLS).transpose(0, 2, 1, 3, 4).reshape(dev_total, 3, ROWS, COLS)

    def accumulate(summed, device):
        view_index = device // BANDS
        band_index = device % BANDS
        grads_list = backward_band(fetch(device), camera[view_index], starts[device], endings[device], band_index * ROWS, grad_bands[device])
        target_rows = jnp.where(position < counts[device], list_rows[device], nblk_total).astype(jnp.int32)
        summed = summed.at[target_rows].add(grads_list, mode='drop')
        return (summed, None)
    gradient, unused = lax.scan(accumulate, jnp.zeros_like(gaussians), jnp.arange(dev_total, dtype=jnp.int32))
    new_params, new_one, new_two = adam_update(gaussians, first_moment, second_moment, gradient)
    return (new_params, new_one, new_two, mean_loss, gradient)
```

```python
import functools
import math

import jax
import jax.numpy as jnp
import numpy as np
from jax import lax
from jax.experimental import pallas as pl
from jax.experimental.pallas import tpu as pltpu
from jax.sharding import PartitionSpec as P

TILE = 16
TILE_MOST = 2
HALO = 5
REACH = 2 * HALO
GEO_REC = 6
PIECES = 4

HIGHEST_MODE = lax.Precision.HIGHEST
SSIM_WEIGHT = 0.2
ABS_WEIGHT = 0.8
STAB_MEAN = 0.0001
STAB_VAR = 0.0009
BIAS_FIRST = 1.0 - math.exp(100.0 * math.log(0.9))
BIAS_SECOND = 1.0 - math.exp(100.0 * math.log(0.999))
LOG2_E = math.log2(math.e)
SH_ZERO = 0.28209479177387814
SH_ONE = 0.4886025119029199
SH_TWO = [
    1.0925484305920792,
    -1.0925484305920792,
    0.31539156525252005,
    -1.0925484305920792,
    0.5462742152960396,
]
SH_THREE = [
    -0.5900435899266435,
    2.890611442640554,
    -0.4570457994644658,
    0.3731763325901154,
    -0.4570457994644658,
    1.445305721320277,
    -0.5900435899266435,
]
F32 = jnp.float32
BF16 = jnp.bfloat16
MESH = pl.DeviceIdType.MESH
NEVER = -1e30


RATES = ((6, 0.016), (9, 0.005), (13, 0.001), (14, 0.05), (17, 0.0025), (62, 0.000125))


def learning_rate(component):
    rate = RATES[-1][1] / BIAS_FIRST
    for end, value in reversed(RATES[:-1]):
        rate = jnp.where(component < end, value / BIAS_FIRST, rate)
    return rate


def kernel_taps():
    raw_taps = [math.exp(-(offset * offset) / 4.5) for offset in range(-5, 6)]
    tap_total = sum(raw_taps)
    return [raw_tap / tap_total for raw_tap in raw_taps]


def up8(value):
    return (value + 7) // 8 * 8


def smoothing_tables(rows, cols, channels):
    taps = kernel_taps()
    in_rows, mid_rows = up8(rows + 2 * REACH), up8(rows + REACH)
    across = np.zeros((cols, cols), np.float32)
    for out in range(cols):
        for m in range(-HALO, HALO + 1):
            if 0 <= out + m < cols:
                across[out + m, out] = taps[m + HALO]
    first = np.zeros((channels * mid_rows, channels * in_rows), np.float32)
    second = np.zeros((channels * rows, channels * mid_rows), np.float32)
    for c in range(channels):
        for e in range(rows + REACH):
            for m in range(REACH + 1):
                first[c * mid_rows + e, c * in_rows + e + m] = taps[m]
        for i in range(rows):
            for m in range(REACH + 1):
                second[c * rows + i, c * mid_rows + i + m] = taps[m]
    return across, first, second


def power_table(tiles, cols):
    lane = np.arange(cols)
    local = lane % TILE + 0.5 - TILE / 2
    belongs = (lane[None, :] // TILE == np.arange(tiles)[:, None]).astype(np.float32)
    return np.concatenate([belongs, belongs * local, belongs * local * local]).astype(np.float32)


def harmonics(dir_x, dir_y, dir_z):
    sq_x, sq_y, sq_z = (dir_x * dir_x, dir_y * dir_y, dir_z * dir_z)
    return [
        SH_ZERO + 0.0 * dir_x,
        -SH_ONE * dir_y,
        SH_ONE * dir_z,
        -SH_ONE * dir_x,
        SH_TWO[0] * dir_x * dir_y,
        SH_TWO[1] * dir_y * dir_z,
        SH_TWO[2] * (2.0 * sq_z - sq_x - sq_y),
        SH_TWO[3] * dir_x * dir_z,
        SH_TWO[4] * (sq_x - sq_y),
        SH_THREE[0] * dir_y * (3.0 * sq_x - sq_y),
        SH_THREE[1] * dir_x * dir_y * dir_z,
        SH_THREE[2] * dir_y * (4.0 * sq_z - sq_x - sq_y),
        SH_THREE[3] * dir_z * (2.0 * sq_z - 3.0 * sq_x - 3.0 * sq_y),
        SH_THREE[4] * dir_x * (4.0 * sq_z - sq_x - sq_y),
        SH_THREE[5] * dir_z * (sq_x - sq_y),
        SH_THREE[6] * dir_x * (sq_x - 3.0 * sq_y),
    ]


def camera_basis(affine):
    a, b = affine[0:3], affine[3:6]
    n_x = a[1] * b[2] - a[2] * b[1]
    n_y = a[2] * b[0] - a[0] * b[2]
    n_z = a[0] * b[1] - a[1] * b[0]
    length = jnp.sqrt(n_x * n_x + n_y * n_y + n_z * n_z)
    return harmonics(n_x / length, n_y / length, n_z / length)


def split3(value, axis=0):
    high = value.astype(BF16)
    rest = value - high.astype(F32)
    middle = rest.astype(BF16)
    low = (rest - middle.astype(F32)).astype(BF16)
    return high, middle, low


NN = ((1,), (0,))
NT = ((1,), (1,))
TN = ((0,), (0,))


def mx(a, b, dims=NN):
    return lax.dot_general(a, b, (dims, ((), ())), preferred_element_type=F32)


def split2(value):
    high = value.astype(BF16)
    return high, (value - high.astype(F32)).astype(BF16)


def stack3(value):
    return jnp.concatenate(split3(value), axis=0)


def stack2(value):
    return jnp.concatenate(split2(value), axis=0)


def exact_dot(table, value, dims):
    table = table.astype(BF16)
    total = None
    for part in split3(value):
        term = mx(table, part, dims)
        total = term if total is None else total + term
    return total


def tree_sum(vregs, lane_count):
    sub = lax.broadcasted_iota(jnp.int32, (8, lane_count), 0)

    def join(a, b, mask, shift):
        return jnp.where(mask, a, b) + pltpu.roll(jnp.where(mask, b, a), 8 - shift, 0)

    def half(offset):
        return ((sub + (8 - offset)) % 8) < 4

    def quarter(offset):
        return ((sub + (8 - offset)) % 4) < 2

    z1 = join(
        join(vregs[0], vregs[4], half(0), 4), join(vregs[2], vregs[6], half(2), 4), quarter(0), 2
    )
    z2 = join(
        join(vregs[1], vregs[5], half(1), 4), join(vregs[3], vregs[7], half(3), 4), quarter(1), 2
    )
    return join(z1, z2, (sub % 2) < 1, 1)


def block_shape(logs, quats, logit):
    squares = [jnp.exp(value) for value in logs]
    squares = [value * value for value in squares]
    quat_len = jnp.sqrt(
        quats[0] * quats[0] + quats[1] * quats[1] + quats[2] * quats[2] + quats[3] * quats[3]
    )
    r, i, j, k = [value / quat_len for value in quats]
    rotation = [
        [1.0 - 2.0 * (j * j + k * k), 2.0 * (i * j - r * k), 2.0 * (i * k + r * j)],
        [2.0 * (i * j + r * k), 1.0 - 2.0 * (i * i + k * k), 2.0 * (j * k - r * i)],
        [2.0 * (i * k - r * j), 2.0 * (j * k + r * i), 1.0 - 2.0 * (i * i + j * j)],
    ]
    spread = [[rotation[a][c] * squares[c] for c in range(3)] for a in range(3)]

    def moment(a, b):
        return (
            spread[a][0] * rotation[b][0]
            + spread[a][1] * rotation[b][1]
            + spread[a][2] * rotation[b][2]
        )

    pairs = ((0, 0), (1, 1), (2, 2), (0, 1), (0, 2), (1, 2))
    return [moment(a, b) for a, b in pairs], 1.0 / (1.0 + jnp.exp(-logit))


def view_terms(cam):
    a, b, time = cam[0:3], cam[3:6], cam[8]
    terms = a + [time * value for value in a] + b + [time * value for value in b]
    crossed = ((0, 1), (0, 2), (1, 2))
    terms += [a[c] * a[c] for c in range(3)] + [2.0 * a[c] * a[d] for c, d in crossed]
    terms += [a[c] * b[c] for c in range(3)] + [a[c] * b[d] + a[d] * b[c] for c, d in crossed]
    terms += [b[c] * b[c] for c in range(3)] + [2.0 * b[c] * b[d] for c, d in crossed]
    return terms + [cam[6], cam[7]] + camera_basis(cam[0:6])


TERM_ROWS = 6
SHIFT_AT = 30
BASIS_AT = 32
BASIS = 16
TERMS = 48
GEO_COMPS = 13


def step_kernel(
    geometry,
    camera_hbm,
    list_hbm,
    start_hbm,
    end_hbm,
    target_hbm,
    gauss_hbm,
    one_hbm,
    two_hbm,
    across_hbm,
    first_hbm,
    second_hbm,
    power_hbm,
    quad_hbm,
    tone_hbm,
    grad_ref,
    gauss_ref,
    one_ref,
    two_ref,
    loss_ref,
    camera_s,
    list_s,
    start_s,
    end_s,
    target_ref,
    across_ref,
    first_ref,
    second_ref,
    power_ref,
    quad_ref,
    tone_ref,
    msg_out,
    msg_in,
    hot_map,
    wide_map,
    geo_tab,
    tint_tab,
    tint_back,
    line_back,
    shape_back,
    geo_out,
    geo_in,
    tint_out,
    tint_in,
    geo_pick,
    tint_pick,
    shade_out,
    shade_in,
    grad_out,
    grad_in,
    halo_out,
    halo_in,
    thalo_out,
    thalo_in,
    coef,
    alpha_s,
    weight_s,
    moment_s,
    send_sem,
    recv_sem,
    halo_send,
    halo_recv,
    fetch_sem,
):
    views_n, bands_n, blocks, list_len, rows, cols, block_len = geometry
    devices = views_n * bands_n
    tiles = cols // TILE
    pairs = TILE_MOST * tiles
    window = TILE_MOST * block_len
    halves = block_len // 128
    geo_rows = GEO_REC * halves
    tint_rows = 3 * halves
    hot_lanes = bands_n * blocks
    basis_lanes = BASIS * blocks
    view = lax.axis_index("view")
    band = lax.axis_index("band")
    me = band * views_n + view
    has_up = band > 0
    has_down = band < bands_n - 1

    halo_in[...] = jnp.zeros_like(halo_in)
    thalo_in[...] = jnp.zeros_like(thalo_in)
    peer_view = [lax.rem(view + d, views_n) for d in range(views_n)]
    peer_band = [lax.rem(band + d, bands_n) for d in range(bands_n)]
    barrier = pltpu.get_barrier_semaphore()
    for d in range(1, views_n):
        pl.semaphore_signal(barrier, inc=1, device_id=(peer_view[d], band), device_id_type=MESH)
    for d in range(1, bands_n):
        pl.semaphore_signal(barrier, inc=1, device_id=(view, peer_band[d]), device_id_type=MESH)

    sources = (
        (camera_hbm, camera_s),
        (list_hbm, list_s),
        (start_hbm, start_s),
        (end_hbm, end_s),
        (target_hbm, target_ref),
        (gauss_hbm, gauss_ref),
        (quad_hbm, quad_ref),
        (tone_hbm, tone_ref),
        (power_hbm, power_ref),
        (across_hbm, across_ref),
        (first_hbm, first_ref),
        (second_hbm, second_ref),
        (one_hbm, one_ref),
        (two_hbm, two_ref),
    )
    fetches = [
        pltpu.make_async_copy(source, landing, fetch_sem.at[n])
        for n, (source, landing) in enumerate(sources)
    ]
    for fetch in fetches:
        fetch.start()

    def to_all(source, landing, length, phase):
        for d_view in range(views_n):
            for d_band in range(bands_n):
                if d_view + d_band == 0:
                    continue
                peer = peer_band[d_band] * views_n + peer_view[d_view]
                pltpu.make_async_remote_copy(
                    src_ref=source.at[peer, pl.ds(0, length)],
                    dst_ref=landing.at[me, pl.ds(0, length)],
                    send_sem=send_sem.at[phase],
                    recv_sem=recv_sem.at[phase],
                    device_id=(peer_view[d_view], peer_band[d_band]),
                    device_id_type=MESH,
                ).start()

    def wait_all(landing, length, phase):
        every = landing.at[pl.ds(0, devices - 1), pl.ds(0, length)]
        pltpu.make_async_copy(every, every, recv_sem.at[phase]).wait()
        pltpu.make_async_copy(every, every, send_sem.at[phase]).wait()

    def edge_copy(source, landing, direction, phase):
        step = -1 if direction == 0 else 1
        return pltpu.make_async_remote_copy(
            src_ref=source.at[direction],
            dst_ref=landing.at[1 - direction],
            send_sem=halo_send.at[phase, direction],
            recv_sem=halo_recv.at[phase, 1 - direction],
            device_id=(view, band + step),
            device_id_type=MESH,
        )

    def edges_start(source, landing, phase):
        @pl.when(has_up)
        def _():
            edge_copy(source, landing, 0, phase).start()

        @pl.when(has_down)
        def _():
            edge_copy(source, landing, 1, phase).start()

    def edges_wait(source, landing, phase):
        @pl.when(has_up)
        def _():
            up = edge_copy(source, landing, 0, phase)
            up.wait_send()
            pltpu.make_async_copy(
                landing.at[0], landing.at[0], halo_recv.at[phase, 0]
            ).wait()

        @pl.when(has_down)
        def _():
            down = edge_copy(source, landing, 1, phase)
            down.wait_send()
            pltpu.make_async_copy(
                landing.at[1], landing.at[1], halo_recv.at[phase, 1]
            ).wait()

    def lanes_of(shape):
        return lax.broadcasted_iota(jnp.int32, shape, len(shape) - 1)

    map_lane = lanes_of((128, 128))
    map_row = lax.broadcasted_iota(jnp.int32, (128, 128), 0)
    hot_map[...] = jnp.where(
        map_row == band * blocks + lax.rem(map_lane, blocks), 1.0, 0.0
    ).astype(BF16)
    for part in range(basis_lanes // 128):
        wide_map[:, part * 128 : (part + 1) * 128] = jnp.where(
            map_row == hot_lanes + BASIS_AT + part * (128 // blocks) + map_lane // blocks, 1.0, 0.0
        ).astype(BF16)
    for kind in range(5):
        at = basis_lanes + kind * 128
        wide_map[:, at : at + 128] = jnp.where(
            (map_row == hot_lanes + TERM_ROWS * kind + map_lane // blocks)
            & (map_lane < TERM_ROWS * blocks),
            1.0,
            0.0,
        ).astype(BF16)

    fetches[0].wait()
    fetches[1].wait()
    lane = lanes_of((1, 128))
    terms = view_terms([jnp.full((1, 128), camera_s[0, c], F32) for c in range(9)])
    row = jnp.zeros((1, 128), F32)
    for n in range(TERMS):
        row = jnp.where(lane == hot_lanes + n, terms[n], row)
    wanted = lax.broadcasted_iota(jnp.int32, (views_n, 128), 0) * hot_lanes + lanes_of(
        (views_n, 128)
    )
    hits = jnp.zeros((views_n, 128), F32)
    for n in range(list_len):
        hits = jnp.where(wanted == list_s[0, 0, n], 1.0, hits)
    message = jnp.where(lanes_of((views_n, 128)) < hot_lanes, hits, row)
    for v in range(views_n):
        msg_out[v] = message[v : v + 1]

    pl.semaphore_wait(barrier, views_n + bands_n - 2)
    for d in range(1, views_n):
        pltpu.make_async_remote_copy(
            src_ref=msg_out.at[peer_view[d]],
            dst_ref=msg_in.at[me],
            send_sem=send_sem.at[0],
            recv_sem=recv_sem.at[0],
            device_id=(peer_view[d], band),
            device_id_type=MESH,
        ).start()
    msg_in[me] = msg_out[view]
    fetches[2].wait()
    fetches[3].wait()
    fetches[4].wait()
    thalo_out[0] = target_ref[0, :, 0:REACH, :]
    thalo_out[1] = target_ref[0, :, rows - REACH : rows, :]
    edges_start(thalo_out, thalo_in, 0)

    owners, alive = [], []
    for k in range(TILE_MOST):
        for t in range(tiles):
            low, high = start_s[0, 0, t], end_s[0, 0, t]
            block = list_s[0, 0, jnp.clip(jnp.minimum(low + k, high - 1), 0, list_len - 1)]
            device = lax.div(jnp.clip(block, 0, devices * blocks - 1), blocks)
            owners.append(lax.rem(device, bands_n) * views_n + lax.div(device, bands_n))
            alive.append(jnp.where(low + k < high, 1.0, 0.0))
    put_lane = lax.rem(lanes_of((devices, 2 * pairs)), pairs)
    put_row = lax.broadcasted_iota(jnp.int32, (devices, 2 * pairs), 0)
    put = jnp.zeros((devices, 2 * pairs), F32)
    for n in range(pairs):
        put = jnp.where((put_lane == n) & (put_row == owners[n]), alive[n], put)
    put = put.astype(BF16)
    tile_sub = lax.broadcasted_iota(jnp.int32, (tiles, block_len), 0)
    parts = []
    for k in range(TILE_MOST):
        part = jnp.zeros((tiles, block_len), F32)
        for t in range(tiles):
            part = jnp.where(tile_sub == t, alive[k * tiles + t], part)
        parts.append(part)
    keep = jnp.concatenate(parts, axis=1) > 0.5

    plane = msg_in.at[pl.ds(0, views_n - 1)]
    pltpu.make_async_copy(plane, plane, recv_sem.at[0]).wait()
    pltpu.make_async_copy(plane, plane, send_sem.at[0]).wait()
    bundle = msg_in.at[pl.ds(band * views_n, views_n)]
    for d in range(1, bands_n):
        pltpu.make_async_remote_copy(
            src_ref=bundle,
            dst_ref=bundle,
            send_sem=send_sem.at[1],
            recv_sem=recv_sem.at[1],
            device_id=(view, peer_band[d]),
            device_id_type=MESH,
        ).start()

    fetches[5].wait()
    (sigma, opacity), pullback = jax.vjp(
        block_shape,
        [gauss_ref[6 + c] for c in range(3)],
        [gauss_ref[9 + c] for c in range(4)],
        gauss_ref[13],
    )
    for c, value in enumerate([gauss_ref[c] for c in range(6)] + list(sigma) + [opacity]):
        geo_tab[c] = stack3(value)
    for ch in range(3):
        for q in range(BASIS):
            high, low = split2(gauss_ref[14 + 3 * q + ch])
            tint_tab[ch, 0, q * blocks : (q + 1) * blocks, :] = high
            tint_tab[ch, 1, q * blocks : (q + 1) * blocks, :] = low

    lines = msg_in.at[pl.ds(0, devices - views_n)]
    pltpu.make_async_copy(lines, lines, recv_sem.at[1]).wait()
    pltpu.make_async_copy(lines, lines, send_sem.at[1]).wait()

    asked = msg_in[...].reshape(devices, 128)
    asked_parts = split3(asked)
    hot = mx(asked_parts[0], hot_map[...])
    hot_3 = hot[:, 0 : 3 * blocks].astype(BF16)
    picked = [mx(hot_3, geo_tab[c]) for c in range(GEO_COMPS)]

    def term(n):
        return asked[:, hot_lanes + n : hot_lanes + n + 1]

    def combine(at, low):
        total = term(at) * picked[low]
        for n in range(1, TERM_ROWS):
            total = total + term(at + n) * picked[low + n]
        return total

    records = [
        combine(0, 0) + term(SHIFT_AT),
        combine(6, 0) + term(SHIFT_AT + 1),
        combine(12, 6) + 0.3,
        combine(18, 6),
        combine(24, 6) + 0.3,
        picked[12],
    ]
    geo_flat = geo_out.reshape(devices * geo_out.shape[1], 128)
    for p in range(GEO_REC):
        for h in range(halves):
            geo_flat[pl.ds(p * halves + h, devices, stride=geo_out.shape[1]), :] = records[p][
                :, h * 128 : (h + 1) * 128
            ]
    to_all(geo_out, geo_in, geo_rows, 2)
    geo_in[me] = geo_out[me]
    stacked = jnp.concatenate(asked_parts, axis=0)

    def widen(low, high):
        wide = mx(stacked, wide_map[:, low:high])
        return wide[0:devices] + wide[devices : 2 * devices] + wide[2 * devices :]

    hot_wide = jnp.concatenate([hot] * (basis_lanes // 128), axis=1)
    basis = widen(0, basis_lanes) * hot_wide
    basis_high, basis_low = split2(basis)
    basis_two = jnp.concatenate([basis_high, basis_low], axis=0)
    tint_flat = tint_out.reshape(devices * tint_out.shape[1], 128)
    for ch in range(3):
        both = mx(basis_two, tint_tab[ch, 0])
        colour = 0.5 + both[0:devices] + both[devices:] + mx(basis_high, tint_tab[ch, 1])
        for h in range(halves):
            tint_flat[pl.ds(ch * halves + h, devices, stride=tint_out.shape[1]), :] = colour[
                :, h * 128 : (h + 1) * 128
            ]
    to_all(tint_out, tint_in, tint_rows, 3)
    tint_in[me] = tint_out[me]

    tint_back[...] = jnp.concatenate([basis_high, basis_low, basis_high], axis=0)
    spans = [
        widen(basis_lanes + kind * 128, basis_lanes + (kind + 1) * 128) * hot for kind in range(5)
    ]
    hot_lane = lanes_of((devices, 128))
    hot_last = jnp.where(
        (hot_lane >= TERM_ROWS * blocks) & (hot_lane < (TERM_ROWS + 1) * blocks), hot, 0.0
    )
    for landing, group in ((line_back, spans[0:2] + [hot_last]), (shape_back, spans[2:5])):
        high, low = split2(jnp.concatenate(group, axis=0))
        landing[...] = jnp.concatenate([high, low, high], axis=0)

    for n in range(6, 12):
        fetches[n].wait()
    edges_wait(thalo_out, thalo_in, 0)
    in_rows, mid_rows = up8(rows + 2 * REACH), up8(rows + REACH)
    high_rows = 3 * mid_rows
    fill = jnp.zeros((in_rows - rows - 2 * REACH, cols), F32)

    def smooth(fields):
        down = jnp.dot(
            first_ref[...],
            jnp.concatenate(fields, axis=1),
            precision=HIGHEST_MODE,
            preferred_element_type=F32,
        )
        stack = jnp.concatenate(
            [down[:, f * cols : (f + 1) * cols] for f in range(len(fields))], axis=0
        )
        flat = jnp.dot(
            stack, across_ref[...], precision=HIGHEST_MODE, preferred_element_type=F32
        )
        return [flat[f * high_rows : (f + 1) * high_rows] for f in range(len(fields))]

    mine = target_ref[0]
    ext_y = jnp.concatenate(
        [v for ch in range(3) for v in (thalo_in[0, ch], mine[ch], thalo_in[1, ch], fill)], axis=0
    )
    mean_y, square_y = smooth([ext_y, ext_y * ext_y])

    wait_all(geo_in, geo_rows, 2)
    for k in range(TILE_MOST):
        for t in range(tiles):
            geo_pick[k, pl.ds(t, geo_rows, stride=tiles), :] = geo_in[
                owners[k * tiles + t], 0:geo_rows, :
            ]

    def gathered(landed, p):
        return jnp.concatenate(
            [
                landed[k, (p * halves + h) * tiles : (p * halves + h + 1) * tiles, :]
                for k in range(TILE_MOST)
                for h in range(halves)
            ],
            axis=1,
        )

    tile_row = lax.broadcasted_iota(jnp.int32, (tiles, window), 0).astype(F32)
    u_rel = gathered(geo_pick, 0) - (tile_row * TILE + 0.5 * TILE)
    w_rel = gathered(geo_pick, 1) - ((band * rows).astype(F32) + 0.5 * TILE)
    c_a = gathered(geo_pick, 2)
    c_b = gathered(geo_pick, 3)
    c_c = gathered(geo_pick, 4)
    opac = gathered(geo_pick, 5)
    inv_det = 1.0 / (c_a * c_c - c_b * c_b)
    coef_a = -0.5 * c_c * inv_det
    coef_b = c_b * inv_det
    coef_c = -0.5 * c_a * inv_det

    def masked(value, other=0.0):
        return jnp.where(keep, value, other)

    flat = LOG2_E * (
        coef_a * u_rel * u_rel + coef_b * u_rel * w_rel + coef_c * w_rel * w_rel
    ) + LOG2_E * jnp.log(opac)
    quads = jnp.concatenate(
        [
            masked(flat, NEVER),
            masked(LOG2_E * (-2.0 * coef_a * u_rel - coef_b * w_rel)),
            masked(LOG2_E * coef_a),
            masked(LOG2_E * (-coef_b * u_rel - 2.0 * coef_c * w_rel)),
            masked(LOG2_E * coef_b),
            masked(LOG2_E * coef_c),
        ],
        axis=0,
    )
    grown = mx(stack3(quads), quad_ref[...], TN)
    for n in range(3):
        coef[n] = grown[:, n * cols : (n + 1) * cols]
    wait_all(tint_in, tint_rows, 3)
    for k in range(TILE_MOST):
        for t in range(tiles):
            tint_pick[k, pl.ds(t, tint_rows, stride=tiles), :] = tint_in[
                owners[k * tiles + t], 0:tint_rows, :
            ]
    tones = jnp.concatenate([masked(gathered(tint_pick, ch)) for ch in range(3)], axis=0)
    grown = mx(stack2(tones), tone_ref[...], TN)
    for ch in range(3):
        coef[3 + ch] = grown[:, ch * cols : (ch + 1) * cols]

    sub8 = lax.broadcasted_iota(jnp.int32, (8, cols), 0).astype(F32)
    parts_n = rows // 8
    row_local = [sub8 + (8.0 * part + 0.5 - 0.5 * TILE) for part in range(parts_n)]

    def spread_row(kind, j):
        return coef[kind, pl.ds(j, 8, stride=0), :]

    def blend(group, carry):
        trans, image = carry
        trans, image = list(trans), list(image)
        for k in range(8):
            j = group * 8 + k
            q0, q1, q2 = spread_row(0, j), spread_row(1, j), spread_row(2, j)
            tint = [spread_row(3 + ch, j) for ch in range(3)]
            for part in range(parts_n):
                r = row_local[part]
                alpha = jnp.exp2(q0 + r * (q1 + r * q2))
                weight = alpha * trans[part]
                alpha_s[j, part] = alpha
                weight_s[j, part] = weight
                trans[part] = trans[part] * (1.0 - alpha)
                for ch in range(3):
                    at = ch * parts_n + part
                    image[at] = image[at] + weight * tint[ch]
        return tuple(trans), tuple(image)

    zero = jnp.zeros((8, cols), F32)
    _, image = lax.fori_loop(
        0,
        window // 8,
        blend,
        (tuple([zero + 1.0] * parts_n), tuple([zero] * (3 * parts_n))),
    )
    pred = [
        jnp.concatenate([image[ch * parts_n + part] for part in range(parts_n)], axis=0)
        for ch in range(3)
    ]
    for ch in range(3):
        halo_out[0, ch] = pred[ch][0:REACH]
        halo_out[1, ch] = pred[ch][rows - REACH : rows]
    edges_start(halo_out, halo_in, 1)
    edges_wait(halo_out, halo_in, 1)

    ext_x = jnp.concatenate(
        [v for ch in range(3) for v in (halo_in[0, ch], pred[ch], halo_in[1, ch], fill)], axis=0
    )
    mean_x, square_x, cross = smooth([ext_x, ext_x * ext_x, ext_x * ext_y])
    n_mean = 2.0 * mean_x * mean_y + STAB_MEAN
    n_var = 2.0 * (cross - mean_x * mean_y) + STAB_VAR
    d_mean = mean_x * mean_x + mean_y * mean_y + STAB_MEAN
    d_var = (square_x - mean_x * mean_x) + (square_y - mean_y * mean_y) + STAB_VAR
    inv_mean = 1.0 / d_mean
    inv_var = 1.0 / d_var
    inverse = inv_mean * inv_var
    ssim = n_mean * n_var * inverse
    ext_row = lax.broadcasted_iota(jnp.int32, (high_rows, cols), 0) % mid_rows
    image_row = ext_row + (band * rows - HALO)
    inside = (image_row >= 0) & (image_row < bands_n * rows) & (ext_row < rows + REACH)
    scale = -SSIM_WEIGHT / 3.0
    part_mean = 2.0 * mean_y * (n_var - n_mean) * inverse - 2.0 * mean_x * ssim * (
        inv_mean - inv_var
    )
    adjoint = jnp.concatenate(
        [
            jnp.where(inside, scale * part_mean, 0.0),
            jnp.where(inside, -scale * ssim * inv_var, 0.0),
            jnp.where(inside, (2.0 * scale) * n_mean * inverse, 0.0),
        ],
        axis=1,
    )
    down2 = jnp.dot(second_ref[...], adjoint, precision=HIGHEST_MODE, preferred_element_type=F32)
    stacked2 = jnp.concatenate([down2[:, f * cols : (f + 1) * cols] for f in range(3)], axis=0)
    spread = jnp.dot(
        stacked2, across_ref[...], precision=HIGHEST_MODE, preferred_element_type=F32
    )
    deep = 3 * rows
    pred_all = jnp.concatenate(pred, axis=0)
    mine_all = jnp.concatenate([mine[ch] for ch in range(3)], axis=0)
    error = pred_all - mine_all
    sign = jnp.where(error > 0.0, 1.0, jnp.where(error < 0.0, -1.0, 0.0))
    grad_pred = (
        ABS_WEIGHT / 3.0 * sign
        + spread[0:deep]
        + 2.0 * pred_all * spread[deep : 2 * deep]
        + mine_all * spread[2 * deep : 3 * deep]
    )
    own = (ext_row >= HALO) & (ext_row < HALO + rows)
    loss = jnp.sum(ABS_WEIGHT / 3.0 * jnp.abs(error), keepdims=True) + jnp.sum(
        jnp.where(own, SSIM_WEIGHT / 3.0 * (1.0 - ssim), 0.0), keepdims=True
    )

    pull = [
        [grad_pred[ch * rows + 8 * part : ch * rows + 8 * part + 8] for part in range(parts_n)]
        for ch in range(3)
    ]

    def shades(group, carry):
        sums = [[None] * 8 for _ in range(3)]
        for k in range(8):
            j = group * 8 + k
            weight = [weight_s[j, part] for part in range(parts_n)]
            for ch in range(3):
                total = weight[0] * pull[ch][0]
                for part in range(1, parts_n):
                    total = total + weight[part] * pull[ch][part]
                sums[ch][k] = total
        at = pl.multiple_of(group * 8, 8)
        for ch in range(3):
            moment_s[3 + ch, pl.ds(at, 8), :] = tree_sum(sums[ch], cols)
        return carry

    lax.fori_loop(0, window // 8, shades, 0)

    def route(value):
        stack = jnp.concatenate(
            [value[:, k * block_len : (k + 1) * block_len] for k in range(TILE_MOST)], axis=0
        )
        return mx(put, stack2(stack))

    power = power_ref[...]
    shade_flat = shade_out.reshape(devices * shade_out.shape[1], 128)
    for ch in range(3):
        routed = route(exact_dot(power[0:tiles], moment_s[3 + ch], NT))
        for h in range(halves):
            shade_flat[pl.ds(ch * halves + h, devices, stride=shade_out.shape[1]), :] = routed[
                :, h * 128 : (h + 1) * 128
            ]
    shade_flat[pl.ds(tint_rows, devices, stride=shade_out.shape[1]), :] = jnp.broadcast_to(
        loss, (devices, 128)
    )
    to_all(shade_out, shade_in, tint_rows + 1, 4)
    shade_in[me] = shade_out[me]

    def unblend(step, behind):
        group = window // 8 - 1 - step
        behind = list(behind)
        sums = [[None] * 8 for _ in range(3)]
        for k in reversed(range(8)):
            j = group * 8 + k
            tint = [spread_row(3 + ch, j) for ch in range(3)]
            totals = [None] * 3
            for part in range(parts_n):
                alpha = alpha_s[j, part]
                shade = (
                    tint[0] * pull[0][part] + tint[1] * pull[1][part] + tint[2] * pull[2][part]
                )
                gap = shade - behind[part]
                behind[part] = alpha * shade + (1.0 - alpha) * behind[part]
                lean = weight_s[j, part] * gap
                lean_r = lean * row_local[part]
                terms = [lean, lean_r, lean_r * row_local[part]]
                totals = [
                    value if total is None else total + value
                    for value, total in zip(terms, totals)
                ]
            for kind in range(3):
                sums[kind][k] = totals[kind]
        at = pl.multiple_of(group * 8, 8)
        for kind in range(3):
            moment_s[kind, pl.ds(at, 8), :] = tree_sum(sums[kind], cols)
        return tuple(behind)

    lax.fori_loop(0, window // 8, unblend, tuple([zero] * parts_n))

    by_x = exact_dot(power, moment_s[0], NT)
    m_00, m_10, m_20 = by_x[0:tiles], by_x[tiles : 2 * tiles], by_x[2 * tiles : 3 * tiles]
    by_xr = exact_dot(power[0 : 2 * tiles], moment_s[1], NT)
    m_01, m_11 = by_xr[0:tiles], by_xr[tiles : 2 * tiles]
    m_02 = exact_dot(power[0:tiles], moment_s[2], NT)
    s_x = m_10 - u_rel * m_00
    s_y = m_01 - w_rel * m_00
    s_xx = m_20 - 2.0 * u_rel * m_10 + u_rel * u_rel * m_00
    s_xy = m_11 - u_rel * m_01 - w_rel * m_10 + u_rel * w_rel * m_00
    s_yy = m_02 - 2.0 * w_rel * m_01 + w_rel * w_rel * m_00
    by_det = -(coef_a * s_xx + coef_b * s_xy + coef_c * s_yy) * inv_det
    derivs = [
        -(2.0 * coef_a * s_x + coef_b * s_y),
        -(2.0 * coef_c * s_y + coef_b * s_x),
        -0.5 * inv_det * s_yy + by_det * c_c,
        inv_det * s_xy - 2.0 * c_b * by_det,
        -0.5 * inv_det * s_xx + by_det * c_a,
        m_00 / opac,
    ]
    grad_flat = grad_out.reshape(devices * grad_out.shape[1], 128)
    for p in range(GEO_REC):
        routed = route(derivs[p])
        for h in range(halves):
            grad_flat[pl.ds(p * halves + h, devices, stride=grad_out.shape[1]), :] = routed[
                :, h * 128 : (h + 1) * 128
            ]
    to_all(grad_out, grad_in, geo_rows, 5)
    grad_in[me] = grad_out[me]

    wait_all(shade_in, tint_rows + 1, 4)
    shade_back = shade_in.reshape(devices * shade_in.shape[1], 128)
    grad_back = grad_in.reshape(devices * grad_in.shape[1], 128)

    def arrived(landed, stride, p):
        return jnp.concatenate(
            [landed[pl.ds(p * halves + h, devices, stride=stride), :] for h in range(halves)],
            axis=1,
        )

    def spread_back(table, values):
        high, low = split2(jnp.concatenate(values, axis=0))
        return mx(table[...], jnp.concatenate([high, high, low], axis=0), TN)

    for ch in range(3):
        colour = spread_back(tint_back, [arrived(shade_back, shade_in.shape[1], ch)])
        for q in range(BASIS):
            grad_ref[14 + 3 * q + ch] = colour[q * blocks : (q + 1) * blocks]
    losses = shade_back[pl.ds(tint_rows, devices, stride=shade_in.shape[1]), :]
    loss_ref[...] = jnp.sum(losses, axis=0, keepdims=True)[:, 0:1] * (
        1.0 / (devices * rows * cols)
    )
    fetches[12].wait()
    fetches[13].wait()

    wait_all(grad_in, geo_rows, 5)
    geos = [arrived(grad_back, grad_in.shape[1], p) for p in range(GEO_REC)]
    line = spread_back(line_back, [geos[0], geos[1], geos[5]])
    shape = spread_back(shape_back, geos[2:5])

    def comp(value, n):
        return value[n * blocks : (n + 1) * blocks]

    d_logs, d_quats, d_logit = pullback(
        ([comp(shape, n) for n in range(TERM_ROWS)], comp(line, TERM_ROWS))
    )
    columns = [comp(line, n) for n in range(TERM_ROWS)] + list(d_logs) + list(d_quats) + [d_logit]
    for c, value in enumerate(columns):
        grad_ref[c] = value


def adam_kernel(
    grad_ref,
    gauss_ref,
    one_ref,
    two_ref,
    loss_in,
    out_gauss,
    out_one,
    out_two,
    out_grad,
    loss_out,
    gauss_v,
    one_v,
    two_v,
    write_sem,
):
    whole = pltpu.make_async_copy(grad_ref, out_grad, write_sem.at[3, 0])
    whole.start()
    total = pltpu.make_async_copy(loss_in, loss_out, write_sem.at[3, 1])
    total.start()
    comps = gauss_ref.shape[0]
    pieces = [whole, total]
    for piece in range(PIECES):
        low, high = piece * comps // PIECES, (piece + 1) * comps // PIECES

        def update(c, carry):
            gradient = grad_ref[c]
            new_one = 0.9 * one_ref[c] + 0.1 * gradient
            new_two = 0.999 * two_ref[c] + 0.001 * gradient * gradient
            one_v[c] = new_one
            two_v[c] = new_two
            bottom = jnp.sqrt(new_two * (1.0 / BIAS_SECOND)) + 1e-08
            gauss_v[c] = gauss_ref[c] - learning_rate(c) * new_one / bottom
            return carry

        lax.fori_loop(low, high, update, 0, unroll=2)
        part = pl.ds(low, high - low)
        for source, landing, sem in (
            (one_v, out_one, 0),
            (two_v, out_two, 1),
            (gauss_v, out_gauss, 2),
        ):
            copy = pltpu.make_async_copy(
                source.at[part], landing.at[part], write_sem.at[sem, piece]
            )
            copy.start()
            pieces.append(copy)
    for copy in pieces:
        copy.wait()


def quad_table(tiles, cols):
    lane = np.arange(cols)
    local = lane % TILE + 0.5 - TILE / 2
    belongs = (lane[None, :] // TILE == np.arange(tiles)[:, None]).astype(np.float32)
    nothing = np.zeros_like(belongs)
    rows = [
        [belongs, nothing, nothing],
        [belongs * local, nothing, nothing],
        [belongs * local * local, nothing, nothing],
        [nothing, belongs, nothing],
        [nothing, belongs * local, nothing],
        [nothing, nothing, belongs],
    ]
    return np.tile(np.block(rows), (3, 1))


def tone_table(tiles, cols):
    belongs = (np.arange(cols)[None, :] // TILE == np.arange(tiles)[:, None]).astype(np.float32)
    return np.tile(np.kron(np.eye(3, dtype=np.float32), belongs), (2, 1))


def per_device(
    gaussians,
    first_moment,
    second_moment,
    camera,
    target,
    block_list,
    block_count,
    tile_start,
    tile_end,
):
    views_n = lax.axis_size("view")
    bands_n = lax.axis_size("band")
    devices = views_n * bands_n
    blocks, comps, block_len = gaussians.shape
    list_len = block_list.shape[2]
    rows, cols = target.shape[2:]
    tiles = cols // TILE
    halves = block_len // 128
    geometry = (views_n, bands_n, blocks, list_len, rows, cols, block_len)

    across, first, second = smoothing_tables(rows, cols, 3)
    power = power_table(tiles, cols)
    quad = quad_table(tiles, cols).astype(BF16)
    tone = tone_table(tiles, cols).astype(BF16)
    vmem = pl.BlockSpec(memory_space=pltpu.VMEM)
    hbm = pl.BlockSpec(memory_space=pltpu.HBM)

    def by_comp(array):
        return jnp.transpose(array, (1, 0, 2))

    window = TILE_MOST * block_len
    geo_pad, tint_pad = up8(GEO_REC * halves), up8(3 * halves + 1)
    basis_lanes = BASIS * blocks
    shape = jax.ShapeDtypeStruct((comps, blocks, block_len), F32)
    scalar = jax.ShapeDtypeStruct((1, 1), F32)
    kept = pltpu.VMEM(shape.shape, F32)
    gradient, params, one, two, mean_loss = pl.pallas_call(
        functools.partial(step_kernel, geometry),
        out_shape=(kept, kept, kept, kept, pltpu.VMEM((1, 1), F32)),
        in_specs=[hbm] * 14,
        out_specs=(vmem,) * 5,
        scratch_shapes=[
            pltpu.SMEM((1, 9), F32),
            pltpu.SMEM((1, 1, list_len), jnp.int32),
            pltpu.SMEM((1, 1, tiles), jnp.int32),
            pltpu.SMEM((1, 1, tiles), jnp.int32),
            pltpu.VMEM((1, 3, rows, cols), F32),
            pltpu.VMEM(across.shape, F32),
            pltpu.VMEM(first.shape, F32),
            pltpu.VMEM(second.shape, F32),
            pltpu.VMEM(power.shape, F32),
            pltpu.VMEM(quad.shape, BF16),
            pltpu.VMEM(tone.shape, BF16),
            pltpu.VMEM((views_n, 1, 128), F32),
            pltpu.VMEM((devices, 1, 128), F32),
            pltpu.VMEM((128, 128), BF16),
            pltpu.VMEM((128, basis_lanes + 5 * 128), BF16),
            pltpu.VMEM((GEO_COMPS, 3 * blocks, block_len), BF16),
            pltpu.VMEM((3, 2, basis_lanes, block_len), BF16),
            pltpu.VMEM((3 * devices, basis_lanes), BF16),
            pltpu.VMEM((9 * devices, 128), BF16),
            pltpu.VMEM((9 * devices, 128), BF16),
            pltpu.VMEM((devices, geo_pad, 128), F32),
            pltpu.VMEM((devices, geo_pad, 128), F32),
            pltpu.VMEM((devices, tint_pad, 128), F32),
            pltpu.VMEM((devices, tint_pad, 128), F32),
            pltpu.VMEM((TILE_MOST, GEO_REC * halves * tiles, 128), F32),
            pltpu.VMEM((TILE_MOST, 3 * halves * tiles, 128), F32),
            pltpu.VMEM((devices, tint_pad, 128), F32),
            pltpu.VMEM((devices, tint_pad, 128), F32),
            pltpu.VMEM((devices, geo_pad, 128), F32),
            pltpu.VMEM((devices, geo_pad, 128), F32),
            pltpu.VMEM((2, 3, REACH, cols), F32),
            pltpu.VMEM((2, 3, REACH, cols), F32),
            pltpu.VMEM((2, 3, REACH, cols), F32),
            pltpu.VMEM((2, 3, REACH, cols), F32),
            pltpu.VMEM((6, window, cols), F32),
            pltpu.VMEM((window, rows // 8, 8, cols), F32),
            pltpu.VMEM((window, rows // 8, 8, cols), F32),
            pltpu.VMEM((6, window, cols), F32),
            pltpu.SemaphoreType.DMA((6,)),
            pltpu.SemaphoreType.DMA((6,)),
            pltpu.SemaphoreType.DMA((2, 2)),
            pltpu.SemaphoreType.DMA((2, 2)),
            pltpu.SemaphoreType.DMA((14,)),
        ],
        compiler_params=pltpu.CompilerParams(
            collective_id=0, has_side_effects=True, vmem_limit_bytes=40 * 1024 * 1024
        ),
        name="render_step",
    )(
        *[
            pltpu.with_memory_space_constraint(array, pltpu.HBM)
            for array in (
                camera,
                block_list,
                tile_start,
                tile_end,
                target,
                by_comp(gaussians),
                by_comp(first_moment),
                by_comp(second_moment),
                across,
                first,
                second,
                power,
                quad,
                tone,
            )
        ]
    )

    new_params, new_one, new_two, out_gradient, out_loss = pl.pallas_call(
        adam_kernel,
        out_shape=(shape, shape, shape, shape, scalar),
        in_specs=[vmem] * 5,
        out_specs=(hbm, hbm, hbm, hbm, hbm),
        scratch_shapes=[pltpu.VMEM((comps, blocks, block_len), F32)] * 3
        + [pltpu.SemaphoreType.DMA((4, PIECES))],
        compiler_params=pltpu.CompilerParams(vmem_limit_bytes=16 * 1024 * 1024),
        name="adam_step",
    )(gradient, params, one, two, mean_loss)
    return (
        by_comp(new_params),
        by_comp(new_one),
        by_comp(new_two),
        out_loss.reshape(()),
        by_comp(out_gradient),
    )


def solution(mesh):
    return jax.shard_map(
        per_device,
        mesh=mesh,
        in_specs=(
            P(("view", "band"), None, None),
            P(("view", "band"), None, None),
            P(("view", "band"), None, None),
            P("view", None),
            P("view", None, "band", None),
            P("view", "band", None),
            P("view", "band"),
            P("view", "band", None),
            P("view", "band", None),
        ),
        out_specs=(
            P(("view", "band"), None, None),
            P(("view", "band"), None, None),
            P(("view", "band"), None, None),
            P(),
            P(("view", "band"), None, None),
        ),
        check_vma=False,
    )
```

```python
import functools
import math

import jax
import jax.numpy as jnp
import numpy as np
from jax import lax
from jax.experimental import pallas as pl
from jax.experimental.pallas import tpu as pltpu
from jax.sharding import PartitionSpec as P

TILE = 16
TILE_MOST = 2
HALO = 5
REACH = 2 * HALO
GEO_REC = 6
RECORDS = 9
PIECES = 3
SHAPE_COMPS = 14
UNROLL = 4

HIGHEST_MODE = lax.Precision.HIGHEST
SSIM_WEIGHT = 0.2
ABS_WEIGHT = 0.8
STAB_MEAN = 0.0001
STAB_VAR = 0.0009
BIAS_FIRST = 1.0 - math.exp(100.0 * math.log(0.9))
BIAS_SECOND = 1.0 - math.exp(100.0 * math.log(0.999))
LOG2_E = math.log2(math.e)
SH_ZERO = 0.28209479177387814
SH_ONE = 0.4886025119029199
SH_TWO = [
    1.0925484305920792,
    -1.0925484305920792,
    0.31539156525252005,
    -1.0925484305920792,
    0.5462742152960396,
]
SH_THREE = [
    -0.5900435899266435,
    2.890611442640554,
    -0.4570457994644658,
    0.3731763325901154,
    -0.4570457994644658,
    1.445305721320277,
    -0.5900435899266435,
]
F32 = jnp.float32
BF16 = jnp.bfloat16
MESH = pl.DeviceIdType.MESH
NEVER = -1e30


RATES = ((6, 0.016), (9, 0.005), (13, 0.001), (14, 0.05), (17, 0.0025), (62, 0.000125))


def learning_rate(component):
    rate = RATES[-1][1] / BIAS_FIRST
    if isinstance(component, int):
        return next(value for end, value in RATES if component < end) / BIAS_FIRST
    for end, value in reversed(RATES[:-1]):
        rate = jnp.where(component < end, value / BIAS_FIRST, rate)
    return rate


def kernel_taps():
    raw_taps = [math.exp(-(offset * offset) / 4.5) for offset in range(-5, 6)]
    tap_total = sum(raw_taps)
    return [raw_tap / tap_total for raw_tap in raw_taps]


def up8(value):
    return (value + 7) // 8 * 8


def smoothing_tables(rows, cols, channels):
    taps = kernel_taps()
    in_rows, mid_rows = up8(rows + 2 * REACH), up8(rows + REACH)
    across = np.zeros((cols, cols), np.float32)
    for out in range(cols):
        for m in range(-HALO, HALO + 1):
            if 0 <= out + m < cols:
                across[out + m, out] = taps[m + HALO]
    first = np.zeros((channels * mid_rows, channels * in_rows), np.float32)
    second = np.zeros((channels * rows, channels * mid_rows), np.float32)
    for c in range(channels):
        for e in range(rows + REACH):
            for m in range(REACH + 1):
                first[c * mid_rows + e, c * in_rows + e + m] = taps[m]
        for i in range(rows):
            for m in range(REACH + 1):
                second[c * rows + i, c * mid_rows + i + m] = taps[m]
    return across, first, second


def power_table(tiles, cols):
    lane = np.arange(cols)
    local = lane % TILE + 0.5 - TILE / 2
    belongs = (lane[None, :] // TILE == np.arange(tiles)[:, None]).astype(np.float32)
    return np.concatenate([belongs, belongs * local, belongs * local * local]).astype(np.float32)


def harmonics(dir_x, dir_y, dir_z):
    sq_x, sq_y, sq_z = (dir_x * dir_x, dir_y * dir_y, dir_z * dir_z)
    return [
        SH_ZERO + 0.0 * dir_x,
        -SH_ONE * dir_y,
        SH_ONE * dir_z,
        -SH_ONE * dir_x,
        SH_TWO[0] * dir_x * dir_y,
        SH_TWO[1] * dir_y * dir_z,
        SH_TWO[2] * (2.0 * sq_z - sq_x - sq_y),
        SH_TWO[3] * dir_x * dir_z,
        SH_TWO[4] * (sq_x - sq_y),
        SH_THREE[0] * dir_y * (3.0 * sq_x - sq_y),
        SH_THREE[1] * dir_x * dir_y * dir_z,
        SH_THREE[2] * dir_y * (4.0 * sq_z - sq_x - sq_y),
        SH_THREE[3] * dir_z * (2.0 * sq_z - 3.0 * sq_x - 3.0 * sq_y),
        SH_THREE[4] * dir_x * (4.0 * sq_z - sq_x - sq_y),
        SH_THREE[5] * dir_z * (sq_x - sq_y),
        SH_THREE[6] * dir_x * (sq_x - 3.0 * sq_y),
    ]


def camera_basis(affine):
    a, b = affine[0:3], affine[3:6]
    n_x = a[1] * b[2] - a[2] * b[1]
    n_y = a[2] * b[0] - a[0] * b[2]
    n_z = a[0] * b[1] - a[1] * b[0]
    length = jnp.sqrt(n_x * n_x + n_y * n_y + n_z * n_z)
    return harmonics(n_x / length, n_y / length, n_z / length)


def split3(value, axis=0):
    high = value.astype(BF16)
    rest = value - high.astype(F32)
    middle = rest.astype(BF16)
    low = (rest - middle.astype(F32)).astype(BF16)
    return high, middle, low


NN = ((1,), (0,))
NT = ((1,), (1,))
TN = ((0,), (0,))


def mx(a, b, dims=NN):
    return lax.dot_general(a, b, (dims, ((), ())), preferred_element_type=F32)


def split2(value):
    high = value.astype(BF16)
    return high, (value - high.astype(F32)).astype(BF16)


def stack3(value):
    return jnp.concatenate(split3(value), axis=0)


def stack2(value):
    return jnp.concatenate(split2(value), axis=0)


def exact_dot(table, value, dims):
    table = table.astype(BF16)
    total = None
    for part in split3(value):
        term = mx(table, part, dims)
        total = term if total is None else total + term
    return total


def tree_sum(vregs, lane_count):
    sub = lax.broadcasted_iota(jnp.int32, (8, lane_count), 0)

    def join(a, b, mask, shift):
        return jnp.where(mask, a, b) + pltpu.roll(jnp.where(mask, b, a), 8 - shift, 0)

    def half(offset):
        return ((sub + (8 - offset)) % 8) < 4

    def quarter(offset):
        return ((sub + (8 - offset)) % 4) < 2

    z1 = join(
        join(vregs[0], vregs[4], half(0), 4), join(vregs[2], vregs[6], half(2), 4), quarter(0), 2
    )
    z2 = join(
        join(vregs[1], vregs[5], half(1), 4), join(vregs[3], vregs[7], half(3), 4), quarter(1), 2
    )
    return join(z1, z2, (sub % 2) < 1, 1)


def adam_step(c, grad_ref, source, landing):
    gradient = grad_ref[c]
    new_one = 0.9 * source[1][c] + 0.1 * gradient
    new_two = 0.999 * source[2][c] + 0.001 * gradient * gradient
    landing[1][c] = new_one
    landing[2][c] = new_two
    bottom = jnp.sqrt(new_two * (1.0 / BIAS_SECOND)) + 1e-08
    landing[0][c] = source[0][c] - learning_rate(c) * new_one / bottom


def block_axes(logs, quats):
    scales = [jnp.exp(value) for value in logs]
    quat_len = jnp.sqrt(
        quats[0] * quats[0] + quats[1] * quats[1] + quats[2] * quats[2] + quats[3] * quats[3]
    )
    r, i, j, k = [value / quat_len for value in quats]
    rotation = [
        [1.0 - 2.0 * (j * j + k * k), 2.0 * (i * j - r * k), 2.0 * (i * k + r * j)],
        [2.0 * (i * j + r * k), 1.0 - 2.0 * (i * i + k * k), 2.0 * (j * k - r * i)],
        [2.0 * (i * k - r * j), 2.0 * (j * k + r * i), 1.0 - 2.0 * (i * i + j * j)],
    ]
    return rotation, scales


def block_shape(logs, quats, logit):
    rotation, scales = block_axes(logs, quats)
    axes = [[rotation[a][c] * scales[c] for c in range(3)] for a in range(3)]

    def moment(a, b):
        return axes[a][0] * axes[b][0] + axes[a][1] * axes[b][1] + axes[a][2] * axes[b][2]

    pairs = ((0, 0), (1, 1), (2, 2), (0, 1), (0, 2), (1, 2))
    return [moment(a, b) for a, b in pairs], 1.0 / (1.0 + jnp.exp(-logit))


def view_terms(cam):
    a, b, time = cam[0:3], cam[3:6], cam[8]
    terms = a + [time * value for value in a] + b + [time * value for value in b]
    crossed = ((0, 1), (0, 2), (1, 2))
    terms += [a[c] * a[c] for c in range(3)] + [2.0 * a[c] * a[d] for c, d in crossed]
    terms += [a[c] * b[c] for c in range(3)] + [a[c] * b[d] + a[d] * b[c] for c, d in crossed]
    terms += [b[c] * b[c] for c in range(3)] + [2.0 * b[c] * b[d] for c, d in crossed]
    return terms + [cam[6], cam[7], time] + camera_basis(cam[0:6])


TERM_ROWS = 6
SHIFT_AT = 30
BASIS_AT = 33
BASIS = 16
TERMS = 49
GEO_COMPS = 19


def step_kernel(
    geometry,
    camera_hbm,
    list_hbm,
    start_hbm,
    end_hbm,
    target_hbm,
    gauss_hbm,
    one_hbm,
    two_hbm,
    across_hbm,
    first_hbm,
    second_hbm,
    power_hbm,
    quad_hbm,
    tone_hbm,
    grad_ref,
    gauss_ref,
    one_ref,
    two_ref,
    loss_ref,
    camera_s,
    list_s,
    start_s,
    end_s,
    target_ref,
    across_ref,
    first_ref,
    second_ref,
    second_k,
    across_k,
    power_ref,
    quad_ref,
    tone_ref,
    msg_out,
    msg_in,
    asked_ref,
    hot_map,
    wide_map,
    geo_tab,
    tint_tab,
    tint_back,
    line_back,
    shape_back,
    rec_out,
    rec_in,
    rec_pick,
    shade_out,
    shade_in,
    grad_out,
    grad_in,
    halo_out,
    halo_in,
    thalo_out,
    thalo_in,
    coef,
    alpha_s,
    weight_s,
    moment_s,
    send_sem,
    recv_sem,
    halo_send,
    halo_recv,
    fetch_sem,
):
    views_n, bands_n, blocks, list_len, rows, cols, block_len = geometry
    devices = views_n * bands_n
    tiles = cols // TILE
    pairs = TILE_MOST * tiles
    window = TILE_MOST * block_len
    halves = block_len // 128
    pair_len = TILE_MOST * 128
    tint_rows = 3 * halves
    hot_lanes = bands_n * blocks
    basis_lanes = BASIS * blocks
    view = lax.axis_index("view")
    band = lax.axis_index("band")
    me = band * views_n + view
    has_up = band > 0
    has_down = band < bands_n - 1

    halo_in[...] = jnp.zeros_like(halo_in)
    thalo_in[...] = jnp.zeros_like(thalo_in)
    peer_view = [lax.rem(view + d, views_n) for d in range(views_n)]
    peer_band = [lax.rem(band + d, bands_n) for d in range(bands_n)]
    barrier = pltpu.get_barrier_semaphore()
    for d in range(1, views_n):
        pl.semaphore_signal(barrier, inc=1, device_id=(peer_view[d], band), device_id_type=MESH)
    for d in range(1, bands_n):
        pl.semaphore_signal(barrier, inc=1, device_id=(view, peer_band[d]), device_id_type=MESH)

    sources = (
        (camera_hbm, camera_s),
        (list_hbm, list_s),
        (start_hbm, start_s),
        (end_hbm, end_s),
        (target_hbm, target_ref),
        (gauss_hbm, gauss_ref),
        (quad_hbm, quad_ref),
        (tone_hbm, tone_ref),
        (power_hbm, power_ref),
        (across_hbm, across_ref),
        (first_hbm, first_ref),
        (second_hbm, second_ref),
        (one_hbm, one_ref),
        (two_hbm, two_ref),
    )
    fetches = [
        pltpu.make_async_copy(source, landing, fetch_sem.at[n])
        for n, (source, landing) in enumerate(sources)
    ]
    for fetch in fetches:
        fetch.start()

    def to_all(source, landing, length, phase):
        for d_view in range(views_n):
            for d_band in range(bands_n):
                if d_view + d_band == 0:
                    continue
                peer = peer_band[d_band] * views_n + peer_view[d_view]
                pltpu.make_async_remote_copy(
                    src_ref=source.at[peer, pl.ds(0, length)],
                    dst_ref=landing.at[me, pl.ds(0, length)],
                    send_sem=send_sem.at[phase],
                    recv_sem=recv_sem.at[phase],
                    device_id=(peer_view[d_view], peer_band[d_band]),
                    device_id_type=MESH,
                ).start()

    def wait_all(landing, length, phase):
        every = landing.at[pl.ds(0, devices - 1), pl.ds(0, length)]
        pltpu.make_async_copy(every, every, recv_sem.at[phase]).wait()
        pltpu.make_async_copy(every, every, send_sem.at[phase]).wait()

    def edge_copy(source, landing, direction, phase):
        step = -1 if direction == 0 else 1
        return pltpu.make_async_remote_copy(
            src_ref=source.at[direction],
            dst_ref=landing.at[1 - direction],
            send_sem=halo_send.at[phase, direction],
            recv_sem=halo_recv.at[phase, 1 - direction],
            device_id=(view, band + step),
            device_id_type=MESH,
        )

    def edges_start(source, landing, phase):
        @pl.when(has_up)
        def _():
            edge_copy(source, landing, 0, phase).start()

        @pl.when(has_down)
        def _():
            edge_copy(source, landing, 1, phase).start()

    def edges_wait(source, landing, phase):
        @pl.when(has_up)
        def _():
            up = edge_copy(source, landing, 0, phase)
            up.wait_send()
            pltpu.make_async_copy(
                landing.at[0], landing.at[0], halo_recv.at[phase, 0]
            ).wait()

        @pl.when(has_down)
        def _():
            down = edge_copy(source, landing, 1, phase)
            down.wait_send()
            pltpu.make_async_copy(
                landing.at[1], landing.at[1], halo_recv.at[phase, 1]
            ).wait()

    def lanes_of(shape):
        return lax.broadcasted_iota(jnp.int32, shape, len(shape) - 1)

    map_lane = lanes_of((128, 128))
    map_row = lax.broadcasted_iota(jnp.int32, (128, 128), 0)
    hot_map[...] = jnp.where(
        map_row == band * blocks + lax.rem(map_lane, blocks), 1.0, 0.0
    ).astype(BF16)
    for part in range(basis_lanes // 128):
        wide_map[:, part * 128 : (part + 1) * 128] = jnp.where(
            map_row == hot_lanes + BASIS_AT + part * (128 // blocks) + map_lane // blocks, 1.0, 0.0
        ).astype(BF16)
    for kind in range(5):
        at = basis_lanes + kind * 128
        wide_map[:, at : at + 128] = jnp.where(
            (map_row == hot_lanes + TERM_ROWS * kind + map_lane // blocks)
            & (map_lane < TERM_ROWS * blocks),
            1.0,
            0.0,
        ).astype(BF16)

    fetches[0].wait()
    fetches[1].wait()
    lane = lanes_of((1, 128))
    terms = view_terms([jnp.full((1, 128), camera_s[0, c], F32) for c in range(9)])
    row = jnp.zeros((1, 128), F32)
    for n in range(TERMS):
        row = jnp.where(lane == hot_lanes + n, terms[n], row)
    wanted = lax.broadcasted_iota(jnp.int32, (views_n, 128), 0) * hot_lanes + lanes_of(
        (views_n, 128)
    )
    hits = jnp.zeros((views_n, 128), F32)
    for n in range(list_len):
        hits = jnp.where(wanted == list_s[0, 0, n], 1.0, hits)
    message = jnp.where(lanes_of((views_n, 128)) < hot_lanes, hits, row)
    for v in range(views_n):
        msg_out[v] = message[v : v + 1]

    pl.semaphore_wait(barrier, views_n + bands_n - 2)
    for d in range(1, views_n):
        pltpu.make_async_remote_copy(
            src_ref=msg_out.at[peer_view[d]],
            dst_ref=msg_in.at[me],
            send_sem=send_sem.at[0],
            recv_sem=recv_sem.at[0],
            device_id=(peer_view[d], band),
            device_id_type=MESH,
        ).start()
    msg_in[me] = msg_out[view]
    fetches[2].wait()
    fetches[3].wait()
    fetches[4].wait()
    thalo_out[0] = target_ref[0, :, 0:REACH, :]
    thalo_out[1] = target_ref[0, :, rows - REACH : rows, :]
    edges_start(thalo_out, thalo_in, 0)

    owners, alive = [], []
    for k in range(TILE_MOST):
        for t in range(tiles):
            low, high = start_s[0, 0, t], end_s[0, 0, t]
            block = list_s[0, 0, jnp.clip(jnp.minimum(low + k, high - 1), 0, list_len - 1)]
            device = lax.div(jnp.clip(block, 0, devices * blocks - 1), blocks)
            owners.append(lax.rem(device, bands_n) * views_n + lax.div(device, bands_n))
            alive.append(jnp.where(low + k < high, 1.0, 0.0))
    put_lane = lax.rem(lanes_of((devices, 2 * pairs)), pairs)
    put_row = lax.broadcasted_iota(jnp.int32, (devices, 2 * pairs), 0)
    put = jnp.zeros((devices, 2 * pairs), F32)
    for n in range(pairs):
        put = jnp.where((put_lane == n) & (put_row == owners[n]), alive[n], put)
    put = put.astype(BF16)
    tile_sub = lax.broadcasted_iota(jnp.int32, (tiles, 128), 0)
    parts = []
    for k in range(TILE_MOST):
        part = jnp.zeros((tiles, 128), F32)
        for t in range(tiles):
            part = jnp.where(tile_sub == t, alive[k * tiles + t], part)
        parts.append(part)
    keep = jnp.concatenate(parts, axis=1) > 0.5

    plane = msg_in.at[pl.ds(0, views_n - 1)]
    pltpu.make_async_copy(plane, plane, recv_sem.at[0]).wait()
    pltpu.make_async_copy(plane, plane, send_sem.at[0]).wait()
    bundle = msg_in.at[pl.ds(band * views_n, views_n)]
    for d in range(1, bands_n):
        pltpu.make_async_remote_copy(
            src_ref=bundle,
            dst_ref=bundle,
            send_sem=send_sem.at[1],
            recv_sem=recv_sem.at[1],
            device_id=(view, peer_band[d]),
            device_id_type=MESH,
        ).start()

    fetches[5].wait()
    (sigma, opacity), pullback = jax.vjp(
        block_shape,
        [gauss_ref[6 + c] for c in range(3)],
        [gauss_ref[9 + c] for c in range(4)],
        gauss_ref[13],
    )
    rotation, scales = block_axes(
        [gauss_ref[6 + c] for c in range(3)], [gauss_ref[9 + c] for c in range(4)]
    )
    tabled = [gauss_ref[c] for c in range(6)] + [v for line in rotation for v in line] + scales
    for c, value in enumerate(tabled + [opacity]):
        both = stack3(value)
        for h in range(halves):
            geo_tab[h, c] = both[:, h * 128 : (h + 1) * 128]
    for ch in range(3):
        for q in range(BASIS):
            for n, piece in enumerate(split3(gauss_ref[14 + 3 * q + ch])):
                for h in range(halves):
                    tint_tab[
                        h, n, q * blocks : (q + 1) * blocks, ch * 128 : (ch + 1) * 128
                    ] = piece[:, h * 128 : (h + 1) * 128]

    lines = msg_in.at[pl.ds(0, devices - views_n)]
    pltpu.make_async_copy(lines, lines, recv_sem.at[1]).wait()
    pltpu.make_async_copy(lines, lines, send_sem.at[1]).wait()

    for p in range(devices):
        asked_ref[p : p + 1, :] = msg_in[p]
    asked = asked_ref[...]
    asked_parts = split3(asked)
    hot = mx(asked_parts[0], hot_map[...])
    hot_3 = hot[:, 0 : 3 * blocks].astype(BF16)

    def term(n):
        return asked[:, hot_lanes + n : hot_lanes + n + 1]

    ones = [term(c) for c in range(3)], [term(TERM_ROWS + c) for c in range(3)]
    shifts = [term(SHIFT_AT), term(SHIFT_AT + 1), term(SHIFT_AT + 2)]
    stacked = jnp.concatenate(asked_parts, axis=0)

    def widen(low, high):
        wide = mx(stacked, wide_map[:, low:high])
        return wide[0:devices] + wide[devices : 2 * devices] + wide[2 * devices :]

    hot_wide = jnp.concatenate([hot] * (basis_lanes // 128), axis=1)
    basis_parts = split3(widen(0, basis_lanes) * hot_wide)
    basis_three = jnp.concatenate(basis_parts, axis=0)

    def records_of(h):
        picked = [mx(hot_3, geo_tab[h, c]) for c in range(GEO_COMPS)]
        centre = [picked[c] + shifts[2] * picked[3 + c] for c in range(3)]
        turns, scales = [picked[6 + 3 * a : 9 + 3 * a] for a in range(3)], picked[15:18]

        def placed(row, shift):
            return row[0] * centre[0] + row[1] * centre[1] + row[2] * centre[2] + shift

        def turned(row, c):
            return (row[0] * turns[0][c] + row[1] * turns[1][c] + row[2] * turns[2][c]) * scales[c]

        m = [[turned(row, c) for c in range(3)] for row in ones]
        small = mx(basis_parts[0], tint_tab[h, 2])
        middle = mx(basis_three[0 : 2 * devices], tint_tab[h, 1])
        large = mx(basis_three, tint_tab[h, 0])
        colour = small + large[2 * devices :] + middle[devices:]
        colour = colour + (middle[0:devices] + large[devices : 2 * devices])
        colour = 0.5 + (colour + large[0:devices])
        return [
            placed(ones[0], shifts[0]),
            placed(ones[1], shifts[1]),
            m[0][0] * m[0][0] + m[0][1] * m[0][1] + m[0][2] * m[0][2] + 0.3,
            m[0][0] * m[1][0] + m[0][1] * m[1][1] + m[0][2] * m[1][2],
            m[1][0] * m[1][0] + m[1][1] * m[1][1] + m[1][2] * m[1][2] + 0.3,
            picked[18],
        ] + [colour[:, ch * 128 : (ch + 1) * 128] for ch in range(3)]

    for h in range(halves):
        flat_out = rec_out[h].reshape(devices * rec_out[h].shape[1], 128)
        for p, record in enumerate(records_of(h)):
            flat_out[pl.ds(p, devices, stride=rec_out[h].shape[1]), :] = record
        to_all(rec_out[h], rec_in[h], RECORDS, 2 + h)
        rec_in[h][me] = rec_out[h][me]

    tint_back[...] = jnp.concatenate([basis_parts[0], basis_parts[1], basis_parts[0]], axis=0)
    spans = [
        widen(basis_lanes + kind * 128, basis_lanes + (kind + 1) * 128) * hot for kind in range(5)
    ]
    hot_lane = lanes_of((devices, 128))
    hot_last = jnp.where(
        (hot_lane >= TERM_ROWS * blocks) & (hot_lane < (TERM_ROWS + 1) * blocks), hot, 0.0
    )
    for landing, group in ((line_back, spans[0:2] + [hot_last]), (shape_back, spans[2:5])):
        high, low = split2(jnp.concatenate(group, axis=0))
        landing[...] = jnp.concatenate([high, low, high], axis=0)

    for n in range(6, 12):
        fetches[n].wait()
    high, low = split2(second_ref[...])
    second_k[...] = jnp.concatenate([high, high, low], axis=1)
    high, low = split2(across_ref[...])
    across_k[...] = jnp.concatenate([high, high, low], axis=0)
    edges_wait(thalo_out, thalo_in, 0)
    in_rows, mid_rows = up8(rows + 2 * REACH), up8(rows + REACH)
    high_rows = 3 * mid_rows
    fill = jnp.zeros((in_rows - rows - 2 * REACH, cols), F32)

    def smooth(fields):
        down = jnp.dot(
            first_ref[...],
            jnp.concatenate(fields, axis=1),
            precision=HIGHEST_MODE,
            preferred_element_type=F32,
        )
        stack = jnp.concatenate(
            [down[:, f * cols : (f + 1) * cols] for f in range(len(fields))], axis=0
        )
        flat = jnp.dot(
            stack, across_ref[...], precision=HIGHEST_MODE, preferred_element_type=F32
        )
        return [flat[f * high_rows : (f + 1) * high_rows] for f in range(len(fields))]

    mine = target_ref[0]
    ext_y = jnp.concatenate(
        [v for ch in range(3) for v in (thalo_in[0, ch], mine[ch], thalo_in[1, ch], fill)], axis=0
    )
    mean_y, square_y = smooth([ext_y, ext_y * ext_y])

    tile_row = lax.broadcasted_iota(jnp.int32, (tiles, pair_len), 0).astype(F32)
    column = lax.rem(lanes_of((128, cols)), TILE).astype(F32) + (0.5 - 0.5 * TILE)

    def prepare(h):
        for k in range(TILE_MOST):
            for t in range(tiles):
                rec_pick[h, k, pl.ds(t, RECORDS, stride=tiles), :] = rec_in[h][
                    owners[k * tiles + t], 0:RECORDS, :
                ]

        def gathered(p):
            return jnp.concatenate(
                [rec_pick[h, k, p * tiles : (p + 1) * tiles, :] for k in range(TILE_MOST)], axis=1
            )

        u_rel = gathered(0) - (tile_row * TILE + 0.5 * TILE)
        w_rel = gathered(1) - ((band * rows).astype(F32) + 0.5 * TILE)
        c_a, c_b, c_c, opac = [gathered(p) for p in range(2, GEO_REC)]
        inv_det = 1.0 / (c_a * c_c - c_b * c_b)
        coef_a = -0.5 * c_c * inv_det
        coef_b = c_b * inv_det
        coef_c = -0.5 * c_a * inv_det

        def masked(value, other=0.0):
            return jnp.where(keep, value, other)

        quads = jnp.concatenate(
            [
                masked(LOG2_E * jnp.log(opac), NEVER),
                LOG2_E * coef_a,
                LOG2_E * coef_b,
                LOG2_E * coef_c,
                u_rel,
                w_rel,
            ],
            axis=0,
        )
        tones = jnp.concatenate(
            [masked(gathered(GEO_REC + ch)) for ch in range(3)], axis=0
        )
        grown = [
            mx(stack3(quads), quad_ref[...], TN),
            mx(stack3(tones), tone_ref[...], TN),
        ]
        for k in range(TILE_MOST):
            at = k * block_len + h * 128
            flat, part_a, part_b, part_c, u_wide, w_wide = [
                grown[0][k * 128 : (k + 1) * 128, n * cols : (n + 1) * cols] for n in range(6)
            ]
            e_x = column - u_wide
            coef[0, at : at + 128, :] = flat + part_a * e_x * e_x
            coef[1, at : at + 128, :] = part_b * e_x
            coef[2, at : at + 128, :] = part_c
            coef[6, at : at + 128, :] = w_wide
            for ch in range(3):
                coef[3 + ch, at : at + 128, :] = grown[1][
                    k * 128 : (k + 1) * 128, ch * cols : (ch + 1) * cols
                ]
        return u_rel, w_rel, c_a, c_b, c_c, opac, inv_det, coef_a, coef_b, coef_c

    wait_all(rec_in[0], RECORDS, 2)
    shapes = [prepare(0)]

    sub8 = lax.broadcasted_iota(jnp.int32, (8, cols), 0).astype(F32)
    parts_n = rows // 8
    row_local = [sub8 + (8.0 * part + 0.5 - 0.5 * TILE) for part in range(parts_n)]

    def spread_row(kind, j):
        return coef[kind, pl.ds(j, 8, stride=0), :]

    def blend(group, carry):
        trans, image = carry
        trans, image = list(trans), list(image)
        for k in range(8):
            j = group * 8 + k
            q0, q1, q2 = spread_row(0, j), spread_row(1, j), spread_row(2, j)
            low = spread_row(6, j)
            tint = [spread_row(3 + ch, j) for ch in range(3)]
            for part in range(parts_n):
                e_y = row_local[part] - low
                alpha = jnp.exp2(q0 + e_y * (q1 + e_y * q2))
                weight = alpha * trans[part]
                alpha_s[j, part] = alpha
                weight_s[j, part] = weight
                trans[part] = trans[part] * (1.0 - alpha)
                for ch in range(3):
                    at = ch * parts_n + part
                    image[at] = image[at] + weight * tint[ch]
        return tuple(trans), tuple(image)

    zero = jnp.zeros((8, cols), F32)
    state = (tuple([zero + 1.0] * parts_n), tuple([zero] * (3 * parts_n)))
    state = lax.fori_loop(0, 128 // 8, blend, state, unroll=UNROLL)
    for h in range(1, halves):
        wait_all(rec_in[h], RECORDS, 2 + h)
        shapes.append(prepare(h))
    _, image = lax.fori_loop(128 // 8, window // 8, blend, state, unroll=UNROLL)
    pred = [
        jnp.concatenate([image[ch * parts_n + part] for part in range(parts_n)], axis=0)
        for ch in range(3)
    ]
    for ch in range(3):
        halo_out[0, ch] = pred[ch][0:REACH]
        halo_out[1, ch] = pred[ch][rows - REACH : rows]
    edges_start(halo_out, halo_in, 1)
    edges_wait(halo_out, halo_in, 1)

    ext_x = jnp.concatenate(
        [v for ch in range(3) for v in (halo_in[0, ch], pred[ch], halo_in[1, ch], fill)], axis=0
    )
    mean_x, square_x, cross = smooth([ext_x, ext_x * ext_x, ext_x * ext_y])
    n_mean = 2.0 * mean_x * mean_y + STAB_MEAN
    n_var = 2.0 * (cross - mean_x * mean_y) + STAB_VAR
    d_mean = mean_x * mean_x + mean_y * mean_y + STAB_MEAN
    d_var = (square_x - mean_x * mean_x) + (square_y - mean_y * mean_y) + STAB_VAR
    inv_mean = 1.0 / d_mean
    inv_var = 1.0 / d_var
    inverse = inv_mean * inv_var
    ssim = n_mean * n_var * inverse
    ext_row = lax.broadcasted_iota(jnp.int32, (high_rows, cols), 0) % mid_rows
    image_row = ext_row + (band * rows - HALO)
    inside = (image_row >= 0) & (image_row < bands_n * rows) & (ext_row < rows + REACH)
    scale = -SSIM_WEIGHT / 3.0
    part_mean = 2.0 * mean_y * (n_var - n_mean) * inverse - 2.0 * mean_x * ssim * (
        inv_mean - inv_var
    )
    adjoint = jnp.concatenate(
        [
            jnp.where(inside, scale * part_mean, 0.0),
            jnp.where(inside, -scale * ssim * inv_var, 0.0),
            jnp.where(inside, (2.0 * scale) * n_mean * inverse, 0.0),
        ],
        axis=1,
    )
    high, low = split2(adjoint)
    down2 = mx(second_k[...], jnp.concatenate([high, low, high], axis=0))
    stacked2 = jnp.concatenate([down2[:, f * cols : (f + 1) * cols] for f in range(3)], axis=0)
    high, low = split2(stacked2)
    spread = mx(jnp.concatenate([high, low, high], axis=1), across_k[...])
    deep = 3 * rows
    pred_all = jnp.concatenate(pred, axis=0)
    mine_all = jnp.concatenate([mine[ch] for ch in range(3)], axis=0)
    error = pred_all - mine_all
    sign = jnp.where(error > 0.0, 1.0, jnp.where(error < 0.0, -1.0, 0.0))
    grad_pred = (
        ABS_WEIGHT / 3.0 * sign
        + spread[0:deep]
        + 2.0 * pred_all * spread[deep : 2 * deep]
        + mine_all * spread[2 * deep : 3 * deep]
    )
    own = (ext_row >= HALO) & (ext_row < HALO + rows)
    loss = jnp.sum(ABS_WEIGHT / 3.0 * jnp.abs(error), keepdims=True) + jnp.sum(
        jnp.where(own, SSIM_WEIGHT / 3.0 * (1.0 - ssim), 0.0), keepdims=True
    )

    pull = [
        [grad_pred[ch * rows + 8 * part : ch * rows + 8 * part + 8] for part in range(parts_n)]
        for ch in range(3)
    ]

    def shades(group, carry):
        sums = [[None] * 8 for _ in range(3)]
        for k in range(8):
            j = group * 8 + k
            weight = [weight_s[j, part] for part in range(parts_n)]
            for ch in range(3):
                total = weight[0] * pull[ch][0]
                for part in range(1, parts_n):
                    total = total + weight[part] * pull[ch][part]
                sums[ch][k] = total
        at = pl.multiple_of(group * 8, 8)
        for ch in range(3):
            moment_s[3 + ch, pl.ds(at, 8), :] = tree_sum(sums[ch], cols)
        return carry

    lax.fori_loop(0, window // 8, shades, 0, unroll=UNROLL)

    def route(value, length):
        stack = jnp.concatenate(
            [value[:, k * length : (k + 1) * length] for k in range(TILE_MOST)], axis=0
        )
        return mx(put, stack2(stack))

    power = power_ref[...]
    power_low = power[0:tiles].astype(BF16)
    shade_flat = shade_out.reshape(devices * shade_out.shape[1], 128)
    for ch in range(3):
        high, low = split2(moment_s[3 + ch])
        routed = route(mx(power_low, high, NT) + mx(power_low, low, NT), block_len)
        for h in range(halves):
            shade_flat[pl.ds(ch * halves + h, devices, stride=shade_out.shape[1]), :] = routed[
                :, h * 128 : (h + 1) * 128
            ]
    shade_flat[pl.ds(tint_rows, devices, stride=shade_out.shape[1]), :] = jnp.broadcast_to(
        loss, (devices, 128)
    )
    to_all(shade_out, shade_in, tint_rows + 1, 2 + halves)
    shade_in[me] = shade_out[me]

    def unblend(step, behind):
        group = window // 8 - 1 - step
        behind = list(behind)
        sums = [[None] * 8 for _ in range(3)]
        for k in reversed(range(8)):
            j = group * 8 + k
            tint = [spread_row(3 + ch, j) for ch in range(3)]
            totals = [None] * 3
            for part in range(parts_n):
                alpha = alpha_s[j, part]
                shade = (
                    tint[0] * pull[0][part] + tint[1] * pull[1][part] + tint[2] * pull[2][part]
                )
                gap = shade - behind[part]
                behind[part] = behind[part] + alpha * gap
                lean = weight_s[j, part] * gap
                lean_r = lean * row_local[part]
                terms = [lean, lean_r, lean_r * row_local[part]]
                totals = [
                    value if total is None else total + value
                    for value, total in zip(terms, totals)
                ]
            for kind in range(3):
                sums[kind][k] = totals[kind]
        at = pl.multiple_of(group * 8, 8)
        for kind in range(3):
            moment_s[kind, pl.ds(at, 8), :] = tree_sum(sums[kind], cols)
        return tuple(behind)

    def derive(h):
        u_rel, w_rel, c_a, c_b, c_c, opac, inv_det, coef_a, coef_b, coef_c = shapes[h]
        moments = [
            jnp.concatenate(
                [
                    moment_s[n, k * block_len + h * 128 : k * block_len + (h + 1) * 128, :]
                    for k in range(TILE_MOST)
                ],
                axis=0,
            )
            for n in range(3)
        ]
        by_x = exact_dot(power, moments[0], NT)
        m_00, m_10, m_20 = by_x[0:tiles], by_x[tiles : 2 * tiles], by_x[2 * tiles : 3 * tiles]
        by_xr = exact_dot(power[0 : 2 * tiles], moments[1], NT)
        m_01, m_11 = by_xr[0:tiles], by_xr[tiles : 2 * tiles]
        m_02 = exact_dot(power[0:tiles], moments[2], NT)
        s_x = m_10 - u_rel * m_00
        s_y = m_01 - w_rel * m_00
        s_xx = m_20 - 2.0 * u_rel * m_10 + u_rel * u_rel * m_00
        s_xy = m_11 - u_rel * m_01 - w_rel * m_10 + u_rel * w_rel * m_00
        s_yy = m_02 - 2.0 * w_rel * m_01 + w_rel * w_rel * m_00
        by_det = -(coef_a * s_xx + coef_b * s_xy + coef_c * s_yy) * inv_det
        derivs = [
            -(2.0 * coef_a * s_x + coef_b * s_y),
            -(2.0 * coef_c * s_y + coef_b * s_x),
            -0.5 * inv_det * s_yy + by_det * c_c,
            inv_det * s_xy - 2.0 * c_b * by_det,
            -0.5 * inv_det * s_xx + by_det * c_a,
            m_00 / opac,
        ]
        flat_out = grad_out[h].reshape(devices * grad_out[h].shape[1], 128)
        for p in range(GEO_REC):
            flat_out[pl.ds(p, devices, stride=grad_out[h].shape[1]), :] = route(derivs[p], 128)
        to_all(grad_out[h], grad_in[h], GEO_REC, 2 + halves + 1 + h)
        grad_in[h][me] = grad_out[h][me]

    groups = window // 8
    last = groups - 128 // 8
    behind = lax.fori_loop(0, last, unblend, tuple([zero] * parts_n), unroll=UNROLL)
    for h in range(halves - 1, 0, -1):
        derive(h)
    lax.fori_loop(last, groups, unblend, behind, unroll=UNROLL)
    derive(0)
    wait_all(shade_in, tint_rows + 1, 2 + halves)
    shade_back = shade_in.reshape(devices * shade_in.shape[1], 128)

    def arrived(landed, stride, p):
        return jnp.concatenate(
            [landed[pl.ds(p * halves + h, devices, stride=stride), :] for h in range(halves)],
            axis=1,
        )

    def spread_back(table, values):
        high, low = split2(jnp.concatenate(values, axis=0))
        return mx(table[...], jnp.concatenate([high, high, low], axis=0), TN)

    for ch in range(3):
        colour = spread_back(tint_back, [arrived(shade_back, shade_in.shape[1], ch)])
        for q in range(BASIS):
            grad_ref[14 + 3 * q + ch] = colour[q * blocks : (q + 1) * blocks]
    losses = shade_back[pl.ds(tint_rows, devices, stride=shade_in.shape[1]), :]
    loss_ref[...] = jnp.sum(losses, axis=0, keepdims=True)[:, 0:1] * (
        1.0 / (devices * rows * cols)
    )
    fetches[12].wait()
    fetches[13].wait()

    def update(c, carry):
        adam_step(c, grad_ref, (gauss_ref, one_ref, two_ref), (gauss_ref, one_ref, two_ref))
        return carry

    lax.fori_loop(SHAPE_COMPS, gauss_ref.shape[0], update, 0, unroll=4)

    for h in range(halves - 1, -1, -1):
        wait_all(grad_in[h], GEO_REC, 2 + halves + 1 + h)
    grad_back = [
        grad_in[h].reshape(devices * grad_in[h].shape[1], 128) for h in range(halves)
    ]
    geos = [
        jnp.concatenate(
            [back[pl.ds(p, devices, stride=grad_in[0].shape[1]), :] for back in grad_back], axis=1
        )
        for p in range(GEO_REC)
    ]
    line = spread_back(line_back, [geos[0], geos[1], geos[5]])
    shape = spread_back(shape_back, geos[2:5])

    def comp(value, n):
        return value[n * blocks : (n + 1) * blocks]

    d_logs, d_quats, d_logit = pullback(
        ([comp(shape, n) for n in range(TERM_ROWS)], comp(line, TERM_ROWS))
    )
    columns = [comp(line, n) for n in range(TERM_ROWS)] + list(d_logs) + list(d_quats) + [d_logit]
    for c, value in enumerate(columns):
        grad_ref[c] = value


def adam_kernel(
    grad_ref,
    gauss_ref,
    one_ref,
    two_ref,
    loss_in,
    out_gauss,
    out_one,
    out_two,
    out_grad,
    loss_out,
    gauss_v,
    one_v,
    two_v,
    write_sem,
):
    comps = gauss_ref.shape[0]
    held = [(grad_ref, out_grad), (gauss_ref, out_gauss), (one_ref, out_one), (two_ref, out_two)]
    fresh = [(gauss_v, out_gauss), (one_v, out_one), (two_v, out_two)]
    copies = [pltpu.make_async_copy(loss_in, loss_out, write_sem.at[4, 0])]
    copies[0].start()

    def send(group, low, high, slot):
        part = pl.ds(low, high - low)
        for n, (source, landing) in enumerate(group):
            copy = pltpu.make_async_copy(
                source.at[part], landing.at[part], write_sem.at[n, slot]
            )
            copy.start()
            copies.append(copy)

    for piece in range(PIECES):
        low = SHAPE_COMPS + piece * (comps - SHAPE_COMPS) // PIECES
        high = SHAPE_COMPS + (piece + 1) * (comps - SHAPE_COMPS) // PIECES
        send(held, low, high, piece)
    send(held[0:1], 0, SHAPE_COMPS, PIECES)
    for c in range(SHAPE_COMPS):
        adam_step(c, grad_ref, (gauss_ref, one_ref, two_ref), (gauss_v, one_v, two_v))
    send(fresh, 0, SHAPE_COMPS, PIECES + 1)
    for copy in copies:
        copy.wait()


def wide_table(tiles, cols, kinds):
    belongs = (np.arange(cols)[None, :] // TILE == np.arange(tiles)[:, None]).astype(np.float32)
    return np.tile(np.kron(np.eye(kinds, dtype=np.float32), belongs), (3, 1))


def per_device(
    gaussians,
    first_moment,
    second_moment,
    camera,
    target,
    block_list,
    block_count,
    tile_start,
    tile_end,
):
    views_n = lax.axis_size("view")
    bands_n = lax.axis_size("band")
    devices = views_n * bands_n
    blocks, comps, block_len = gaussians.shape
    list_len = block_list.shape[2]
    rows, cols = target.shape[2:]
    tiles = cols // TILE
    halves = block_len // 128
    geometry = (views_n, bands_n, blocks, list_len, rows, cols, block_len)

    across, first, second = smoothing_tables(rows, cols, 3)
    power = power_table(tiles, cols)
    quad = wide_table(tiles, cols, 6).astype(BF16)
    tone = wide_table(tiles, cols, 3).astype(BF16)
    vmem = pl.BlockSpec(memory_space=pltpu.VMEM)
    hbm = pl.BlockSpec(memory_space=pltpu.HBM)

    def by_comp(array):
        return jnp.transpose(array, (1, 0, 2))

    window = TILE_MOST * block_len
    tint_pad = up8(3 * halves + 1)
    basis_lanes = BASIS * blocks
    shape = jax.ShapeDtypeStruct((comps, blocks, block_len), F32)
    scalar = jax.ShapeDtypeStruct((1, 1), F32)
    kept = pltpu.VMEM(shape.shape, F32)
    gradient, params, one, two, mean_loss = pl.pallas_call(
        functools.partial(step_kernel, geometry),
        out_shape=(kept, kept, kept, kept, pltpu.VMEM((1, 1), F32)),
        in_specs=[hbm] * 14,
        out_specs=(vmem,) * 5,
        scratch_shapes=[
            pltpu.SMEM((1, 9), F32),
            pltpu.SMEM((1, 1, list_len), jnp.int32),
            pltpu.SMEM((1, 1, tiles), jnp.int32),
            pltpu.SMEM((1, 1, tiles), jnp.int32),
            pltpu.VMEM((1, 3, rows, cols), F32),
            pltpu.VMEM(across.shape, F32),
            pltpu.VMEM(first.shape, F32),
            pltpu.VMEM(second.shape, F32),
            pltpu.VMEM((second.shape[0], 3 * second.shape[1]), BF16),
            pltpu.VMEM((3 * cols, cols), BF16),
            pltpu.VMEM(power.shape, F32),
            pltpu.VMEM(quad.shape, BF16),
            pltpu.VMEM(tone.shape, BF16),
            pltpu.VMEM((views_n, 1, 128), F32),
            pltpu.VMEM((devices, 1, 128), F32),
            pltpu.VMEM((devices, 128), F32),
            pltpu.VMEM((128, 128), BF16),
            pltpu.VMEM((128, basis_lanes + 5 * 128), BF16),
            pltpu.VMEM((halves, GEO_COMPS, 3 * blocks, 128), BF16),
            pltpu.VMEM((halves, 3, basis_lanes, 3 * 128), BF16),
            pltpu.VMEM((3 * devices, basis_lanes), BF16),
            pltpu.VMEM((9 * devices, 128), BF16),
            pltpu.VMEM((9 * devices, 128), BF16),
            (pltpu.VMEM((devices, up8(RECORDS), 128), F32),) * halves,
            (pltpu.VMEM((devices, up8(RECORDS), 128), F32),) * halves,
            pltpu.VMEM((halves, TILE_MOST, RECORDS * tiles, 128), F32),
            pltpu.VMEM((devices, tint_pad, 128), F32),
            pltpu.VMEM((devices, tint_pad, 128), F32),
            (pltpu.VMEM((devices, up8(GEO_REC), 128), F32),) * halves,
            (pltpu.VMEM((devices, up8(GEO_REC), 128), F32),) * halves,
            pltpu.VMEM((2, 3, REACH, cols), F32),
            pltpu.VMEM((2, 3, REACH, cols), F32),
            pltpu.VMEM((2, 3, REACH, cols), F32),
            pltpu.VMEM((2, 3, REACH, cols), F32),
            pltpu.VMEM((7, window, cols), F32),
            pltpu.VMEM((window, rows // 8, 8, cols), F32),
            pltpu.VMEM((window, rows // 8, 8, cols), F32),
            pltpu.VMEM((6, window, cols), F32),
            pltpu.SemaphoreType.DMA((3 + 2 * halves,)),
            pltpu.SemaphoreType.DMA((3 + 2 * halves,)),
            pltpu.SemaphoreType.DMA((2, 2)),
            pltpu.SemaphoreType.DMA((2, 2)),
            pltpu.SemaphoreType.DMA((14,)),
        ],
        compiler_params=pltpu.CompilerParams(
            collective_id=0, has_side_effects=True, vmem_limit_bytes=40 * 1024 * 1024
        ),
        name="render_step",
    )(
        *[
            pltpu.with_memory_space_constraint(array, pltpu.HBM)
            for array in (
                camera,
                block_list,
                tile_start,
                tile_end,
                target,
                by_comp(gaussians),
                by_comp(first_moment),
                by_comp(second_moment),
                across,
                first,
                second,
                power,
                quad,
                tone,
            )
        ]
    )

    new_params, new_one, new_two, out_gradient, out_loss = pl.pallas_call(
        adam_kernel,
        out_shape=(shape, shape, shape, shape, scalar),
        in_specs=[vmem] * 5,
        out_specs=(hbm, hbm, hbm, hbm, hbm),
        scratch_shapes=[pltpu.VMEM((SHAPE_COMPS, blocks, block_len), F32)] * 3
        + [pltpu.SemaphoreType.DMA((5, PIECES + 2))],
        compiler_params=pltpu.CompilerParams(vmem_limit_bytes=16 * 1024 * 1024),
        name="adam_step",
    )(gradient, params, one, two, mean_loss)
    return (
        by_comp(new_params),
        by_comp(new_one),
        by_comp(new_two),
        out_loss.reshape(()),
        by_comp(out_gradient),
    )


def solution(mesh):
    return jax.shard_map(
        per_device,
        mesh=mesh,
        in_specs=(
            P(("view", "band"), None, None),
            P(("view", "band"), None, None),
            P(("view", "band"), None, None),
            P("view", None),
            P("view", None, "band", None),
            P("view", "band", None),
            P("view", "band"),
            P("view", "band", None),
            P("view", "band", None),
        ),
        out_specs=(
            P(("view", "band"), None, None),
            P(("view", "band"), None, None),
            P(("view", "band"), None, None),
            P(),
            P(("view", "band"), None, None),
        ),
        check_vma=False,
    )
```

```python
import functools
import math

import jax
import jax.numpy as jnp
import numpy as np
from jax import lax
from jax.experimental import pallas as pl
from jax.experimental.pallas import tpu as pltpu
from jax.sharding import PartitionSpec as P

TILE = 16
TILE_MOST = 2
HALO = 5
REACH = 2 * HALO
GEO_REC = 6
RECORDS = 9
PIECES = 3
SHAPE_COMPS = 14
UNROLL = 4

HIGHEST_MODE = lax.Precision.HIGHEST
SSIM_WEIGHT = 0.2
ABS_WEIGHT = 0.8
STAB_MEAN = 0.0001
STAB_VAR = 0.0009
BIAS_FIRST = 1.0 - math.exp(100.0 * math.log(0.9))
BIAS_SECOND = 1.0 - math.exp(100.0 * math.log(0.999))
LOG2_E = math.log2(math.e)
SH_ZERO = 0.28209479177387814
SH_ONE = 0.4886025119029199
SH_TWO = [
    1.0925484305920792,
    -1.0925484305920792,
    0.31539156525252005,
    -1.0925484305920792,
    0.5462742152960396,
]
SH_THREE = [
    -0.5900435899266435,
    2.890611442640554,
    -0.4570457994644658,
    0.3731763325901154,
    -0.4570457994644658,
    1.445305721320277,
    -0.5900435899266435,
]
F32 = jnp.float32
BF16 = jnp.bfloat16
MESH = pl.DeviceIdType.MESH
NEVER = -1e30


RATES = ((6, 0.016), (9, 0.005), (13, 0.001), (14, 0.05), (17, 0.0025), (62, 0.000125))


def learning_rate(component):
    rate = RATES[-1][1] / BIAS_FIRST
    if isinstance(component, int):
        return next(value for end, value in RATES if component < end) / BIAS_FIRST
    for end, value in reversed(RATES[:-1]):
        rate = jnp.where(component < end, value / BIAS_FIRST, rate)
    return rate


def kernel_taps():
    raw_taps = [math.exp(-(offset * offset) / 4.5) for offset in range(-5, 6)]
    tap_total = sum(raw_taps)
    return [raw_tap / tap_total for raw_tap in raw_taps]


def up8(value):
    return (value + 7) // 8 * 8


def smoothing_tables(rows, cols, channels):
    taps = kernel_taps()
    in_rows, mid_rows = up8(rows + 2 * REACH), up8(rows + REACH)
    across = np.zeros((cols, cols), np.float32)
    for out in range(cols):
        for m in range(-HALO, HALO + 1):
            if 0 <= out + m < cols:
                across[out + m, out] = taps[m + HALO]
    first = np.zeros((channels * mid_rows, channels * in_rows), np.float32)
    second = np.zeros((channels * rows, channels * mid_rows), np.float32)
    for c in range(channels):
        for e in range(rows + REACH):
            for m in range(REACH + 1):
                first[c * mid_rows + e, c * in_rows + e + m] = taps[m]
        for i in range(rows):
            for m in range(REACH + 1):
                second[c * rows + i, c * mid_rows + i + m] = taps[m]
    return across, first, second


def power_table(tiles, cols):
    lane = np.arange(cols)
    local = lane % TILE + 0.5 - TILE / 2
    belongs = (lane[None, :] // TILE == np.arange(tiles)[:, None]).astype(np.float32)
    return np.concatenate([belongs, belongs * local, belongs * local * local]).astype(np.float32)


def harmonics(dir_x, dir_y, dir_z):
    sq_x, sq_y, sq_z = (dir_x * dir_x, dir_y * dir_y, dir_z * dir_z)
    return [
        SH_ZERO + 0.0 * dir_x,
        -SH_ONE * dir_y,
        SH_ONE * dir_z,
        -SH_ONE * dir_x,
        SH_TWO[0] * dir_x * dir_y,
        SH_TWO[1] * dir_y * dir_z,
        SH_TWO[2] * (2.0 * sq_z - sq_x - sq_y),
        SH_TWO[3] * dir_x * dir_z,
        SH_TWO[4] * (sq_x - sq_y),
        SH_THREE[0] * dir_y * (3.0 * sq_x - sq_y),
        SH_THREE[1] * dir_x * dir_y * dir_z,
        SH_THREE[2] * dir_y * (4.0 * sq_z - sq_x - sq_y),
        SH_THREE[3] * dir_z * (2.0 * sq_z - 3.0 * sq_x - 3.0 * sq_y),
        SH_THREE[4] * dir_x * (4.0 * sq_z - sq_x - sq_y),
        SH_THREE[5] * dir_z * (sq_x - sq_y),
        SH_THREE[6] * dir_x * (sq_x - 3.0 * sq_y),
    ]


def camera_basis(affine):
    a, b = affine[0:3], affine[3:6]
    n_x = a[1] * b[2] - a[2] * b[1]
    n_y = a[2] * b[0] - a[0] * b[2]
    n_z = a[0] * b[1] - a[1] * b[0]
    length = jnp.sqrt(n_x * n_x + n_y * n_y + n_z * n_z)
    return harmonics(n_x / length, n_y / length, n_z / length)


def split3(value, axis=0):
    high = value.astype(BF16)
    rest = value - high.astype(F32)
    middle = rest.astype(BF16)
    low = (rest - middle.astype(F32)).astype(BF16)
    return high, middle, low


NN = ((1,), (0,))
NT = ((1,), (1,))
TN = ((0,), (0,))


def mx(a, b, dims=NN):
    return lax.dot_general(a, b, (dims, ((), ())), preferred_element_type=F32)


def split2(value):
    high = value.astype(BF16)
    return high, (value - high.astype(F32)).astype(BF16)


def stack3(value):
    return jnp.concatenate(split3(value), axis=0)


def stack2(value):
    return jnp.concatenate(split2(value), axis=0)


def exact_dot(table, value, dims):
    table = table.astype(BF16)
    total = None
    for part in split3(value):
        term = mx(table, part, dims)
        total = term if total is None else total + term
    return total


def adam_step(c, grad_ref, source, landing):
    gradient = grad_ref[c]
    new_one = 0.9 * source[1][c] + 0.1 * gradient
    new_two = 0.999 * source[2][c] + 0.001 * gradient * gradient
    landing[1][c] = new_one
    landing[2][c] = new_two
    bottom = jnp.sqrt(new_two * (1.0 / BIAS_SECOND)) + 1e-08
    landing[0][c] = source[0][c] - learning_rate(c) * new_one / bottom


def block_axes(logs, quats):
    scales = [jnp.exp(value) for value in logs]
    quat_len = jnp.sqrt(
        quats[0] * quats[0] + quats[1] * quats[1] + quats[2] * quats[2] + quats[3] * quats[3]
    )
    r, i, j, k = [value / quat_len for value in quats]
    rotation = [
        [1.0 - 2.0 * (j * j + k * k), 2.0 * (i * j - r * k), 2.0 * (i * k + r * j)],
        [2.0 * (i * j + r * k), 1.0 - 2.0 * (i * i + k * k), 2.0 * (j * k - r * i)],
        [2.0 * (i * k - r * j), 2.0 * (j * k + r * i), 1.0 - 2.0 * (i * i + j * j)],
    ]
    return rotation, scales


def block_shape(logs, quats, logit):
    rotation, scales = block_axes(logs, quats)
    axes = [[rotation[a][c] * scales[c] for c in range(3)] for a in range(3)]

    def moment(a, b):
        return axes[a][0] * axes[b][0] + axes[a][1] * axes[b][1] + axes[a][2] * axes[b][2]

    pairs = ((0, 0), (1, 1), (2, 2), (0, 1), (0, 2), (1, 2))
    return [moment(a, b) for a, b in pairs], 1.0 / (1.0 + jnp.exp(-logit))


def view_terms(cam):
    a, b, time = cam[0:3], cam[3:6], cam[8]
    terms = a + [time * value for value in a] + b + [time * value for value in b]
    crossed = ((0, 1), (0, 2), (1, 2))
    terms += [a[c] * a[c] for c in range(3)] + [2.0 * a[c] * a[d] for c, d in crossed]
    terms += [a[c] * b[c] for c in range(3)] + [a[c] * b[d] + a[d] * b[c] for c, d in crossed]
    terms += [b[c] * b[c] for c in range(3)] + [2.0 * b[c] * b[d] for c, d in crossed]
    return terms + [cam[6], cam[7], time] + camera_basis(cam[0:6])


TERM_ROWS = 6
SHIFT_AT = 30
BASIS_AT = 33
BASIS = 16
TERMS = 49
GEO_COMPS = 19


def step_kernel(
    geometry,
    camera_hbm,
    list_hbm,
    start_hbm,
    end_hbm,
    target_hbm,
    gauss_hbm,
    one_hbm,
    two_hbm,
    across_hbm,
    first_hbm,
    second_hbm,
    power_hbm,
    quad_hbm,
    tone_hbm,
    grad_ref,
    gauss_ref,
    one_ref,
    two_ref,
    loss_ref,
    camera_s,
    list_s,
    start_s,
    end_s,
    target_ref,
    across_ref,
    first_ref,
    second_ref,
    second_k,
    across_k,
    power_ref,
    quad_ref,
    tone_ref,
    msg_out,
    msg_in,
    asked_ref,
    loss_v,
    hot_map,
    wide_map,
    geo_tab,
    tint_tab,
    tint_back,
    line_back,
    shape_back,
    rec_out,
    rec_in,
    rec_pick,
    shade_out,
    shade_in,
    grad_out,
    grad_in,
    halo_out,
    halo_in,
    thalo_out,
    thalo_in,
    coef,
    alpha_s,
    weight_s,
    moment_s,
    send_sem,
    recv_sem,
    halo_send,
    halo_recv,
    fetch_sem,
):
    views_n, bands_n, blocks, list_len, rows, cols, block_len = geometry
    devices = views_n * bands_n
    tiles = cols // TILE
    pairs = TILE_MOST * tiles
    window = TILE_MOST * block_len
    halves = block_len // 128
    pair_len = TILE_MOST * 128
    tint_rows = 3 * halves
    hot_lanes = bands_n * blocks
    basis_lanes = BASIS * blocks
    view = lax.axis_index("view")
    band = lax.axis_index("band")
    me = band * views_n + view
    has_up = band > 0
    has_down = band < bands_n - 1

    halo_in[...] = jnp.zeros_like(halo_in)
    thalo_in[...] = jnp.zeros_like(thalo_in)
    peer_view = [lax.rem(view + d, views_n) for d in range(views_n)]
    peer_band = [lax.rem(band + d, bands_n) for d in range(bands_n)]
    barrier = pltpu.get_barrier_semaphore()
    for d in range(1, views_n):
        pl.semaphore_signal(barrier, inc=1, device_id=(peer_view[d], band), device_id_type=MESH)
    for d in range(1, bands_n):
        pl.semaphore_signal(barrier, inc=1, device_id=(view, peer_band[d]), device_id_type=MESH)

    sources = (
        (camera_hbm, camera_s),
        (list_hbm, list_s),
        (start_hbm, start_s),
        (end_hbm, end_s),
        (target_hbm, target_ref),
        (gauss_hbm, gauss_ref),
        (quad_hbm, quad_ref),
        (tone_hbm, tone_ref),
        (power_hbm, power_ref),
        (across_hbm, across_ref),
        (first_hbm, first_ref),
        (second_hbm, second_ref),
        (one_hbm, one_ref),
        (two_hbm, two_ref),
    )
    fetches = [
        pltpu.make_async_copy(source, landing, fetch_sem.at[n])
        for n, (source, landing) in enumerate(sources)
    ]
    for fetch in fetches:
        fetch.start()

    def to_all(source, landing, length, phase):
        for d_view in range(views_n):
            for d_band in range(bands_n):
                if d_view + d_band == 0:
                    continue
                peer = peer_band[d_band] * views_n + peer_view[d_view]
                pltpu.make_async_remote_copy(
                    src_ref=source.at[peer, pl.ds(0, length)],
                    dst_ref=landing.at[me, pl.ds(0, length)],
                    send_sem=send_sem.at[phase],
                    recv_sem=recv_sem.at[phase],
                    device_id=(peer_view[d_view], peer_band[d_band]),
                    device_id_type=MESH,
                ).start()

    def wait_all(landing, length, phase):
        every = landing.at[pl.ds(0, devices - 1), pl.ds(0, length)]
        pltpu.make_async_copy(every, every, recv_sem.at[phase]).wait()
        pltpu.make_async_copy(every, every, send_sem.at[phase]).wait()

    def edge_copy(source, landing, direction, phase):
        step = -1 if direction == 0 else 1
        return pltpu.make_async_remote_copy(
            src_ref=source.at[direction],
            dst_ref=landing.at[1 - direction],
            send_sem=halo_send.at[phase, direction],
            recv_sem=halo_recv.at[phase, 1 - direction],
            device_id=(view, band + step),
            device_id_type=MESH,
        )

    def edges_start(source, landing, phase):
        @pl.when(has_up)
        def _():
            edge_copy(source, landing, 0, phase).start()

        @pl.when(has_down)
        def _():
            edge_copy(source, landing, 1, phase).start()

    def edges_wait(source, landing, phase):
        @pl.when(has_up)
        def _():
            up = edge_copy(source, landing, 0, phase)
            up.wait_send()
            pltpu.make_async_copy(
                landing.at[0], landing.at[0], halo_recv.at[phase, 0]
            ).wait()

        @pl.when(has_down)
        def _():
            down = edge_copy(source, landing, 1, phase)
            down.wait_send()
            pltpu.make_async_copy(
                landing.at[1], landing.at[1], halo_recv.at[phase, 1]
            ).wait()

    def lanes_of(shape):
        return lax.broadcasted_iota(jnp.int32, shape, len(shape) - 1)

    map_lane = lanes_of((128, 128))
    map_row = lax.broadcasted_iota(jnp.int32, (128, 128), 0)
    hot_map[...] = jnp.where(
        map_row == band * blocks + lax.rem(map_lane, blocks), 1.0, 0.0
    ).astype(BF16)
    for part in range(basis_lanes // 128):
        wide_map[:, part * 128 : (part + 1) * 128] = jnp.where(
            map_row == hot_lanes + BASIS_AT + part * (128 // blocks) + map_lane // blocks, 1.0, 0.0
        ).astype(BF16)
    for kind in range(5):
        at = basis_lanes + kind * 128
        wide_map[:, at : at + 128] = jnp.where(
            (map_row == hot_lanes + TERM_ROWS * kind + map_lane // blocks)
            & (map_lane < TERM_ROWS * blocks),
            1.0,
            0.0,
        ).astype(BF16)

    fetches[0].wait()
    fetches[1].wait()
    lane = lanes_of((1, 128))
    terms = view_terms([jnp.full((1, 128), camera_s[0, c], F32) for c in range(9)])
    row = jnp.zeros((1, 128), F32)
    for n in range(TERMS):
        row = jnp.where(lane == hot_lanes + n, terms[n], row)
    wanted = lax.broadcasted_iota(jnp.int32, (views_n, 128), 0) * hot_lanes + lanes_of(
        (views_n, 128)
    )
    hits = jnp.zeros((views_n, 128), F32)
    for n in range(list_len):
        hits = jnp.where(wanted == list_s[0, 0, n], 1.0, hits)
    message = jnp.where(lanes_of((views_n, 128)) < hot_lanes, hits, row)
    for v in range(views_n):
        msg_out[v] = message[v : v + 1]

    pl.semaphore_wait(barrier, views_n + bands_n - 2)
    for d in range(1, views_n):
        pltpu.make_async_remote_copy(
            src_ref=msg_out.at[peer_view[d]],
            dst_ref=msg_in.at[me],
            send_sem=send_sem.at[0],
            recv_sem=recv_sem.at[0],
            device_id=(peer_view[d], band),
            device_id_type=MESH,
        ).start()
    msg_in[me] = msg_out[view]
    fetches[2].wait()
    fetches[3].wait()
    fetches[4].wait()
    thalo_out[0] = target_ref[0, :, 0:REACH, :]
    thalo_out[1] = target_ref[0, :, rows - REACH : rows, :]
    edges_start(thalo_out, thalo_in, 0)

    owners, alive = [], []
    for k in range(TILE_MOST):
        for t in range(tiles):
            low, high = start_s[0, 0, t], end_s[0, 0, t]
            block = list_s[0, 0, jnp.clip(jnp.minimum(low + k, high - 1), 0, list_len - 1)]
            device = lax.div(jnp.clip(block, 0, devices * blocks - 1), blocks)
            owners.append(lax.rem(device, bands_n) * views_n + lax.div(device, bands_n))
            alive.append(jnp.where(low + k < high, 1.0, 0.0))
    put_lane = lax.rem(lanes_of((devices, 2 * pairs)), pairs)
    put_row = lax.broadcasted_iota(jnp.int32, (devices, 2 * pairs), 0)
    put = jnp.zeros((devices, 2 * pairs), F32)
    for n in range(pairs):
        put = jnp.where((put_lane == n) & (put_row == owners[n]), alive[n], put)
    put = put.astype(BF16)
    tile_sub = lax.broadcasted_iota(jnp.int32, (tiles, 128), 0)
    parts = []
    for k in range(TILE_MOST):
        part = jnp.zeros((tiles, 128), F32)
        for t in range(tiles):
            part = jnp.where(tile_sub == t, alive[k * tiles + t], part)
        parts.append(part)
    keep = jnp.concatenate(parts, axis=1) > 0.5

    plane = msg_in.at[pl.ds(0, views_n - 1)]
    pltpu.make_async_copy(plane, plane, recv_sem.at[0]).wait()
    pltpu.make_async_copy(plane, plane, send_sem.at[0]).wait()
    bundle = msg_in.at[pl.ds(band * views_n, views_n)]
    for d in range(1, bands_n):
        pltpu.make_async_remote_copy(
            src_ref=bundle,
            dst_ref=bundle,
            send_sem=send_sem.at[1],
            recv_sem=recv_sem.at[1],
            device_id=(view, peer_band[d]),
            device_id_type=MESH,
        ).start()

    fetches[5].wait()
    (sigma, opacity), pullback = jax.vjp(
        block_shape,
        [gauss_ref[6 + c] for c in range(3)],
        [gauss_ref[9 + c] for c in range(4)],
        gauss_ref[13],
    )
    rotation, scales = block_axes(
        [gauss_ref[6 + c] for c in range(3)], [gauss_ref[9 + c] for c in range(4)]
    )
    tabled = [gauss_ref[c] for c in range(6)] + [v for line in rotation for v in line] + scales
    for c, value in enumerate(tabled + [opacity]):
        both = stack3(value)
        for h in range(halves):
            geo_tab[h, c] = both[:, h * 128 : (h + 1) * 128]
    for ch in range(3):
        for q in range(BASIS):
            for n, piece in enumerate(split3(gauss_ref[14 + 3 * q + ch])):
                for h in range(halves):
                    tint_tab[
                        h, n, q * blocks : (q + 1) * blocks, ch * 128 : (ch + 1) * 128
                    ] = piece[:, h * 128 : (h + 1) * 128]

    lines = msg_in.at[pl.ds(0, devices - views_n)]
    pltpu.make_async_copy(lines, lines, recv_sem.at[1]).wait()
    pltpu.make_async_copy(lines, lines, send_sem.at[1]).wait()

    for p in range(devices):
        asked_ref[p : p + 1, :] = msg_in[p]
    asked = asked_ref[...]
    asked_parts = split3(asked)
    hot = mx(asked_parts[0], hot_map[...])
    hot_3 = hot[:, 0 : 3 * blocks].astype(BF16)

    def term(n):
        return asked[:, hot_lanes + n : hot_lanes + n + 1]

    ones = [term(c) for c in range(3)], [term(TERM_ROWS + c) for c in range(3)]
    shifts = [term(SHIFT_AT), term(SHIFT_AT + 1), term(SHIFT_AT + 2)]
    stacked = jnp.concatenate(asked_parts, axis=0)

    def widen(low, high):
        wide = mx(stacked, wide_map[:, low:high])
        return wide[0:devices] + wide[devices : 2 * devices] + wide[2 * devices :]

    hot_wide = jnp.concatenate([hot] * (basis_lanes // 128), axis=1)
    basis_parts = split3(widen(0, basis_lanes) * hot_wide)
    basis_three = jnp.concatenate(basis_parts, axis=0)

    def records_of(h):
        picked = [mx(hot_3, geo_tab[h, c]) for c in range(GEO_COMPS)]
        centre = [picked[c] + shifts[2] * picked[3 + c] for c in range(3)]
        turns, scales = [picked[6 + 3 * a : 9 + 3 * a] for a in range(3)], picked[15:18]

        def placed(row, shift):
            return row[0] * centre[0] + row[1] * centre[1] + row[2] * centre[2] + shift

        def turned(row, c):
            return (row[0] * turns[0][c] + row[1] * turns[1][c] + row[2] * turns[2][c]) * scales[c]

        m = [[turned(row, c) for c in range(3)] for row in ones]
        small = mx(basis_parts[0], tint_tab[h, 2])
        middle = mx(basis_three[0 : 2 * devices], tint_tab[h, 1])
        large = mx(basis_three, tint_tab[h, 0])
        colour = small + large[2 * devices :] + middle[devices:]
        colour = colour + (middle[0:devices] + large[devices : 2 * devices])
        colour = 0.5 + (colour + large[0:devices])
        return [
            placed(ones[0], shifts[0]),
            placed(ones[1], shifts[1]),
            m[0][0] * m[0][0] + m[0][1] * m[0][1] + m[0][2] * m[0][2] + 0.3,
            m[0][0] * m[1][0] + m[0][1] * m[1][1] + m[0][2] * m[1][2],
            m[1][0] * m[1][0] + m[1][1] * m[1][1] + m[1][2] * m[1][2] + 0.3,
            picked[18],
        ] + [colour[:, ch * 128 : (ch + 1) * 128] for ch in range(3)]

    for h in range(halves):
        flat_out = rec_out[h].reshape(devices * rec_out[h].shape[1], 128)
        for p, record in enumerate(records_of(h)):
            flat_out[pl.ds(p, devices, stride=rec_out[h].shape[1]), :] = record
        to_all(rec_out[h], rec_in[h], RECORDS, 2 + h)
        rec_in[h][me] = rec_out[h][me]

    tint_back[...] = jnp.concatenate([basis_parts[0], basis_parts[1], basis_parts[0]], axis=0)
    spans = [
        widen(basis_lanes + kind * 128, basis_lanes + (kind + 1) * 128) * hot for kind in range(5)
    ]
    hot_lane = lanes_of((devices, 128))
    hot_last = jnp.where(
        (hot_lane >= TERM_ROWS * blocks) & (hot_lane < (TERM_ROWS + 1) * blocks), hot, 0.0
    )
    for landing, group in ((line_back, spans[0:2] + [hot_last]), (shape_back, spans[2:5])):
        high, low = split2(jnp.concatenate(group, axis=0))
        landing[...] = jnp.concatenate([high, low, high], axis=0)

    for n in range(6, 12):
        fetches[n].wait()
    high, low = split2(second_ref[...])
    second_k[...] = jnp.concatenate([high, high, low], axis=1)
    high, low = split2(across_ref[...])
    across_k[...] = jnp.concatenate([high, high, low], axis=0)
    edges_wait(thalo_out, thalo_in, 0)
    in_rows, mid_rows = up8(rows + 2 * REACH), up8(rows + REACH)
    high_rows = 3 * mid_rows
    fill = jnp.zeros((in_rows - rows - 2 * REACH, cols), F32)

    def smooth(fields):
        down = jnp.dot(
            first_ref[...],
            jnp.concatenate(fields, axis=1),
            precision=HIGHEST_MODE,
            preferred_element_type=F32,
        )
        stack = jnp.concatenate(
            [down[:, f * cols : (f + 1) * cols] for f in range(len(fields))], axis=0
        )
        flat = jnp.dot(
            stack, across_ref[...], precision=HIGHEST_MODE, preferred_element_type=F32
        )
        return [flat[f * high_rows : (f + 1) * high_rows] for f in range(len(fields))]

    mine = target_ref[0]
    ext_y = jnp.concatenate(
        [v for ch in range(3) for v in (thalo_in[0, ch], mine[ch], thalo_in[1, ch], fill)], axis=0
    )
    mean_y, square_y = smooth([ext_y, ext_y * ext_y])

    tile_row = lax.broadcasted_iota(jnp.int32, (tiles, pair_len), 0).astype(F32)
    column = lax.rem(lanes_of((128, cols)), TILE).astype(F32) + (0.5 - 0.5 * TILE)

    def prepare(h):
        for k in range(TILE_MOST):
            for t in range(tiles):
                rec_pick[h, k, pl.ds(t, RECORDS, stride=tiles), :] = rec_in[h][
                    owners[k * tiles + t], 0:RECORDS, :
                ]

        def gathered(p):
            return jnp.concatenate(
                [rec_pick[h, k, p * tiles : (p + 1) * tiles, :] for k in range(TILE_MOST)], axis=1
            )

        u_rel = gathered(0) - (tile_row * TILE + 0.5 * TILE)
        w_rel = gathered(1) - ((band * rows).astype(F32) + 0.5 * TILE)
        c_a, c_b, c_c, opac = [gathered(p) for p in range(2, GEO_REC)]
        inv_det = 1.0 / (c_a * c_c - c_b * c_b)
        coef_a = -0.5 * c_c * inv_det
        coef_b = c_b * inv_det
        coef_c = -0.5 * c_a * inv_det

        def masked(value, other=0.0):
            return jnp.where(keep, value, other)

        quads = jnp.concatenate(
            [
                masked(LOG2_E * jnp.log(opac), NEVER),
                LOG2_E * coef_a,
                LOG2_E * coef_b,
                LOG2_E * coef_c,
                u_rel,
                w_rel,
            ],
            axis=0,
        )
        tones = jnp.concatenate(
            [masked(gathered(GEO_REC + ch)) for ch in range(3)], axis=0
        )
        grown = [
            mx(stack3(quads), quad_ref[...], TN),
            mx(stack3(tones), tone_ref[...], TN),
        ]
        for k in range(TILE_MOST):
            at = k * block_len + h * 128
            flat, part_a, part_b, part_c, u_wide, w_wide = [
                grown[0][k * 128 : (k + 1) * 128, n * cols : (n + 1) * cols] for n in range(6)
            ]
            e_x = column - u_wide
            coef[0, at : at + 128, :] = flat + part_a * e_x * e_x
            coef[1, at : at + 128, :] = part_b * e_x
            coef[2, at : at + 128, :] = part_c
            coef[6, at : at + 128, :] = w_wide
            for ch in range(3):
                coef[3 + ch, at : at + 128, :] = grown[1][
                    k * 128 : (k + 1) * 128, ch * cols : (ch + 1) * cols
                ]
        return u_rel, w_rel, c_a, c_b, c_c, opac, inv_det, coef_a, coef_b, coef_c

    wait_all(rec_in[0], RECORDS, 2)
    shapes = [prepare(0)]

    sub8 = lax.broadcasted_iota(jnp.int32, (8, cols), 0).astype(F32)
    parts_n = rows // 8
    row_local = [sub8 + (8.0 * part + 0.5 - 0.5 * TILE) for part in range(parts_n)]

    def spread_row(kind, j):
        return coef[kind, pl.ds(j, 8, stride=0), :]

    def blend(group, carry):
        trans, image = carry
        trans, image = list(trans), list(image)
        for k in range(8):
            j = group * 8 + k
            q0, q1, q2 = spread_row(0, j), spread_row(1, j), spread_row(2, j)
            low = spread_row(6, j)
            tint = [spread_row(3 + ch, j) for ch in range(3)]
            for part in range(parts_n):
                e_y = row_local[part] - low
                alpha = jnp.exp2(q0 + e_y * (q1 + e_y * q2))
                weight = alpha * trans[part]
                alpha_s[j, part] = alpha
                weight_s[j, part] = weight
                trans[part] = trans[part] * (1.0 - alpha)
                for ch in range(3):
                    at = ch * parts_n + part
                    image[at] = image[at] + weight * tint[ch]
        return tuple(trans), tuple(image)

    zero = jnp.zeros((8, cols), F32)
    state = (tuple([zero + 1.0] * parts_n), tuple([zero] * (3 * parts_n)))
    state = lax.fori_loop(0, 128 // 8, blend, state, unroll=UNROLL)
    for h in range(1, halves):
        wait_all(rec_in[h], RECORDS, 2 + h)
        shapes.append(prepare(h))
    _, image = lax.fori_loop(128 // 8, window // 8, blend, state, unroll=UNROLL)
    pred = [
        jnp.concatenate([image[ch * parts_n + part] for part in range(parts_n)], axis=0)
        for ch in range(3)
    ]
    for ch in range(3):
        halo_out[0, ch] = pred[ch][0:REACH]
        halo_out[1, ch] = pred[ch][rows - REACH : rows]
    edges_start(halo_out, halo_in, 1)
    edges_wait(halo_out, halo_in, 1)

    ext_x = jnp.concatenate(
        [v for ch in range(3) for v in (halo_in[0, ch], pred[ch], halo_in[1, ch], fill)], axis=0
    )
    mean_x, square_x, cross = smooth([ext_x, ext_x * ext_x, ext_x * ext_y])
    n_mean = 2.0 * mean_x * mean_y + STAB_MEAN
    n_var = 2.0 * (cross - mean_x * mean_y) + STAB_VAR
    d_mean = mean_x * mean_x + mean_y * mean_y + STAB_MEAN
    d_var = (square_x - mean_x * mean_x) + (square_y - mean_y * mean_y) + STAB_VAR
    inv_mean = 1.0 / d_mean
    inv_var = 1.0 / d_var
    inverse = inv_mean * inv_var
    ssim = n_mean * n_var * inverse
    ext_row = lax.broadcasted_iota(jnp.int32, (high_rows, cols), 0) % mid_rows
    image_row = ext_row + (band * rows - HALO)
    inside = (image_row >= 0) & (image_row < bands_n * rows) & (ext_row < rows + REACH)
    scale = -SSIM_WEIGHT / 3.0
    part_mean = 2.0 * mean_y * (n_var - n_mean) * inverse - 2.0 * mean_x * ssim * (
        inv_mean - inv_var
    )
    adjoint = jnp.concatenate(
        [
            jnp.where(inside, scale * part_mean, 0.0),
            jnp.where(inside, -scale * ssim * inv_var, 0.0),
            jnp.where(inside, (2.0 * scale) * n_mean * inverse, 0.0),
        ],
        axis=1,
    )
    high, low = split2(adjoint)
    down2 = mx(second_k[...], jnp.concatenate([high, low, high], axis=0))
    stacked2 = jnp.concatenate([down2[:, f * cols : (f + 1) * cols] for f in range(3)], axis=0)
    high, low = split2(stacked2)
    spread = mx(jnp.concatenate([high, low, high], axis=1), across_k[...])
    deep = 3 * rows
    pred_all = jnp.concatenate(pred, axis=0)
    mine_all = jnp.concatenate([mine[ch] for ch in range(3)], axis=0)
    error = pred_all - mine_all
    sign = jnp.where(error > 0.0, 1.0, jnp.where(error < 0.0, -1.0, 0.0))
    grad_pred = (
        ABS_WEIGHT / 3.0 * sign
        + spread[0:deep]
        + 2.0 * pred_all * spread[deep : 2 * deep]
        + mine_all * spread[2 * deep : 3 * deep]
    )
    own = (ext_row >= HALO) & (ext_row < HALO + rows)
    loss = jnp.sum(ABS_WEIGHT / 3.0 * jnp.abs(error), keepdims=True) + jnp.sum(
        jnp.where(own, SSIM_WEIGHT / 3.0 * (1.0 - ssim), 0.0), keepdims=True
    )

    pull = [
        [grad_pred[ch * rows + 8 * part : ch * rows + 8 * part + 8] for part in range(parts_n)]
        for ch in range(3)
    ]

    upper = lax.broadcasted_iota(jnp.int32, (8, cols), 0) < 4

    def keep_pair(held, kind, group, k, total):
        other = held.pop((kind, k // 2), None)
        if other is None:
            held[kind, k // 2] = total
            return
        a, b = (other, total) if k % 2 else (total, other)
        joined = jnp.where(upper, a, b) + pltpu.roll(jnp.where(upper, b, a), 4, 0)
        at = pl.multiple_of(group * 32 + k // 2 * 8, 8)
        moment_s[kind, pl.ds(at, 8), :] = joined

    def shades(group, carry):
        held = {}
        for k in range(8):
            j = group * 8 + k
            weight = [weight_s[j, part] for part in range(parts_n)]
            for ch in range(3):
                total = weight[0] * pull[ch][0]
                for part in range(1, parts_n):
                    total = total + weight[part] * pull[ch][part]
                keep_pair(held, ch, group, k, total)
        return carry

    def summed(kind, start, count):
        folded = moment_s.at[kind]
        quarter = [folded[pl.ds(start * 4 + sub, count, stride=4), :] for sub in range(4)]
        return (quarter[0] + quarter[1]) + (quarter[2] + quarter[3])

    lax.fori_loop(0, window // 8, shades, 0, unroll=UNROLL)

    def route(value, length):
        stack = jnp.concatenate(
            [value[:, k * length : (k + 1) * length] for k in range(TILE_MOST)], axis=0
        )
        return mx(put, stack2(stack))

    power = power_ref[...]
    power_low = power[0:tiles].astype(BF16)
    shade_flat = shade_out.reshape(devices * shade_out.shape[1], 128)
    for ch in range(3):
        high, low = split2(summed(ch, 0, window))
        routed = route(mx(power_low, high, NT) + mx(power_low, low, NT), block_len)
        for h in range(halves):
            shade_flat[pl.ds(ch * halves + h, devices, stride=shade_out.shape[1]), :] = routed[
                :, h * 128 : (h + 1) * 128
            ]
    shade_flat[pl.ds(tint_rows, devices, stride=shade_out.shape[1]), :] = jnp.broadcast_to(
        loss, (devices, 128)
    )
    to_all(shade_out, shade_in, tint_rows + 1, 2 + halves)
    shade_in[me] = shade_out[me]

    def unblend(step, behind):
        group = window // 8 - 1 - step
        behind = list(behind)
        held = {}
        for k in reversed(range(8)):
            j = group * 8 + k
            tint = [spread_row(3 + ch, j) for ch in range(3)]
            totals = [None] * 3
            for part in range(parts_n):
                alpha = alpha_s[j, part]
                shade = (
                    tint[0] * pull[0][part] + tint[1] * pull[1][part] + tint[2] * pull[2][part]
                )
                gap = shade - behind[part]
                behind[part] = behind[part] + alpha * gap
                lean = weight_s[j, part] * gap
                lean_r = lean * row_local[part]
                terms = [lean, lean_r, lean_r * row_local[part]]
                totals = [
                    value if total is None else total + value
                    for value, total in zip(terms, totals)
                ]
            for kind in range(3):
                keep_pair(held, kind, group, k, totals[kind])
        return tuple(behind)

    def derive(h):
        u_rel, w_rel, c_a, c_b, c_c, opac, inv_det, coef_a, coef_b, coef_c = shapes[h]
        moments = [
            jnp.concatenate(
                [summed(n, k * block_len + h * 128, 128) for k in range(TILE_MOST)],
                axis=0,
            )
            for n in range(3)
        ]
        by_x = exact_dot(power, moments[0], NT)
        m_00, m_10, m_20 = by_x[0:tiles], by_x[tiles : 2 * tiles], by_x[2 * tiles : 3 * tiles]
        by_xr = exact_dot(power[0 : 2 * tiles], moments[1], NT)
        m_01, m_11 = by_xr[0:tiles], by_xr[tiles : 2 * tiles]
        m_02 = exact_dot(power[0:tiles], moments[2], NT)
        s_x = m_10 - u_rel * m_00
        s_y = m_01 - w_rel * m_00
        s_xx = m_20 - 2.0 * u_rel * m_10 + u_rel * u_rel * m_00
        s_xy = m_11 - u_rel * m_01 - w_rel * m_10 + u_rel * w_rel * m_00
        s_yy = m_02 - 2.0 * w_rel * m_01 + w_rel * w_rel * m_00
        by_det = -(coef_a * s_xx + coef_b * s_xy + coef_c * s_yy) * inv_det
        derivs = [
            -(2.0 * coef_a * s_x + coef_b * s_y),
            -(2.0 * coef_c * s_y + coef_b * s_x),
            -0.5 * inv_det * s_yy + by_det * c_c,
            inv_det * s_xy - 2.0 * c_b * by_det,
            -0.5 * inv_det * s_xx + by_det * c_a,
            m_00 / opac,
        ]
        flat_out = grad_out[h].reshape(devices * grad_out[h].shape[1], 128)
        for p in range(GEO_REC):
            flat_out[pl.ds(p, devices, stride=grad_out[h].shape[1]), :] = route(derivs[p], 128)
        to_all(grad_out[h], grad_in[h], GEO_REC, 2 + halves + 1 + h)
        grad_in[h][me] = grad_out[h][me]

    groups = window // 8
    last = groups - 128 // 8
    behind = lax.fori_loop(0, last, unblend, tuple([zero] * parts_n), unroll=UNROLL)
    for h in range(halves - 1, 0, -1):
        derive(h)
    lax.fori_loop(last, groups, unblend, behind, unroll=UNROLL)
    derive(0)
    wait_all(shade_in, tint_rows + 1, 2 + halves)
    shade_back = shade_in.reshape(devices * shade_in.shape[1], 128)

    def arrived(landed, stride, p):
        return jnp.concatenate(
            [landed[pl.ds(p * halves + h, devices, stride=stride), :] for h in range(halves)],
            axis=1,
        )

    def spread_back(table, values):
        high, low = split2(jnp.concatenate(values, axis=0))
        return mx(table[...], jnp.concatenate([high, high, low], axis=0), TN)

    for ch in range(3):
        colour = spread_back(tint_back, [arrived(shade_back, shade_in.shape[1], ch)])
        for q in range(BASIS):
            grad_ref[14 + 3 * q + ch] = colour[q * blocks : (q + 1) * blocks]
    losses = shade_back[pl.ds(tint_rows, devices, stride=shade_in.shape[1]), :]
    loss_v[...] = jnp.sum(losses, axis=0, keepdims=True)[:, 0:1] * (
        1.0 / (devices * rows * cols)
    )
    loss_copy = pltpu.make_async_copy(loss_v, loss_ref, fetch_sem.at[len(sources)])
    loss_copy.start()
    fetches[12].wait()
    fetches[13].wait()

    def update(c, carry):
        adam_step(c, grad_ref, (gauss_ref, one_ref, two_ref), (gauss_ref, one_ref, two_ref))
        return carry

    lax.fori_loop(SHAPE_COMPS, gauss_ref.shape[0], update, 0, unroll=4)

    for h in range(halves - 1, -1, -1):
        wait_all(grad_in[h], GEO_REC, 2 + halves + 1 + h)
    grad_back = [
        grad_in[h].reshape(devices * grad_in[h].shape[1], 128) for h in range(halves)
    ]
    geos = [
        jnp.concatenate(
            [back[pl.ds(p, devices, stride=grad_in[0].shape[1]), :] for back in grad_back], axis=1
        )
        for p in range(GEO_REC)
    ]
    line = spread_back(line_back, [geos[0], geos[1], geos[5]])
    shape = spread_back(shape_back, geos[2:5])

    def comp(value, n):
        return value[n * blocks : (n + 1) * blocks]

    d_logs, d_quats, d_logit = pullback(
        ([comp(shape, n) for n in range(TERM_ROWS)], comp(line, TERM_ROWS))
    )
    columns = [comp(line, n) for n in range(TERM_ROWS)] + list(d_logs) + list(d_quats) + [d_logit]
    for c, value in enumerate(columns):
        grad_ref[c] = value
    loss_copy.wait()


def adam_kernel(
    grad_ref,
    gauss_ref,
    one_ref,
    two_ref,
    loss_in,
    out_gauss,
    out_one,
    out_two,
    out_grad,
    loss_out,
    gauss_v,
    one_v,
    two_v,
    write_sem,
):
    comps = gauss_ref.shape[0]
    held = [(grad_ref, out_grad), (gauss_ref, out_gauss), (one_ref, out_one), (two_ref, out_two)]
    fresh = [(gauss_v, out_gauss), (one_v, out_one), (two_v, out_two)]
    copies = [pltpu.make_async_copy(loss_in, loss_out, write_sem.at[4, 0])]
    copies[0].start()

    def send(group, low, high, slot):
        part = pl.ds(low, high - low)
        for n, (source, landing) in enumerate(group):
            copy = pltpu.make_async_copy(
                source.at[part], landing.at[part], write_sem.at[n, slot]
            )
            copy.start()
            copies.append(copy)

    for piece in range(PIECES):
        low = SHAPE_COMPS + piece * (comps - SHAPE_COMPS) // PIECES
        high = SHAPE_COMPS + (piece + 1) * (comps - SHAPE_COMPS) // PIECES
        send(held, low, high, piece)
    send(held[0:1], 0, SHAPE_COMPS, PIECES)
    for c in range(SHAPE_COMPS):
        adam_step(c, grad_ref, (gauss_ref, one_ref, two_ref), (gauss_v, one_v, two_v))
    send(fresh, 0, SHAPE_COMPS, PIECES + 1)
    for copy in copies:
        copy.wait()


def wide_table(tiles, cols, kinds):
    belongs = (np.arange(cols)[None, :] // TILE == np.arange(tiles)[:, None]).astype(np.float32)
    return np.tile(np.kron(np.eye(kinds, dtype=np.float32), belongs), (3, 1))


def per_device(
    gaussians,
    first_moment,
    second_moment,
    camera,
    target,
    block_list,
    block_count,
    tile_start,
    tile_end,
):
    views_n = lax.axis_size("view")
    bands_n = lax.axis_size("band")
    devices = views_n * bands_n
    blocks, comps, block_len = gaussians.shape
    list_len = block_list.shape[2]
    rows, cols = target.shape[2:]
    tiles = cols // TILE
    halves = block_len // 128
    geometry = (views_n, bands_n, blocks, list_len, rows, cols, block_len)

    across, first, second = smoothing_tables(rows, cols, 3)
    power = power_table(tiles, cols)
    quad = wide_table(tiles, cols, 6).astype(BF16)
    tone = wide_table(tiles, cols, 3).astype(BF16)
    vmem = pl.BlockSpec(memory_space=pltpu.VMEM)
    hbm = pl.BlockSpec(memory_space=pltpu.HBM)

    def by_comp(array):
        return jnp.transpose(array, (1, 0, 2))

    window = TILE_MOST * block_len
    tint_pad = up8(3 * halves + 1)
    basis_lanes = BASIS * blocks
    shape = jax.ShapeDtypeStruct((comps, blocks, block_len), F32)
    scalar = jax.ShapeDtypeStruct((1, 1), F32)
    kept = pltpu.VMEM(shape.shape, F32)
    gradient, params, one, two, mean_loss = pl.pallas_call(
        functools.partial(step_kernel, geometry),
        out_shape=(kept, kept, kept, kept, pltpu.HBM((1, 1), F32)),
        in_specs=[hbm] * 14,
        out_specs=(vmem,) * 4 + (hbm,),
        scratch_shapes=[
            pltpu.SMEM((1, 9), F32),
            pltpu.SMEM((1, 1, list_len), jnp.int32),
            pltpu.SMEM((1, 1, tiles), jnp.int32),
            pltpu.SMEM((1, 1, tiles), jnp.int32),
            pltpu.VMEM((1, 3, rows, cols), F32),
            pltpu.VMEM(across.shape, F32),
            pltpu.VMEM(first.shape, F32),
            pltpu.VMEM(second.shape, F32),
            pltpu.VMEM((second.shape[0], 3 * second.shape[1]), BF16),
            pltpu.VMEM((3 * cols, cols), BF16),
            pltpu.VMEM(power.shape, F32),
            pltpu.VMEM(quad.shape, BF16),
            pltpu.VMEM(tone.shape, BF16),
            pltpu.VMEM((views_n, 1, 128), F32),
            pltpu.VMEM((devices, 1, 128), F32),
            pltpu.VMEM((devices, 128), F32),
            pltpu.VMEM((1, 1), F32),
            pltpu.VMEM((128, 128), BF16),
            pltpu.VMEM((128, basis_lanes + 5 * 128), BF16),
            pltpu.VMEM((halves, GEO_COMPS, 3 * blocks, 128), BF16),
            pltpu.VMEM((halves, 3, basis_lanes, 3 * 128), BF16),
            pltpu.VMEM((3 * devices, basis_lanes), BF16),
            pltpu.VMEM((9 * devices, 128), BF16),
            pltpu.VMEM((9 * devices, 128), BF16),
            (pltpu.VMEM((devices, up8(RECORDS), 128), F32),) * halves,
            (pltpu.VMEM((devices, up8(RECORDS), 128), F32),) * halves,
            pltpu.VMEM((halves, TILE_MOST, RECORDS * tiles, 128), F32),
            pltpu.VMEM((devices, tint_pad, 128), F32),
            pltpu.VMEM((devices, tint_pad, 128), F32),
            (pltpu.VMEM((devices, up8(GEO_REC), 128), F32),) * halves,
            (pltpu.VMEM((devices, up8(GEO_REC), 128), F32),) * halves,
            pltpu.VMEM((2, 3, REACH, cols), F32),
            pltpu.VMEM((2, 3, REACH, cols), F32),
            pltpu.VMEM((2, 3, REACH, cols), F32),
            pltpu.VMEM((2, 3, REACH, cols), F32),
            pltpu.VMEM((7, window, cols), F32),
            pltpu.VMEM((window, rows // 8, 8, cols), F32),
            pltpu.VMEM((window, rows // 8, 8, cols), F32),
            pltpu.VMEM((3, window * 4, cols), F32),
            pltpu.SemaphoreType.DMA((3 + 2 * halves,)),
            pltpu.SemaphoreType.DMA((3 + 2 * halves,)),
            pltpu.SemaphoreType.DMA((2, 2)),
            pltpu.SemaphoreType.DMA((2, 2)),
            pltpu.SemaphoreType.DMA((15,)),
        ],
        compiler_params=pltpu.CompilerParams(
            collective_id=0, has_side_effects=True, vmem_limit_bytes=40 * 1024 * 1024
        ),
        name="render_step",
    )(
        *[
            pltpu.with_memory_space_constraint(array, pltpu.HBM)
            for array in (
                camera,
                block_list,
                tile_start,
                tile_end,
                target,
                by_comp(gaussians),
                by_comp(first_moment),
                by_comp(second_moment),
                across,
                first,
                second,
                power,
                quad,
                tone,
            )
        ]
    )

    new_params, new_one, new_two, out_gradient, out_loss = pl.pallas_call(
        adam_kernel,
        out_shape=(shape, shape, shape, shape, scalar),
        in_specs=[vmem] * 4 + [hbm],
        out_specs=(hbm, hbm, hbm, hbm, hbm),
        scratch_shapes=[pltpu.VMEM((SHAPE_COMPS, blocks, block_len), F32)] * 3
        + [pltpu.SemaphoreType.DMA((5, PIECES + 2))],
        compiler_params=pltpu.CompilerParams(vmem_limit_bytes=16 * 1024 * 1024),
        name="adam_step",
    )(gradient, params, one, two, pltpu.with_memory_space_constraint(mean_loss, pltpu.HBM))
    return (
        by_comp(new_params),
        by_comp(new_one),
        by_comp(new_two),
        out_loss.reshape(()),
        by_comp(out_gradient),
    )


def solution(mesh):
    return jax.shard_map(
        per_device,
        mesh=mesh,
        in_specs=(
            P(("view", "band"), None, None),
            P(("view", "band"), None, None),
            P(("view", "band"), None, None),
            P("view", None),
            P("view", None, "band", None),
            P("view", "band", None),
            P("view", "band"),
            P("view", "band", None),
            P("view", "band", None),
        ),
        out_specs=(
            P(("view", "band"), None, None),
            P(("view", "band"), None, None),
            P(("view", "band"), None, None),
            P(),
            P(("view", "band"), None, None),
        ),
        check_vma=False,
    )
```

```python
import functools
import math

import jax
import jax.numpy as jnp
import numpy as np
from jax import lax
from jax.experimental import pallas as pl
from jax.experimental.pallas import tpu as pltpu
from jax.sharding import PartitionSpec as P

TILE = 16
TILE_MOST = 2
HALO = 5
REACH = 2 * HALO
GEO_REC = 6
RECORDS = 9
PIECES = 3
SHAPE_COMPS = 14
UNROLL = 4

HIGHEST_MODE = lax.Precision.HIGHEST
SSIM_WEIGHT = 0.2
ABS_WEIGHT = 0.8
STAB_MEAN = 0.0001
STAB_VAR = 0.0009
BIAS_FIRST = 1.0 - math.exp(100.0 * math.log(0.9))
BIAS_SECOND = 1.0 - math.exp(100.0 * math.log(0.999))
LOG2_E = math.log2(math.e)
SH_ZERO = 0.28209479177387814
SH_ONE = 0.4886025119029199
SH_TWO = [
    1.0925484305920792,
    -1.0925484305920792,
    0.31539156525252005,
    -1.0925484305920792,
    0.5462742152960396,
]
SH_THREE = [
    -0.5900435899266435,
    2.890611442640554,
    -0.4570457994644658,
    0.3731763325901154,
    -0.4570457994644658,
    1.445305721320277,
    -0.5900435899266435,
]
F32 = jnp.float32
BF16 = jnp.bfloat16
MESH = pl.DeviceIdType.MESH
NEVER = -1e30


RATES = ((6, 0.016), (9, 0.005), (13, 0.001), (14, 0.05), (17, 0.0025), (62, 0.000125))


def learning_rate(component):
    rate = RATES[-1][1] / BIAS_FIRST
    if isinstance(component, int):
        return next(value for end, value in RATES if component < end) / BIAS_FIRST
    for end, value in reversed(RATES[:-1]):
        rate = jnp.where(component < end, value / BIAS_FIRST, rate)
    return rate


def kernel_taps():
    raw_taps = [math.exp(-(offset * offset) / 4.5) for offset in range(-5, 6)]
    tap_total = sum(raw_taps)
    return [raw_tap / tap_total for raw_tap in raw_taps]


def up8(value):
    return (value + 7) // 8 * 8


def smoothing_tables(rows, cols, channels):
    taps = kernel_taps()
    in_rows, mid_rows = up8(rows + 2 * REACH), up8(rows + REACH)
    across = np.zeros((cols, cols), np.float32)
    for out in range(cols):
        for m in range(-HALO, HALO + 1):
            if 0 <= out + m < cols:
                across[out + m, out] = taps[m + HALO]
    first = np.zeros((channels * mid_rows, channels * in_rows), np.float32)
    second = np.zeros((channels * rows, channels * mid_rows), np.float32)
    for c in range(channels):
        for e in range(rows + REACH):
            for m in range(REACH + 1):
                first[c * mid_rows + e, c * in_rows + e + m] = taps[m]
        for i in range(rows):
            for m in range(REACH + 1):
                second[c * rows + i, c * mid_rows + i + m] = taps[m]
    return across, first, second


def harmonics(dir_x, dir_y, dir_z):
    sq_x, sq_y, sq_z = (dir_x * dir_x, dir_y * dir_y, dir_z * dir_z)
    return [
        SH_ZERO + 0.0 * dir_x,
        -SH_ONE * dir_y,
        SH_ONE * dir_z,
        -SH_ONE * dir_x,
        SH_TWO[0] * dir_x * dir_y,
        SH_TWO[1] * dir_y * dir_z,
        SH_TWO[2] * (2.0 * sq_z - sq_x - sq_y),
        SH_TWO[3] * dir_x * dir_z,
        SH_TWO[4] * (sq_x - sq_y),
        SH_THREE[0] * dir_y * (3.0 * sq_x - sq_y),
        SH_THREE[1] * dir_x * dir_y * dir_z,
        SH_THREE[2] * dir_y * (4.0 * sq_z - sq_x - sq_y),
        SH_THREE[3] * dir_z * (2.0 * sq_z - 3.0 * sq_x - 3.0 * sq_y),
        SH_THREE[4] * dir_x * (4.0 * sq_z - sq_x - sq_y),
        SH_THREE[5] * dir_z * (sq_x - sq_y),
        SH_THREE[6] * dir_x * (sq_x - 3.0 * sq_y),
    ]


def camera_basis(affine):
    a, b = affine[0:3], affine[3:6]
    n_x = a[1] * b[2] - a[2] * b[1]
    n_y = a[2] * b[0] - a[0] * b[2]
    n_z = a[0] * b[1] - a[1] * b[0]
    length = jnp.sqrt(n_x * n_x + n_y * n_y + n_z * n_z)
    return harmonics(n_x / length, n_y / length, n_z / length)


def split3(value, axis=0):
    high = value.astype(BF16)
    rest = value - high.astype(F32)
    middle = rest.astype(BF16)
    low = (rest - middle.astype(F32)).astype(BF16)
    return high, middle, low


NN = ((1,), (0,))
NT = ((1,), (1,))
TN = ((0,), (0,))


def mx(a, b, dims=NN):
    return lax.dot_general(a, b, (dims, ((), ())), preferred_element_type=F32)


def split2(value):
    high = value.astype(BF16)
    return high, (value - high.astype(F32)).astype(BF16)


def exact_dot(table, value, dims):
    table = table.astype(BF16)
    total = None
    for part in split3(value):
        term = mx(table, part, dims)
        total = term if total is None else total + term
    return total


def stack3(value):
    return jnp.concatenate(split3(value), axis=0)


def stack2(value):
    return jnp.concatenate(split2(value), axis=0)


def adam_step(c, grad_ref, source, landing):
    gradient = grad_ref[c]
    new_one = 0.9 * source[1][c] + 0.1 * gradient
    new_two = 0.999 * source[2][c] + 0.001 * gradient * gradient
    landing[1][c] = new_one
    landing[2][c] = new_two
    bottom = jnp.sqrt(new_two * (1.0 / BIAS_SECOND)) + 1e-08
    landing[0][c] = source[0][c] - learning_rate(c) * new_one / bottom


def block_axes(logs, quats):
    scales = [jnp.exp(value) for value in logs]
    quat_len = jnp.sqrt(
        quats[0] * quats[0] + quats[1] * quats[1] + quats[2] * quats[2] + quats[3] * quats[3]
    )
    r, i, j, k = [value / quat_len for value in quats]
    rotation = [
        [1.0 - 2.0 * (j * j + k * k), 2.0 * (i * j - r * k), 2.0 * (i * k + r * j)],
        [2.0 * (i * j + r * k), 1.0 - 2.0 * (i * i + k * k), 2.0 * (j * k - r * i)],
        [2.0 * (i * k - r * j), 2.0 * (j * k + r * i), 1.0 - 2.0 * (i * i + j * j)],
    ]
    return rotation, scales


def block_shape(logs, quats, logit):
    rotation, scales = block_axes(logs, quats)
    axes = [[rotation[a][c] * scales[c] for c in range(3)] for a in range(3)]

    def moment(a, b):
        return axes[a][0] * axes[b][0] + axes[a][1] * axes[b][1] + axes[a][2] * axes[b][2]

    pairs = ((0, 0), (1, 1), (2, 2), (0, 1), (0, 2), (1, 2))
    return [moment(a, b) for a, b in pairs], 1.0 / (1.0 + jnp.exp(-logit))


def view_terms(cam):
    a, b, time = cam[0:3], cam[3:6], cam[8]
    terms = a + [time * value for value in a] + b + [time * value for value in b]
    crossed = ((0, 1), (0, 2), (1, 2))
    terms += [a[c] * a[c] for c in range(3)] + [2.0 * a[c] * a[d] for c, d in crossed]
    terms += [a[c] * b[c] for c in range(3)] + [a[c] * b[d] + a[d] * b[c] for c, d in crossed]
    terms += [b[c] * b[c] for c in range(3)] + [2.0 * b[c] * b[d] for c, d in crossed]
    return terms + [cam[6], cam[7], time] + camera_basis(cam[0:6])


TERM_ROWS = 6
SHIFT_AT = 30
BASIS_AT = 33
BASIS = 16
TERMS = 49
GEO_COMPS = 19


def step_kernel(
    geometry,
    camera_hbm,
    list_hbm,
    start_hbm,
    end_hbm,
    target_hbm,
    gauss_hbm,
    one_hbm,
    two_hbm,
    across_hbm,
    first_hbm,
    second_hbm,
    power_hbm,
    shade_hbm,
    quad_hbm,
    tone_hbm,
    grad_ref,
    gauss_ref,
    one_ref,
    two_ref,
    loss_ref,
    camera_s,
    list_s,
    start_s,
    end_s,
    target_ref,
    across_ref,
    first_ref,
    second_ref,
    second_k,
    across_k,
    power_ref,
    shade_ref,
    quad_ref,
    tone_ref,
    msg_out,
    msg_in,
    asked_ref,
    loss_v,
    hot_map,
    wide_map,
    geo_tab,
    tint_tab,
    tint_back,
    line_back,
    shape_back,
    rec_out,
    rec_in,
    rec_pick,
    shade_out,
    shade_in,
    grad_out,
    grad_in,
    halo_out,
    halo_in,
    thalo_out,
    thalo_in,
    coef,
    alpha_s,
    weight_s,
    moment_s,
    send_sem,
    recv_sem,
    halo_send,
    halo_recv,
    fetch_sem,
):
    views_n, bands_n, blocks, list_len, rows, cols, block_len = geometry
    devices = views_n * bands_n
    tiles = cols // TILE
    pairs = TILE_MOST * tiles
    window = TILE_MOST * block_len
    halves = block_len // 128
    pair_len = TILE_MOST * 128
    tint_rows = 3 * halves
    hot_lanes = bands_n * blocks
    basis_lanes = BASIS * blocks
    view = lax.axis_index("view")
    band = lax.axis_index("band")
    me = band * views_n + view
    has_up = band > 0
    has_down = band < bands_n - 1

    halo_in[...] = jnp.zeros_like(halo_in)
    thalo_in[...] = jnp.zeros_like(thalo_in)
    peer_view = [lax.rem(view + d, views_n) for d in range(views_n)]
    peer_band = [lax.rem(band + d, bands_n) for d in range(bands_n)]
    barrier = pltpu.get_barrier_semaphore()
    for d in range(1, views_n):
        pl.semaphore_signal(barrier, inc=1, device_id=(peer_view[d], band), device_id_type=MESH)
    for d in range(1, bands_n):
        pl.semaphore_signal(barrier, inc=1, device_id=(view, peer_band[d]), device_id_type=MESH)

    sources = (
        (camera_hbm, camera_s),
        (list_hbm, list_s),
        (start_hbm, start_s),
        (end_hbm, end_s),
        (target_hbm, target_ref),
        (gauss_hbm, gauss_ref),
        (quad_hbm, quad_ref),
        (tone_hbm, tone_ref),
        (power_hbm, power_ref),
        (shade_hbm, shade_ref),
        (across_hbm, across_ref),
        (first_hbm, first_ref),
        (second_hbm, second_ref),
        (one_hbm, one_ref),
        (two_hbm, two_ref),
    )
    fetches = [
        pltpu.make_async_copy(source, landing, fetch_sem.at[n])
        for n, (source, landing) in enumerate(sources)
    ]
    for fetch in fetches:
        fetch.start()

    def to_all(source, landing, length, phase):
        for d_view in range(views_n):
            for d_band in range(bands_n):
                if d_view + d_band == 0:
                    continue
                peer = peer_band[d_band] * views_n + peer_view[d_view]
                pltpu.make_async_remote_copy(
                    src_ref=source.at[peer, pl.ds(0, length)],
                    dst_ref=landing.at[me, pl.ds(0, length)],
                    send_sem=send_sem.at[phase],
                    recv_sem=recv_sem.at[phase],
                    device_id=(peer_view[d_view], peer_band[d_band]),
                    device_id_type=MESH,
                ).start()

    def wait_all(landing, length, phase):
        every = landing.at[pl.ds(0, devices - 1), pl.ds(0, length)]
        pltpu.make_async_copy(every, every, recv_sem.at[phase]).wait()
        pltpu.make_async_copy(every, every, send_sem.at[phase]).wait()

    def edge_copy(source, landing, direction, phase):
        step = -1 if direction == 0 else 1
        return pltpu.make_async_remote_copy(
            src_ref=source.at[direction],
            dst_ref=landing.at[1 - direction],
            send_sem=halo_send.at[phase, direction],
            recv_sem=halo_recv.at[phase, 1 - direction],
            device_id=(view, band + step),
            device_id_type=MESH,
        )

    def edges_start(source, landing, phase):
        @pl.when(has_up)
        def _():
            edge_copy(source, landing, 0, phase).start()

        @pl.when(has_down)
        def _():
            edge_copy(source, landing, 1, phase).start()

    def edges_wait(source, landing, phase):
        @pl.when(has_up)
        def _():
            up = edge_copy(source, landing, 0, phase)
            up.wait_send()
            pltpu.make_async_copy(
                landing.at[0], landing.at[0], halo_recv.at[phase, 0]
            ).wait()

        @pl.when(has_down)
        def _():
            down = edge_copy(source, landing, 1, phase)
            down.wait_send()
            pltpu.make_async_copy(
                landing.at[1], landing.at[1], halo_recv.at[phase, 1]
            ).wait()

    def lanes_of(shape):
        return lax.broadcasted_iota(jnp.int32, shape, len(shape) - 1)

    map_lane = lanes_of((128, 128))
    map_row = lax.broadcasted_iota(jnp.int32, (128, 128), 0)
    hot_map[...] = jnp.where(
        map_row == band * blocks + lax.rem(map_lane, blocks), 1.0, 0.0
    ).astype(BF16)
    for part in range(basis_lanes // 128):
        wide_map[:, part * 128 : (part + 1) * 128] = jnp.where(
            map_row == hot_lanes + BASIS_AT + part * (128 // blocks) + map_lane // blocks, 1.0, 0.0
        ).astype(BF16)
    for kind in range(5):
        at = basis_lanes + kind * 128
        wide_map[:, at : at + 128] = jnp.where(
            (map_row == hot_lanes + TERM_ROWS * kind + map_lane // blocks)
            & (map_lane < TERM_ROWS * blocks),
            1.0,
            0.0,
        ).astype(BF16)

    fetches[0].wait()
    fetches[1].wait()
    lane = lanes_of((1, 128))
    terms = view_terms([jnp.full((1, 128), camera_s[0, c], F32) for c in range(9)])
    row = jnp.zeros((1, 128), F32)
    for n in range(TERMS):
        row = jnp.where(lane == hot_lanes + n, terms[n], row)
    wanted = lax.broadcasted_iota(jnp.int32, (views_n, 128), 0) * hot_lanes + lanes_of(
        (views_n, 128)
    )
    hits = jnp.zeros((views_n, 128), F32)
    for n in range(list_len):
        hits = jnp.where(wanted == list_s[0, 0, n], 1.0, hits)
    message = jnp.where(lanes_of((views_n, 128)) < hot_lanes, hits, row)
    for v in range(views_n):
        msg_out[v] = message[v : v + 1]

    pl.semaphore_wait(barrier, views_n + bands_n - 2)
    for d in range(1, views_n):
        pltpu.make_async_remote_copy(
            src_ref=msg_out.at[peer_view[d]],
            dst_ref=msg_in.at[me],
            send_sem=send_sem.at[0],
            recv_sem=recv_sem.at[0],
            device_id=(peer_view[d], band),
            device_id_type=MESH,
        ).start()
    msg_in[me] = msg_out[view]
    fetches[2].wait()
    fetches[3].wait()
    fetches[4].wait()
    thalo_out[0] = target_ref[0, :, 0:REACH, :]
    thalo_out[1] = target_ref[0, :, rows - REACH : rows, :]
    edges_start(thalo_out, thalo_in, 0)

    owners, alive = [], []
    for k in range(TILE_MOST):
        for t in range(tiles):
            low, high = start_s[0, 0, t], end_s[0, 0, t]
            block = list_s[0, 0, jnp.clip(jnp.minimum(low + k, high - 1), 0, list_len - 1)]
            device = lax.div(jnp.clip(block, 0, devices * blocks - 1), blocks)
            owners.append(lax.rem(device, bands_n) * views_n + lax.div(device, bands_n))
            alive.append(jnp.where(low + k < high, 1.0, 0.0))
    put_lane = lax.rem(lanes_of((devices, 2 * pairs)), pairs)
    put_row = lax.broadcasted_iota(jnp.int32, (devices, 2 * pairs), 0)
    put = jnp.zeros((devices, 2 * pairs), F32)
    for n in range(pairs):
        put = jnp.where((put_lane == n) & (put_row == owners[n]), alive[n], put)
    put = put.astype(BF16)
    tile_sub = lax.broadcasted_iota(jnp.int32, (tiles, 128), 0)
    parts = []
    for k in range(TILE_MOST):
        part = jnp.zeros((tiles, 128), F32)
        for t in range(tiles):
            part = jnp.where(tile_sub == t, alive[k * tiles + t], part)
        parts.append(part)
    keep = jnp.concatenate(parts, axis=1) > 0.5

    plane = msg_in.at[pl.ds(0, views_n - 1)]
    pltpu.make_async_copy(plane, plane, recv_sem.at[0]).wait()
    pltpu.make_async_copy(plane, plane, send_sem.at[0]).wait()
    bundle = msg_in.at[pl.ds(band * views_n, views_n)]
    for d in range(1, bands_n):
        pltpu.make_async_remote_copy(
            src_ref=bundle,
            dst_ref=bundle,
            send_sem=send_sem.at[1],
            recv_sem=recv_sem.at[1],
            device_id=(view, peer_band[d]),
            device_id_type=MESH,
        ).start()

    fetches[5].wait()
    (sigma, opacity), pullback = jax.vjp(
        block_shape,
        [gauss_ref[6 + c] for c in range(3)],
        [gauss_ref[9 + c] for c in range(4)],
        gauss_ref[13],
    )
    rotation, scales = block_axes(
        [gauss_ref[6 + c] for c in range(3)], [gauss_ref[9 + c] for c in range(4)]
    )
    tabled = [gauss_ref[c] for c in range(6)] + [v for line in rotation for v in line] + scales
    for c, value in enumerate(tabled + [opacity]):
        both = stack3(value)
        for h in range(halves):
            geo_tab[h, c] = both[:, h * 128 : (h + 1) * 128]
    for ch in range(3):
        for q in range(BASIS):
            for n, piece in enumerate(split3(gauss_ref[14 + 3 * q + ch])):
                for h in range(halves):
                    tint_tab[
                        h, n, q * blocks : (q + 1) * blocks, ch * 128 : (ch + 1) * 128
                    ] = piece[:, h * 128 : (h + 1) * 128]

    lines = msg_in.at[pl.ds(0, devices - views_n)]
    pltpu.make_async_copy(lines, lines, recv_sem.at[1]).wait()
    pltpu.make_async_copy(lines, lines, send_sem.at[1]).wait()

    for p in range(devices):
        asked_ref[p : p + 1, :] = msg_in[p]
    asked = asked_ref[...]
    asked_parts = split3(asked)
    hot = mx(asked_parts[0], hot_map[...])
    hot_3 = hot[:, 0 : 3 * blocks].astype(BF16)

    def term(n):
        return asked[:, hot_lanes + n : hot_lanes + n + 1]

    ones = [term(c) for c in range(3)], [term(TERM_ROWS + c) for c in range(3)]
    shifts = [term(SHIFT_AT), term(SHIFT_AT + 1), term(SHIFT_AT + 2)]
    stacked = jnp.concatenate(asked_parts, axis=0)

    def widen(low, high):
        wide = mx(stacked, wide_map[:, low:high])
        return wide[0:devices] + wide[devices : 2 * devices] + wide[2 * devices :]

    hot_wide = jnp.concatenate([hot] * (basis_lanes // 128), axis=1)
    basis_parts = split3(widen(0, basis_lanes) * hot_wide)
    basis_three = jnp.concatenate(basis_parts, axis=0)

    def records_of(h):
        picked = [mx(hot_3, geo_tab[h, c]) for c in range(GEO_COMPS)]
        centre = [picked[c] + shifts[2] * picked[3 + c] for c in range(3)]
        turns, scales = [picked[6 + 3 * a : 9 + 3 * a] for a in range(3)], picked[15:18]

        def placed(row, shift):
            return row[0] * centre[0] + row[1] * centre[1] + row[2] * centre[2] + shift

        def turned(row, c):
            return (row[0] * turns[0][c] + row[1] * turns[1][c] + row[2] * turns[2][c]) * scales[c]

        m = [[turned(row, c) for c in range(3)] for row in ones]
        small = mx(basis_parts[0], tint_tab[h, 2])
        middle = mx(basis_three[0 : 2 * devices], tint_tab[h, 1])
        large = mx(basis_three, tint_tab[h, 0])
        colour = small + large[2 * devices :] + middle[devices:]
        colour = colour + (middle[0:devices] + large[devices : 2 * devices])
        colour = 0.5 + (colour + large[0:devices])
        return [
            placed(ones[0], shifts[0]),
            placed(ones[1], shifts[1]),
            m[0][0] * m[0][0] + m[0][1] * m[0][1] + m[0][2] * m[0][2] + 0.3,
            m[0][0] * m[1][0] + m[0][1] * m[1][1] + m[0][2] * m[1][2],
            m[1][0] * m[1][0] + m[1][1] * m[1][1] + m[1][2] * m[1][2] + 0.3,
            picked[18],
        ] + [colour[:, ch * 128 : (ch + 1) * 128] for ch in range(3)]

    for h in range(halves):
        flat_out = rec_out[h].reshape(devices * rec_out[h].shape[1], 128)
        for p, record in enumerate(records_of(h)):
            flat_out[pl.ds(p, devices, stride=rec_out[h].shape[1]), :] = record
        to_all(rec_out[h], rec_in[h], RECORDS, 2 + h)
        rec_in[h][me] = rec_out[h][me]

    tint_back[...] = jnp.concatenate([basis_parts[0], basis_parts[1], basis_parts[0]], axis=0)
    spans = [
        widen(basis_lanes + kind * 128, basis_lanes + (kind + 1) * 128) * hot for kind in range(5)
    ]
    hot_lane = lanes_of((devices, 128))
    hot_last = jnp.where(
        (hot_lane >= TERM_ROWS * blocks) & (hot_lane < (TERM_ROWS + 1) * blocks), hot, 0.0
    )
    for landing, group in ((line_back, spans[0:2] + [hot_last]), (shape_back, spans[2:5])):
        high, low = split2(jnp.concatenate(group, axis=0))
        landing[...] = jnp.concatenate([high, low, high], axis=0)

    for n in range(6, 13):
        fetches[n].wait()
    high, low = split2(second_ref[...])
    second_k[...] = jnp.concatenate([high, high, low], axis=1)
    high, low = split2(across_ref[...])
    across_k[...] = jnp.concatenate([high, high, low], axis=0)
    edges_wait(thalo_out, thalo_in, 0)
    in_rows, mid_rows = up8(rows + 2 * REACH), up8(rows + REACH)
    high_rows = 3 * mid_rows
    fill = jnp.zeros((in_rows - rows - 2 * REACH, cols), F32)

    def smooth(fields):
        down = jnp.dot(
            first_ref[...],
            jnp.concatenate(fields, axis=1),
            precision=HIGHEST_MODE,
            preferred_element_type=F32,
        )
        stack = jnp.concatenate(
            [down[:, f * cols : (f + 1) * cols] for f in range(len(fields))], axis=0
        )
        flat = jnp.dot(
            stack, across_ref[...], precision=HIGHEST_MODE, preferred_element_type=F32
        )
        return [flat[f * high_rows : (f + 1) * high_rows] for f in range(len(fields))]

    mine = target_ref[0]
    ext_y = jnp.concatenate(
        [v for ch in range(3) for v in (thalo_in[0, ch], mine[ch], thalo_in[1, ch], fill)], axis=0
    )
    mean_y, square_y = smooth([ext_y, ext_y * ext_y])

    tile_row = lax.broadcasted_iota(jnp.int32, (tiles, pair_len), 0).astype(F32)
    column = lax.rem(lanes_of((128, cols)), TILE).astype(F32) + (0.5 - 0.5 * TILE)

    def prepare(h):
        for k in range(TILE_MOST):
            for t in range(tiles):
                rec_pick[h, k, pl.ds(t, RECORDS, stride=tiles), :] = rec_in[h][
                    owners[k * tiles + t], 0:RECORDS, :
                ]

        def gathered(p):
            return jnp.concatenate(
                [rec_pick[h, k, p * tiles : (p + 1) * tiles, :] for k in range(TILE_MOST)], axis=1
            )

        u_rel = gathered(0) - (tile_row * TILE + 0.5 * TILE)
        w_rel = gathered(1) - ((band * rows).astype(F32) + 0.5 * TILE)
        c_a, c_b, c_c, opac = [gathered(p) for p in range(2, GEO_REC)]
        inv_det = 1.0 / (c_a * c_c - c_b * c_b)
        coef_a = -0.5 * c_c * inv_det
        coef_b = c_b * inv_det
        coef_c = -0.5 * c_a * inv_det

        def masked(value, other=0.0):
            return jnp.where(keep, value, other)

        quads = jnp.concatenate(
            [
                masked(LOG2_E * jnp.log(opac), NEVER),
                LOG2_E * coef_a,
                LOG2_E * coef_b,
                LOG2_E * coef_c,
                u_rel,
                w_rel,
            ],
            axis=0,
        )
        tones = jnp.concatenate(
            [masked(gathered(GEO_REC + ch)) for ch in range(3)], axis=0
        )
        grown = [
            mx(stack3(quads), quad_ref[...], TN),
            mx(stack3(tones), tone_ref[...], TN),
        ]
        for k in range(TILE_MOST):
            at = k * block_len + h * 128
            flat, part_a, part_b, part_c, u_wide, w_wide = [
                grown[0][k * 128 : (k + 1) * 128, n * cols : (n + 1) * cols] for n in range(6)
            ]
            e_x = column - u_wide
            coef[0, at : at + 128, :] = flat + part_a * e_x * e_x
            coef[1, at : at + 128, :] = part_b * e_x
            coef[2, at : at + 128, :] = part_c
            coef[6, at : at + 128, :] = w_wide
            for ch in range(3):
                coef[3 + ch, at : at + 128, :] = grown[1][
                    k * 128 : (k + 1) * 128, ch * cols : (ch + 1) * cols
                ]
        return u_rel, w_rel, c_a, c_b, c_c, opac, inv_det, coef_a, coef_b, coef_c

    wait_all(rec_in[0], RECORDS, 2)
    shapes = [prepare(0)]

    sub8 = lax.broadcasted_iota(jnp.int32, (8, cols), 0).astype(F32)
    parts_n = rows // 8
    row_local = [sub8 + (8.0 * part + 0.5 - 0.5 * TILE) for part in range(parts_n)]

    def spread_row(kind, j):
        return coef[kind, pl.ds(j, 8, stride=0), :]

    def blend(group, carry):
        trans, image = carry
        trans, image = list(trans), list(image)
        for k in range(8):
            j = group * 8 + k
            q0, q1, q2 = spread_row(0, j), spread_row(1, j), spread_row(2, j)
            low = spread_row(6, j)
            tint = [spread_row(3 + ch, j) for ch in range(3)]
            for part in range(parts_n):
                e_y = row_local[part] - low
                alpha = jnp.exp2(q0 + e_y * (q1 + e_y * q2))
                weight = alpha * trans[part]
                alpha_s[j, part] = alpha
                weight_s[j, part] = weight
                trans[part] = trans[part] * (1.0 - alpha)
                for ch in range(3):
                    at = ch * parts_n + part
                    image[at] = image[at] + weight * tint[ch]
        return tuple(trans), tuple(image)

    zero = jnp.zeros((8, cols), F32)
    state = (tuple([zero + 1.0] * parts_n), tuple([zero] * (3 * parts_n)))
    state = lax.fori_loop(0, 128 // 8, blend, state, unroll=UNROLL)
    for h in range(1, halves):
        wait_all(rec_in[h], RECORDS, 2 + h)
        shapes.append(prepare(h))
    _, image = lax.fori_loop(128 // 8, window // 8, blend, state, unroll=UNROLL)
    pred = [
        jnp.concatenate([image[ch * parts_n + part] for part in range(parts_n)], axis=0)
        for ch in range(3)
    ]
    for ch in range(3):
        halo_out[0, ch] = pred[ch][0:REACH]
        halo_out[1, ch] = pred[ch][rows - REACH : rows]
    edges_start(halo_out, halo_in, 1)
    edges_wait(halo_out, halo_in, 1)

    ext_x = jnp.concatenate(
        [v for ch in range(3) for v in (halo_in[0, ch], pred[ch], halo_in[1, ch], fill)], axis=0
    )
    mean_x, square_x, cross = smooth([ext_x, ext_x * ext_x, ext_x * ext_y])
    n_mean = 2.0 * mean_x * mean_y + STAB_MEAN
    n_var = 2.0 * (cross - mean_x * mean_y) + STAB_VAR
    d_mean = mean_x * mean_x + mean_y * mean_y + STAB_MEAN
    d_var = (square_x - mean_x * mean_x) + (square_y - mean_y * mean_y) + STAB_VAR
    inv_mean = 1.0 / d_mean
    inv_var = 1.0 / d_var
    inverse = inv_mean * inv_var
    ssim = n_mean * n_var * inverse
    ext_row = lax.broadcasted_iota(jnp.int32, (high_rows, cols), 0) % mid_rows
    image_row = ext_row + (band * rows - HALO)
    inside = (image_row >= 0) & (image_row < bands_n * rows) & (ext_row < rows + REACH)
    scale = -SSIM_WEIGHT / 3.0
    part_mean = 2.0 * mean_y * (n_var - n_mean) * inverse - 2.0 * mean_x * ssim * (
        inv_mean - inv_var
    )
    adjoint = jnp.concatenate(
        [
            jnp.where(inside, scale * part_mean, 0.0),
            jnp.where(inside, -scale * ssim * inv_var, 0.0),
            jnp.where(inside, (2.0 * scale) * n_mean * inverse, 0.0),
        ],
        axis=1,
    )
    high, low = split2(adjoint)
    down2 = mx(second_k[...], jnp.concatenate([high, low, high], axis=0))
    stacked2 = jnp.concatenate([down2[:, f * cols : (f + 1) * cols] for f in range(3)], axis=0)
    high, low = split2(stacked2)
    spread = mx(jnp.concatenate([high, low, high], axis=1), across_k[...])
    deep = 3 * rows
    pred_all = jnp.concatenate(pred, axis=0)
    mine_all = jnp.concatenate([mine[ch] for ch in range(3)], axis=0)
    error = pred_all - mine_all
    sign = jnp.where(error > 0.0, 1.0, jnp.where(error < 0.0, -1.0, 0.0))
    grad_pred = (
        ABS_WEIGHT / 3.0 * sign
        + spread[0:deep]
        + 2.0 * pred_all * spread[deep : 2 * deep]
        + mine_all * spread[2 * deep : 3 * deep]
    )
    own = (ext_row >= HALO) & (ext_row < HALO + rows)
    loss = jnp.sum(ABS_WEIGHT / 3.0 * jnp.abs(error), keepdims=True) + jnp.sum(
        jnp.where(own, SSIM_WEIGHT / 3.0 * (1.0 - ssim), 0.0), keepdims=True
    )

    pull = [
        [grad_pred[ch * rows + 8 * part : ch * rows + 8 * part + 8] for part in range(parts_n)]
        for ch in range(3)
    ]

    upper = lax.broadcasted_iota(jnp.int32, (8, cols), 0) < 4

    def keep_pair(held, kind, group, k, total):
        other = held.pop((kind, k // 2), None)
        if other is None:
            held[kind, k // 2] = total
            return
        a, b = (other, total) if k % 2 else (total, other)
        joined = jnp.where(upper, a, b) + pltpu.roll(jnp.where(upper, b, a), 4, 0)
        at = pl.multiple_of(group * 32 + k // 2 * 8, 8)
        moment_s[kind, pl.ds(at, 8), :] = joined

    def shades(group, carry):
        held = {}
        for k in range(8):
            j = group * 8 + k
            weight = [weight_s[j, part] for part in range(parts_n)]
            for ch in range(3):
                total = weight[0] * pull[ch][0]
                for part in range(1, parts_n):
                    total = total + weight[part] * pull[ch][part]
                keep_pair(held, ch, group, k, total)
        return carry

    def summed(kind, start, count):
        folded = moment_s.at[kind]
        quarter = [folded[pl.ds(start * 4 + sub, count, stride=4), :] for sub in range(4)]
        return (quarter[0] + quarter[1]) + (quarter[2] + quarter[3])

    lax.fori_loop(0, window // 8, shades, 0, unroll=UNROLL)

    def route(value, length):
        stack = jnp.concatenate(
            [value[:, k * length : (k + 1) * length] for k in range(TILE_MOST)], axis=0
        )
        return mx(put, stack2(stack))

    shade_flat = shade_out.reshape(devices * shade_out.shape[1], 128)
    folded = [piece for ch in range(3) for piece in split2(summed(ch, 0, window))]
    by_tile = jnp.transpose(mx(jnp.concatenate(folded, axis=1), shade_ref[...]))
    for ch in range(3):
        routed = route(by_tile[ch * tiles : (ch + 1) * tiles], block_len)
        for h in range(halves):
            shade_flat[pl.ds(ch * halves + h, devices, stride=shade_out.shape[1]), :] = routed[
                :, h * 128 : (h + 1) * 128
            ]
    shade_flat[pl.ds(tint_rows, devices, stride=shade_out.shape[1]), :] = jnp.broadcast_to(
        loss, (devices, 128)
    )
    to_all(shade_out, shade_in, tint_rows + 1, 2 + halves)
    shade_in[me] = shade_out[me]

    def unblend(step, behind):
        group = window // 8 - 1 - step
        behind = list(behind)
        held = {}
        for k in reversed(range(8)):
            j = group * 8 + k
            tint = [spread_row(3 + ch, j) for ch in range(3)]
            totals = [None] * 3
            for part in range(parts_n):
                alpha = alpha_s[j, part]
                shade = (
                    tint[0] * pull[0][part] + tint[1] * pull[1][part] + tint[2] * pull[2][part]
                )
                gap = shade - behind[part]
                behind[part] = behind[part] + alpha * gap
                lean = weight_s[j, part] * gap
                lean_r = lean * row_local[part]
                terms = [lean, lean_r, lean_r * row_local[part]]
                totals = [
                    value if total is None else total + value
                    for value, total in zip(terms, totals)
                ]
            for kind in range(3):
                keep_pair(held, kind, group, k, totals[kind])
        return tuple(behind)

    def derive(h):
        u_rel, w_rel, c_a, c_b, c_c, opac, inv_det, coef_a, coef_b, coef_c = shapes[h]
        moments = [
            jnp.concatenate(
                [summed(n, k * block_len + h * 128, 128) for k in range(TILE_MOST)],
                axis=0,
            )
            for n in range(3)
        ]
        power = power_ref[...]
        by_x = exact_dot(power, moments[0], NT)
        m_00, m_10, m_20 = by_x[0:tiles], by_x[tiles : 2 * tiles], by_x[2 * tiles : 3 * tiles]
        by_xr = exact_dot(power[0 : 2 * tiles], moments[1], NT)
        m_01, m_11 = by_xr[0:tiles], by_xr[tiles : 2 * tiles]
        m_02 = exact_dot(power[0:tiles], moments[2], NT)
        s_x = m_10 - u_rel * m_00
        s_y = m_01 - w_rel * m_00
        s_xx = m_20 - 2.0 * u_rel * m_10 + u_rel * u_rel * m_00
        s_xy = m_11 - u_rel * m_01 - w_rel * m_10 + u_rel * w_rel * m_00
        s_yy = m_02 - 2.0 * w_rel * m_01 + w_rel * w_rel * m_00
        by_det = -(coef_a * s_xx + coef_b * s_xy + coef_c * s_yy) * inv_det
        derivs = [
            -(2.0 * coef_a * s_x + coef_b * s_y),
            -(2.0 * coef_c * s_y + coef_b * s_x),
            -0.5 * inv_det * s_yy + by_det * c_c,
            inv_det * s_xy - 2.0 * c_b * by_det,
            -0.5 * inv_det * s_xx + by_det * c_a,
            m_00 / opac,
        ]
        flat_out = grad_out[h].reshape(devices * grad_out[h].shape[1], 128)
        for p in range(GEO_REC):
            flat_out[pl.ds(p, devices, stride=grad_out[h].shape[1]), :] = route(derivs[p], 128)
        to_all(grad_out[h], grad_in[h], GEO_REC, 2 + halves + 1 + h)
        grad_in[h][me] = grad_out[h][me]

    groups = window // 8
    last = groups - 128 // 8
    behind = lax.fori_loop(0, last, unblend, tuple([zero] * parts_n), unroll=UNROLL)
    for h in range(halves - 1, 0, -1):
        derive(h)
    lax.fori_loop(last, groups, unblend, behind, unroll=UNROLL)
    derive(0)
    wait_all(shade_in, tint_rows + 1, 2 + halves)
    shade_back = shade_in.reshape(devices * shade_in.shape[1], 128)

    def arrived(landed, stride, p):
        return jnp.concatenate(
            [landed[pl.ds(p * halves + h, devices, stride=stride), :] for h in range(halves)],
            axis=1,
        )

    def spread_back(table, values):
        high, low = split2(jnp.concatenate(values, axis=0))
        return mx(table[...], jnp.concatenate([high, high, low], axis=0), TN)

    for ch in range(3):
        colour = spread_back(tint_back, [arrived(shade_back, shade_in.shape[1], ch)])
        for q in range(BASIS):
            grad_ref[14 + 3 * q + ch] = colour[q * blocks : (q + 1) * blocks]
    losses = shade_back[pl.ds(tint_rows, devices, stride=shade_in.shape[1]), :]
    loss_v[...] = jnp.sum(losses, axis=0, keepdims=True)[:, 0:1] * (
        1.0 / (devices * rows * cols)
    )
    loss_copy = pltpu.make_async_copy(loss_v, loss_ref, fetch_sem.at[len(sources)])
    loss_copy.start()
    fetches[13].wait()
    fetches[14].wait()

    def update(c, carry):
        adam_step(c, grad_ref, (gauss_ref, one_ref, two_ref), (gauss_ref, one_ref, two_ref))
        return carry

    lax.fori_loop(SHAPE_COMPS, gauss_ref.shape[0], update, 0, unroll=4)

    for h in range(halves - 1, -1, -1):
        wait_all(grad_in[h], GEO_REC, 2 + halves + 1 + h)
    grad_back = [
        grad_in[h].reshape(devices * grad_in[h].shape[1], 128) for h in range(halves)
    ]
    geos = [
        jnp.concatenate(
            [back[pl.ds(p, devices, stride=grad_in[0].shape[1]), :] for back in grad_back], axis=1
        )
        for p in range(GEO_REC)
    ]
    line = spread_back(line_back, [geos[0], geos[1], geos[5]])
    shape = spread_back(shape_back, geos[2:5])

    def comp(value, n):
        return value[n * blocks : (n + 1) * blocks]

    d_logs, d_quats, d_logit = pullback(
        ([comp(shape, n) for n in range(TERM_ROWS)], comp(line, TERM_ROWS))
    )
    columns = [comp(line, n) for n in range(TERM_ROWS)] + list(d_logs) + list(d_quats) + [d_logit]
    for c, value in enumerate(columns):
        grad_ref[c] = value
    loss_copy.wait()


def adam_kernel(
    grad_ref,
    gauss_ref,
    one_ref,
    two_ref,
    loss_in,
    out_gauss,
    out_one,
    out_two,
    out_grad,
    loss_out,
    gauss_v,
    one_v,
    two_v,
    write_sem,
):
    comps = gauss_ref.shape[0]
    held = [(grad_ref, out_grad), (gauss_ref, out_gauss), (one_ref, out_one), (two_ref, out_two)]
    fresh = [(gauss_v, out_gauss), (one_v, out_one), (two_v, out_two)]
    total = pltpu.make_async_copy(loss_in, loss_out, write_sem.at[4])
    total.start()

    def send(group, low, high, first):
        part = pl.ds(low, high - low)
        for n, (source, landing) in enumerate(group, first):
            copy = pltpu.make_async_copy(
                source.at[part], landing.at[part], write_sem.at[n]
            )
            copy.start()

    for piece in range(PIECES):
        low = SHAPE_COMPS + piece * (comps - SHAPE_COMPS) // PIECES
        high = SHAPE_COMPS + (piece + 1) * (comps - SHAPE_COMPS) // PIECES
        send(held, low, high, 0)
    send(held[0:1], 0, SHAPE_COMPS, 0)
    for c in range(SHAPE_COMPS):
        adam_step(c, grad_ref, (gauss_ref, one_ref, two_ref), (gauss_v, one_v, two_v))
    send(fresh, 0, SHAPE_COMPS, 1)
    total.wait()
    for n, (source, landing) in enumerate(held):
        pltpu.make_async_copy(source, landing, write_sem.at[n]).wait()


def power_table(tiles, cols):
    lane = np.arange(cols)
    local = lane % TILE + 0.5 - TILE / 2
    belongs = (lane[None, :] // TILE == np.arange(tiles)[:, None]).astype(np.float32)
    return np.concatenate([belongs, belongs * local, belongs * local * local]).astype(np.float32)


def shade_table(tiles, cols):
    belongs = (np.arange(cols)[:, None] // TILE == np.arange(tiles)[None, :]).astype(np.float32)
    table = np.zeros((3, 2, cols, cols), np.float32)
    for ch in range(3):
        table[ch, :, :, ch * tiles : (ch + 1) * tiles] = belongs
    return table.reshape(6 * cols, cols)


def wide_table(tiles, cols, kinds):
    belongs = (np.arange(cols)[None, :] // TILE == np.arange(tiles)[:, None]).astype(np.float32)
    return np.tile(np.kron(np.eye(kinds, dtype=np.float32), belongs), (3, 1))


def per_device(
    gaussians,
    first_moment,
    second_moment,
    camera,
    target,
    block_list,
    block_count,
    tile_start,
    tile_end,
):
    views_n = lax.axis_size("view")
    bands_n = lax.axis_size("band")
    devices = views_n * bands_n
    blocks, comps, block_len = gaussians.shape
    list_len = block_list.shape[2]
    rows, cols = target.shape[2:]
    tiles = cols // TILE
    halves = block_len // 128
    geometry = (views_n, bands_n, blocks, list_len, rows, cols, block_len)

    across, first, second = smoothing_tables(rows, cols, 3)
    power = power_table(tiles, cols)
    shade = shade_table(tiles, cols).astype(BF16)
    quad = wide_table(tiles, cols, 6).astype(BF16)
    tone = wide_table(tiles, cols, 3).astype(BF16)
    vmem = pl.BlockSpec(memory_space=pltpu.VMEM)
    hbm = pl.BlockSpec(memory_space=pltpu.HBM)

    def by_comp(array):
        return jnp.transpose(array, (1, 0, 2))

    window = TILE_MOST * block_len
    tint_pad = up8(3 * halves + 1)
    basis_lanes = BASIS * blocks
    shape = jax.ShapeDtypeStruct((comps, blocks, block_len), F32)
    scalar = jax.ShapeDtypeStruct((1, 1), F32)
    kept = pltpu.VMEM(shape.shape, F32)
    gradient, params, one, two, mean_loss = pl.pallas_call(
        functools.partial(step_kernel, geometry),
        out_shape=(kept, kept, kept, kept, pltpu.HBM((1, 1), F32)),
        in_specs=[hbm] * 15,
        out_specs=(vmem,) * 4 + (hbm,),
        scratch_shapes=[
            pltpu.SMEM((1, 9), F32),
            pltpu.SMEM((1, 1, list_len), jnp.int32),
            pltpu.SMEM((1, 1, tiles), jnp.int32),
            pltpu.SMEM((1, 1, tiles), jnp.int32),
            pltpu.VMEM((1, 3, rows, cols), F32),
            pltpu.VMEM(across.shape, F32),
            pltpu.VMEM(first.shape, F32),
            pltpu.VMEM(second.shape, F32),
            pltpu.VMEM((second.shape[0], 3 * second.shape[1]), BF16),
            pltpu.VMEM((3 * cols, cols), BF16),
            pltpu.VMEM(power.shape, F32),
            pltpu.VMEM(shade.shape, BF16),
            pltpu.VMEM(quad.shape, BF16),
            pltpu.VMEM(tone.shape, BF16),
            pltpu.VMEM((views_n, 1, 128), F32),
            pltpu.VMEM((devices, 1, 128), F32),
            pltpu.VMEM((devices, 128), F32),
            pltpu.VMEM((1, 1), F32),
            pltpu.VMEM((128, 128), BF16),
            pltpu.VMEM((128, basis_lanes + 5 * 128), BF16),
            pltpu.VMEM((halves, GEO_COMPS, 3 * blocks, 128), BF16),
            pltpu.VMEM((halves, 3, basis_lanes, 3 * 128), BF16),
            pltpu.VMEM((3 * devices, basis_lanes), BF16),
            pltpu.VMEM((9 * devices, 128), BF16),
            pltpu.VMEM((9 * devices, 128), BF16),
            (pltpu.VMEM((devices, up8(RECORDS), 128), F32),) * halves,
            (pltpu.VMEM((devices, up8(RECORDS), 128), F32),) * halves,
            pltpu.VMEM((halves, TILE_MOST, RECORDS * tiles, 128), F32),
            pltpu.VMEM((devices, tint_pad, 128), F32),
            pltpu.VMEM((devices, tint_pad, 128), F32),
            (pltpu.VMEM((devices, up8(GEO_REC), 128), F32),) * halves,
            (pltpu.VMEM((devices, up8(GEO_REC), 128), F32),) * halves,
            pltpu.VMEM((2, 3, REACH, cols), F32),
            pltpu.VMEM((2, 3, REACH, cols), F32),
            pltpu.VMEM((2, 3, REACH, cols), F32),
            pltpu.VMEM((2, 3, REACH, cols), F32),
            pltpu.VMEM((7, window, cols), F32),
            pltpu.VMEM((window, rows // 8, 8, cols), F32),
            pltpu.VMEM((window, rows // 8, 8, cols), F32),
            pltpu.VMEM((3, window * 4, cols), F32),
            pltpu.SemaphoreType.DMA((3 + 2 * halves,)),
            pltpu.SemaphoreType.DMA((3 + 2 * halves,)),
            pltpu.SemaphoreType.DMA((2, 2)),
            pltpu.SemaphoreType.DMA((2, 2)),
            pltpu.SemaphoreType.DMA((16,)),
        ],
        compiler_params=pltpu.CompilerParams(
            collective_id=0, has_side_effects=True, vmem_limit_bytes=40 * 1024 * 1024
        ),
        name="render_step",
    )(
        *[
            pltpu.with_memory_space_constraint(array, pltpu.HBM)
            for array in (
                camera,
                block_list,
                tile_start,
                tile_end,
                target,
                by_comp(gaussians),
                by_comp(first_moment),
                by_comp(second_moment),
                across,
                first,
                second,
                power,
                shade,
                quad,
                tone,
            )
        ]
    )

    new_params, new_one, new_two, out_gradient, out_loss = pl.pallas_call(
        adam_kernel,
        out_shape=(shape, shape, shape, shape, scalar),
        in_specs=[vmem] * 4 + [hbm],
        out_specs=(hbm, hbm, hbm, hbm, hbm),
        scratch_shapes=[pltpu.VMEM((SHAPE_COMPS, blocks, block_len), F32)] * 3
        + [pltpu.SemaphoreType.DMA((5,))],
        compiler_params=pltpu.CompilerParams(vmem_limit_bytes=16 * 1024 * 1024),
        name="adam_step",
    )(gradient, params, one, two, pltpu.with_memory_space_constraint(mean_loss, pltpu.HBM))
    return (
        by_comp(new_params),
        by_comp(new_one),
        by_comp(new_two),
        out_loss.reshape(()),
        by_comp(out_gradient),
    )


def solution(mesh):
    return jax.shard_map(
        per_device,
        mesh=mesh,
        in_specs=(
            P(("view", "band"), None, None),
            P(("view", "band"), None, None),
            P(("view", "band"), None, None),
            P("view", None),
            P("view", None, "band", None),
            P("view", "band", None),
            P("view", "band"),
            P("view", "band", None),
            P("view", "band", None),
        ),
        out_specs=(
            P(("view", "band"), None, None),
            P(("view", "band"), None, None),
            P(("view", "band"), None, None),
            P(),
            P(("view", "band"), None, None),
        ),
        check_vma=False,
    )
```

```python
import functools
import math

import jax
import jax.numpy as jnp
import numpy as np
from jax import lax
from jax.experimental import pallas as pl
from jax.experimental.pallas import tpu as pltpu
from jax.sharding import PartitionSpec as P

TILE = 16
TILE_MOST = 2
HALO = 5
REACH = 2 * HALO
GEO_REC = 6
RECORDS = 9
PIECES = 3
SHAPE_COMPS = 14
UNROLL = 4

HIGHEST_MODE = lax.Precision.HIGHEST
SSIM_WEIGHT = 0.2
ABS_WEIGHT = 0.8
STAB_MEAN = 0.0001
STAB_VAR = 0.0009
BIAS_FIRST = 1.0 - math.exp(100.0 * math.log(0.9))
BIAS_SECOND = 1.0 - math.exp(100.0 * math.log(0.999))
LOG2_E = math.log2(math.e)
SH_ZERO = 0.28209479177387814
SH_ONE = 0.4886025119029199
SH_TWO = [
    1.0925484305920792,
    -1.0925484305920792,
    0.31539156525252005,
    -1.0925484305920792,
    0.5462742152960396,
]
SH_THREE = [
    -0.5900435899266435,
    2.890611442640554,
    -0.4570457994644658,
    0.3731763325901154,
    -0.4570457994644658,
    1.445305721320277,
    -0.5900435899266435,
]
F32 = jnp.float32
BF16 = jnp.bfloat16
MESH = pl.DeviceIdType.MESH
NEVER = -1e30


RATES = ((6, 0.016), (9, 0.005), (13, 0.001), (14, 0.05), (17, 0.0025), (62, 0.000125))


def learning_rate(component):
    rate = RATES[-1][1] / BIAS_FIRST
    if isinstance(component, int):
        return next(value for end, value in RATES if component < end) / BIAS_FIRST
    for end, value in reversed(RATES[:-1]):
        rate = jnp.where(component < end, value / BIAS_FIRST, rate)
    return rate


def kernel_taps():
    raw_taps = [math.exp(-(offset * offset) / 4.5) for offset in range(-5, 6)]
    tap_total = sum(raw_taps)
    return [raw_tap / tap_total for raw_tap in raw_taps]


def up8(value):
    return (value + 7) // 8 * 8


def smoothing_tables(rows, cols, channels):
    taps = kernel_taps()
    in_rows, mid_rows = up8(rows + 2 * REACH), up8(rows + REACH)
    across = np.zeros((cols, cols), np.float32)
    for out in range(cols):
        for m in range(-HALO, HALO + 1):
            if 0 <= out + m < cols:
                across[out + m, out] = taps[m + HALO]
    first = np.zeros((channels * mid_rows, channels * in_rows), np.float32)
    second = np.zeros((channels * rows, channels * mid_rows), np.float32)
    for c in range(channels):
        for e in range(rows + REACH):
            for m in range(REACH + 1):
                first[c * mid_rows + e, c * in_rows + e + m] = taps[m]
        for i in range(rows):
            for m in range(REACH + 1):
                second[c * rows + i, c * mid_rows + i + m] = taps[m]
    return across, first, second


def harmonics(dir_x, dir_y, dir_z):
    sq_x, sq_y, sq_z = (dir_x * dir_x, dir_y * dir_y, dir_z * dir_z)
    return [
        SH_ZERO + 0.0 * dir_x,
        -SH_ONE * dir_y,
        SH_ONE * dir_z,
        -SH_ONE * dir_x,
        SH_TWO[0] * dir_x * dir_y,
        SH_TWO[1] * dir_y * dir_z,
        SH_TWO[2] * (2.0 * sq_z - sq_x - sq_y),
        SH_TWO[3] * dir_x * dir_z,
        SH_TWO[4] * (sq_x - sq_y),
        SH_THREE[0] * dir_y * (3.0 * sq_x - sq_y),
        SH_THREE[1] * dir_x * dir_y * dir_z,
        SH_THREE[2] * dir_y * (4.0 * sq_z - sq_x - sq_y),
        SH_THREE[3] * dir_z * (2.0 * sq_z - 3.0 * sq_x - 3.0 * sq_y),
        SH_THREE[4] * dir_x * (4.0 * sq_z - sq_x - sq_y),
        SH_THREE[5] * dir_z * (sq_x - sq_y),
        SH_THREE[6] * dir_x * (sq_x - 3.0 * sq_y),
    ]


def camera_basis(affine):
    a, b = affine[0:3], affine[3:6]
    n_x = a[1] * b[2] - a[2] * b[1]
    n_y = a[2] * b[0] - a[0] * b[2]
    n_z = a[0] * b[1] - a[1] * b[0]
    length = jnp.sqrt(n_x * n_x + n_y * n_y + n_z * n_z)
    return harmonics(n_x / length, n_y / length, n_z / length)


def split3(value, axis=0):
    high = value.astype(BF16)
    rest = value - high.astype(F32)
    middle = rest.astype(BF16)
    low = (rest - middle.astype(F32)).astype(BF16)
    return high, middle, low


NN = ((1,), (0,))
NT = ((1,), (1,))
TN = ((0,), (0,))


def mx(a, b, dims=NN):
    return lax.dot_general(a, b, (dims, ((), ())), preferred_element_type=F32)


def split2(value):
    high = value.astype(BF16)
    return high, (value - high.astype(F32)).astype(BF16)


def exact_dot(table, value, dims):
    table = table.astype(BF16)
    total = None
    for part in split3(value):
        term = mx(table, part, dims)
        total = term if total is None else total + term
    return total


def stack3(value):
    return jnp.concatenate(split3(value), axis=0)


def stack2(value):
    return jnp.concatenate(split2(value), axis=0)


def adam_step(c, grad_ref, source, landing):
    gradient = grad_ref[c]
    new_one = 0.9 * source[1][c] + 0.1 * gradient
    new_two = 0.999 * source[2][c] + 0.001 * gradient * gradient
    landing[1][c] = new_one
    landing[2][c] = new_two
    bottom = jnp.sqrt(new_two * (1.0 / BIAS_SECOND)) + 1e-08
    landing[0][c] = source[0][c] - learning_rate(c) * new_one / bottom


def block_axes(logs, quats):
    scales = [jnp.exp(value) for value in logs]
    quat_len = jnp.sqrt(
        quats[0] * quats[0] + quats[1] * quats[1] + quats[2] * quats[2] + quats[3] * quats[3]
    )
    r, i, j, k = [value / quat_len for value in quats]
    rotation = [
        [1.0 - 2.0 * (j * j + k * k), 2.0 * (i * j - r * k), 2.0 * (i * k + r * j)],
        [2.0 * (i * j + r * k), 1.0 - 2.0 * (i * i + k * k), 2.0 * (j * k - r * i)],
        [2.0 * (i * k - r * j), 2.0 * (j * k + r * i), 1.0 - 2.0 * (i * i + j * j)],
    ]
    return rotation, scales


def block_shape(logs, quats, logit):
    rotation, scales = block_axes(logs, quats)
    axes = [[rotation[a][c] * scales[c] for c in range(3)] for a in range(3)]

    def moment(a, b):
        return axes[a][0] * axes[b][0] + axes[a][1] * axes[b][1] + axes[a][2] * axes[b][2]

    pairs = ((0, 0), (1, 1), (2, 2), (0, 1), (0, 2), (1, 2))
    return [moment(a, b) for a, b in pairs], 1.0 / (1.0 + jnp.exp(-logit))


def view_terms(cam):
    a, b, time = cam[0:3], cam[3:6], cam[8]
    terms = a + [time * value for value in a] + b + [time * value for value in b]
    crossed = ((0, 1), (0, 2), (1, 2))
    terms += [a[c] * a[c] for c in range(3)] + [2.0 * a[c] * a[d] for c, d in crossed]
    terms += [a[c] * b[c] for c in range(3)] + [a[c] * b[d] + a[d] * b[c] for c, d in crossed]
    terms += [b[c] * b[c] for c in range(3)] + [2.0 * b[c] * b[d] for c, d in crossed]
    return terms + [cam[6], cam[7], time] + camera_basis(cam[0:6])


TERM_ROWS = 6
SHIFT_AT = 30
BASIS_AT = 33
BASIS = 16
TERMS = 49
GEO_COMPS = 19


def step_kernel(
    geometry,
    camera_hbm,
    list_hbm,
    start_hbm,
    end_hbm,
    target_hbm,
    gauss_hbm,
    one_hbm,
    two_hbm,
    across_hbm,
    first_hbm,
    second_hbm,
    power_hbm,
    shade_hbm,
    quad_hbm,
    tone_hbm,
    grad_ref,
    gauss_ref,
    one_ref,
    two_ref,
    loss_ref,
    camera_s,
    list_s,
    start_s,
    end_s,
    target_ref,
    across_ref,
    first_ref,
    second_ref,
    second_k,
    across_k,
    power_ref,
    shade_ref,
    quad_ref,
    tone_ref,
    msg_out,
    msg_in,
    asked_ref,
    loss_v,
    hot_map,
    wide_map,
    geo_tab,
    tint_tab,
    tint_back,
    line_back,
    shape_back,
    rec_out,
    rec_in,
    rec_pick,
    shade_out,
    shade_in,
    grad_out,
    grad_in,
    halo_out,
    halo_in,
    thalo_out,
    thalo_in,
    coef,
    alpha_s,
    weight_s,
    moment_s,
    send_sem,
    recv_sem,
    halo_send,
    halo_recv,
    fetch_sem,
):
    views_n, bands_n, blocks, list_len, rows, cols, block_len = geometry
    devices = views_n * bands_n
    tiles = cols // TILE
    pairs = TILE_MOST * tiles
    window = TILE_MOST * block_len
    halves = block_len // 128
    pair_len = TILE_MOST * 128
    tint_rows = 3 * halves
    hot_lanes = bands_n * blocks
    basis_lanes = BASIS * blocks
    view = lax.axis_index("view")
    band = lax.axis_index("band")
    me = band * views_n + view
    has_up = band > 0
    has_down = band < bands_n - 1

    halo_in[...] = jnp.zeros_like(halo_in)
    thalo_in[...] = jnp.zeros_like(thalo_in)
    peer_view = [lax.rem(view + d, views_n) for d in range(views_n)]
    peer_band = [lax.rem(band + d, bands_n) for d in range(bands_n)]
    barrier = pltpu.get_barrier_semaphore()
    for d in range(1, views_n):
        pl.semaphore_signal(barrier, inc=1, device_id=(peer_view[d], band), device_id_type=MESH)
    for d in range(1, bands_n):
        pl.semaphore_signal(barrier, inc=1, device_id=(view, peer_band[d]), device_id_type=MESH)

    sources = (
        (camera_hbm, camera_s),
        (list_hbm, list_s),
        (start_hbm, start_s),
        (end_hbm, end_s),
        (target_hbm, target_ref),
        (gauss_hbm, gauss_ref),
        (quad_hbm, quad_ref),
        (tone_hbm, tone_ref),
        (power_hbm, power_ref),
        (shade_hbm, shade_ref),
        (across_hbm, across_ref),
        (first_hbm, first_ref),
        (second_hbm, second_ref),
        (one_hbm, one_ref),
        (two_hbm, two_ref),
    )
    fetches = [
        pltpu.make_async_copy(source, landing, fetch_sem.at[n])
        for n, (source, landing) in enumerate(sources)
    ]
    for fetch in fetches:
        fetch.start()

    def to_all(source, landing, length, phase):
        half = bands_n // 2
        band_order = sorted(range(bands_n), key=lambda d: (d == 0, abs(d - half), d))
        for d_view in range(views_n - 1, -1, -1):
            for d_band in band_order:
                if d_view + d_band == 0:
                    continue
                peer = peer_band[d_band] * views_n + peer_view[d_view]
                pltpu.make_async_remote_copy(
                    src_ref=source.at[peer, pl.ds(0, length)],
                    dst_ref=landing.at[me, pl.ds(0, length)],
                    send_sem=send_sem.at[phase],
                    recv_sem=recv_sem.at[phase],
                    device_id=(peer_view[d_view], peer_band[d_band]),
                    device_id_type=MESH,
                ).start()

    def wait_all(landing, length, phase):
        every = landing.at[pl.ds(0, devices - 1), pl.ds(0, length)]
        pltpu.make_async_copy(every, every, recv_sem.at[phase]).wait()
        pltpu.make_async_copy(every, every, send_sem.at[phase]).wait()

    def edge_copy(source, landing, direction, phase):
        step = -1 if direction == 0 else 1
        return pltpu.make_async_remote_copy(
            src_ref=source.at[direction],
            dst_ref=landing.at[1 - direction],
            send_sem=halo_send.at[phase, direction],
            recv_sem=halo_recv.at[phase, 1 - direction],
            device_id=(view, band + step),
            device_id_type=MESH,
        )

    def edges_start(source, landing, phase):
        @pl.when(has_up)
        def _():
            edge_copy(source, landing, 0, phase).start()

        @pl.when(has_down)
        def _():
            edge_copy(source, landing, 1, phase).start()

    def edges_wait(source, landing, phase):
        @pl.when(has_up)
        def _():
            up = edge_copy(source, landing, 0, phase)
            up.wait_send()
            pltpu.make_async_copy(
                landing.at[0], landing.at[0], halo_recv.at[phase, 0]
            ).wait()

        @pl.when(has_down)
        def _():
            down = edge_copy(source, landing, 1, phase)
            down.wait_send()
            pltpu.make_async_copy(
                landing.at[1], landing.at[1], halo_recv.at[phase, 1]
            ).wait()

    def lanes_of(shape):
        return lax.broadcasted_iota(jnp.int32, shape, len(shape) - 1)

    map_lane = lanes_of((128, 128))
    map_row = lax.broadcasted_iota(jnp.int32, (128, 128), 0)
    hot_map[...] = jnp.where(
        map_row == band * blocks + lax.rem(map_lane, blocks), 1.0, 0.0
    ).astype(BF16)
    for part in range(basis_lanes // 128):
        wide_map[:, part * 128 : (part + 1) * 128] = jnp.where(
            map_row == hot_lanes + BASIS_AT + part * (128 // blocks) + map_lane // blocks, 1.0, 0.0
        ).astype(BF16)
    for kind in range(5):
        at = basis_lanes + kind * 128
        wide_map[:, at : at + 128] = jnp.where(
            (map_row == hot_lanes + TERM_ROWS * kind + map_lane // blocks)
            & (map_lane < TERM_ROWS * blocks),
            1.0,
            0.0,
        ).astype(BF16)

    fetches[0].wait()
    fetches[1].wait()
    lane = lanes_of((1, 128))
    terms = view_terms([jnp.full((1, 128), camera_s[0, c], F32) for c in range(9)])
    row = jnp.zeros((1, 128), F32)
    for n in range(TERMS):
        row = jnp.where(lane == hot_lanes + n, terms[n], row)
    wanted = lax.broadcasted_iota(jnp.int32, (views_n, 128), 0) * hot_lanes + lanes_of(
        (views_n, 128)
    )
    hits = jnp.zeros((views_n, 128), F32)
    for n in range(list_len):
        hits = jnp.where(wanted == list_s[0, 0, n], 1.0, hits)
    message = jnp.where(lanes_of((views_n, 128)) < hot_lanes, hits, row)
    for v in range(views_n):
        msg_out[v] = message[v : v + 1]

    pl.semaphore_wait(barrier, views_n + bands_n - 2)
    for d in range(1, views_n):
        pltpu.make_async_remote_copy(
            src_ref=msg_out.at[peer_view[d]],
            dst_ref=msg_in.at[me],
            send_sem=send_sem.at[0],
            recv_sem=recv_sem.at[0],
            device_id=(peer_view[d], band),
            device_id_type=MESH,
        ).start()
    msg_in[me] = msg_out[view]
    fetches[2].wait()
    fetches[3].wait()
    fetches[4].wait()
    thalo_out[0] = target_ref[0, :, 0:REACH, :]
    thalo_out[1] = target_ref[0, :, rows - REACH : rows, :]
    edges_start(thalo_out, thalo_in, 0)

    owners, alive = [], []
    for k in range(TILE_MOST):
        for t in range(tiles):
            low, high = start_s[0, 0, t], end_s[0, 0, t]
            block = list_s[0, 0, jnp.clip(jnp.minimum(low + k, high - 1), 0, list_len - 1)]
            device = lax.div(jnp.clip(block, 0, devices * blocks - 1), blocks)
            owners.append(lax.rem(device, bands_n) * views_n + lax.div(device, bands_n))
            alive.append(jnp.where(low + k < high, 1.0, 0.0))
    put_lane = lax.rem(lanes_of((devices, 2 * pairs)), pairs)
    put_row = lax.broadcasted_iota(jnp.int32, (devices, 2 * pairs), 0)
    put = jnp.zeros((devices, 2 * pairs), F32)
    for n in range(pairs):
        put = jnp.where((put_lane == n) & (put_row == owners[n]), alive[n], put)
    put = put.astype(BF16)
    tile_sub = lax.broadcasted_iota(jnp.int32, (tiles, 128), 0)
    parts = []
    for k in range(TILE_MOST):
        part = jnp.zeros((tiles, 128), F32)
        for t in range(tiles):
            part = jnp.where(tile_sub == t, alive[k * tiles + t], part)
        parts.append(part)
    keep = jnp.concatenate(parts, axis=1) > 0.5

    plane = msg_in.at[pl.ds(0, views_n - 1)]
    pltpu.make_async_copy(plane, plane, recv_sem.at[0]).wait()
    pltpu.make_async_copy(plane, plane, send_sem.at[0]).wait()
    bundle = msg_in.at[pl.ds(band * views_n, views_n)]
    for d in range(1, bands_n):
        pltpu.make_async_remote_copy(
            src_ref=bundle,
            dst_ref=bundle,
            send_sem=send_sem.at[1],
            recv_sem=recv_sem.at[1],
            device_id=(view, peer_band[d]),
            device_id_type=MESH,
        ).start()

    fetches[5].wait()
    (sigma, opacity), pullback = jax.vjp(
        block_shape,
        [gauss_ref[6 + c] for c in range(3)],
        [gauss_ref[9 + c] for c in range(4)],
        gauss_ref[13],
    )
    rotation, scales = block_axes(
        [gauss_ref[6 + c] for c in range(3)], [gauss_ref[9 + c] for c in range(4)]
    )
    tabled = [gauss_ref[c] for c in range(6)] + [v for line in rotation for v in line] + scales
    for c, value in enumerate(tabled + [opacity]):
        both = stack3(value)
        for h in range(halves):
            geo_tab[h, c] = both[:, h * 128 : (h + 1) * 128]
    for ch in range(3):
        for q in range(BASIS):
            for n, piece in enumerate(split3(gauss_ref[14 + 3 * q + ch])):
                for h in range(halves):
                    tint_tab[
                        h, n, q * blocks : (q + 1) * blocks, ch * 128 : (ch + 1) * 128
                    ] = piece[:, h * 128 : (h + 1) * 128]

    lines = msg_in.at[pl.ds(0, devices - views_n)]
    pltpu.make_async_copy(lines, lines, recv_sem.at[1]).wait()
    pltpu.make_async_copy(lines, lines, send_sem.at[1]).wait()

    for p in range(devices):
        asked_ref[p : p + 1, :] = msg_in[p]
    asked = asked_ref[...]
    asked_parts = split3(asked)
    hot = mx(asked_parts[0], hot_map[...])
    hot_3 = hot[:, 0 : 3 * blocks].astype(BF16)

    def term(n):
        return asked[:, hot_lanes + n : hot_lanes + n + 1]

    ones = [term(c) for c in range(3)], [term(TERM_ROWS + c) for c in range(3)]
    shifts = [term(SHIFT_AT), term(SHIFT_AT + 1), term(SHIFT_AT + 2)]
    stacked = jnp.concatenate(asked_parts, axis=0)

    def widen(low, high):
        wide = mx(stacked, wide_map[:, low:high])
        return wide[0:devices] + wide[devices : 2 * devices] + wide[2 * devices :]

    hot_wide = jnp.concatenate([hot] * (basis_lanes // 128), axis=1)
    basis_parts = split3(widen(0, basis_lanes) * hot_wide)
    basis_three = jnp.concatenate(basis_parts, axis=0)

    def records_of(h):
        picked = [mx(hot_3, geo_tab[h, c]) for c in range(GEO_COMPS)]
        centre = [picked[c] + shifts[2] * picked[3 + c] for c in range(3)]
        turns, scales = [picked[6 + 3 * a : 9 + 3 * a] for a in range(3)], picked[15:18]

        def placed(row, shift):
            return row[0] * centre[0] + row[1] * centre[1] + row[2] * centre[2] + shift

        def turned(row, c):
            return (row[0] * turns[0][c] + row[1] * turns[1][c] + row[2] * turns[2][c]) * scales[c]

        m = [[turned(row, c) for c in range(3)] for row in ones]
        small = mx(basis_parts[0], tint_tab[h, 2])
        middle = mx(basis_three[0 : 2 * devices], tint_tab[h, 1])
        large = mx(basis_three, tint_tab[h, 0])
        colour = small + large[2 * devices :] + middle[devices:]
        colour = colour + (middle[0:devices] + large[devices : 2 * devices])
        colour = 0.5 + (colour + large[0:devices])
        return [
            placed(ones[0], shifts[0]),
            placed(ones[1], shifts[1]),
            m[0][0] * m[0][0] + m[0][1] * m[0][1] + m[0][2] * m[0][2] + 0.3,
            m[0][0] * m[1][0] + m[0][1] * m[1][1] + m[0][2] * m[1][2],
            m[1][0] * m[1][0] + m[1][1] * m[1][1] + m[1][2] * m[1][2] + 0.3,
            picked[18],
        ] + [colour[:, ch * 128 : (ch + 1) * 128] for ch in range(3)]

    for h in range(halves):
        flat_out = rec_out[h].reshape(devices * rec_out[h].shape[1], 128)
        for p, record in enumerate(records_of(h)):
            flat_out[pl.ds(p, devices, stride=rec_out[h].shape[1]), :] = record
        to_all(rec_out[h], rec_in[h], RECORDS, 2 + h)
        rec_in[h][me] = rec_out[h][me]

    tint_back[...] = jnp.concatenate([basis_parts[0], basis_parts[1], basis_parts[0]], axis=0)
    spans = [
        widen(basis_lanes + kind * 128, basis_lanes + (kind + 1) * 128) * hot for kind in range(5)
    ]
    hot_lane = lanes_of((devices, 128))
    hot_last = jnp.where(
        (hot_lane >= TERM_ROWS * blocks) & (hot_lane < (TERM_ROWS + 1) * blocks), hot, 0.0
    )
    for landing, group in ((line_back, spans[0:2] + [hot_last]), (shape_back, spans[2:5])):
        high, low = split2(jnp.concatenate(group, axis=0))
        landing[...] = jnp.concatenate([high, low, high], axis=0)

    for n in range(6, 13):
        fetches[n].wait()
    high, low = split2(second_ref[...])
    second_k[...] = jnp.concatenate([high, high, low], axis=1)
    high, low = split2(across_ref[...])
    across_k[...] = jnp.concatenate([high, high, low], axis=0)
    edges_wait(thalo_out, thalo_in, 0)
    in_rows, mid_rows = up8(rows + 2 * REACH), up8(rows + REACH)
    high_rows = 3 * mid_rows
    fill = jnp.zeros((in_rows - rows - 2 * REACH, cols), F32)

    def smooth(fields):
        down = jnp.dot(
            first_ref[...],
            jnp.concatenate(fields, axis=1),
            precision=HIGHEST_MODE,
            preferred_element_type=F32,
        )
        stack = jnp.concatenate(
            [down[:, f * cols : (f + 1) * cols] for f in range(len(fields))], axis=0
        )
        flat = jnp.dot(
            stack, across_ref[...], precision=HIGHEST_MODE, preferred_element_type=F32
        )
        return [flat[f * high_rows : (f + 1) * high_rows] for f in range(len(fields))]

    mine = target_ref[0]
    ext_y = jnp.concatenate(
        [v for ch in range(3) for v in (thalo_in[0, ch], mine[ch], thalo_in[1, ch], fill)], axis=0
    )
    mean_y, square_y = smooth([ext_y, ext_y * ext_y])

    tile_row = lax.broadcasted_iota(jnp.int32, (tiles, pair_len), 0).astype(F32)
    column = lax.rem(lanes_of((128, cols)), TILE).astype(F32) + (0.5 - 0.5 * TILE)

    def prepare(h):
        for k in range(TILE_MOST):
            for t in range(tiles):
                rec_pick[h, k, pl.ds(t, RECORDS, stride=tiles), :] = rec_in[h][
                    owners[k * tiles + t], 0:RECORDS, :
                ]

        def gathered(p):
            return jnp.concatenate(
                [rec_pick[h, k, p * tiles : (p + 1) * tiles, :] for k in range(TILE_MOST)], axis=1
            )

        u_rel = gathered(0) - (tile_row * TILE + 0.5 * TILE)
        w_rel = gathered(1) - ((band * rows).astype(F32) + 0.5 * TILE)
        c_a, c_b, c_c, opac = [gathered(p) for p in range(2, GEO_REC)]
        inv_det = 1.0 / (c_a * c_c - c_b * c_b)
        coef_a = -0.5 * c_c * inv_det
        coef_b = c_b * inv_det
        coef_c = -0.5 * c_a * inv_det

        def masked(value, other=0.0):
            return jnp.where(keep, value, other)

        quads = jnp.concatenate(
            [
                masked(LOG2_E * jnp.log(opac), NEVER),
                LOG2_E * coef_a,
                LOG2_E * coef_b,
                LOG2_E * coef_c,
                u_rel,
                w_rel,
            ],
            axis=0,
        )
        tones = jnp.concatenate(
            [masked(gathered(GEO_REC + ch)) for ch in range(3)], axis=0
        )
        grown = [
            mx(stack3(quads), quad_ref[...], TN),
            mx(stack3(tones), tone_ref[...], TN),
        ]
        for k in range(TILE_MOST):
            at = k * block_len + h * 128
            flat, part_a, part_b, part_c, u_wide, w_wide = [
                grown[0][k * 128 : (k + 1) * 128, n * cols : (n + 1) * cols] for n in range(6)
            ]
            e_x = column - u_wide
            coef[0, at : at + 128, :] = flat + part_a * e_x * e_x
            coef[1, at : at + 128, :] = part_b * e_x
            coef[2, at : at + 128, :] = part_c
            coef[6, at : at + 128, :] = w_wide
            for ch in range(3):
                coef[3 + ch, at : at + 128, :] = grown[1][
                    k * 128 : (k + 1) * 128, ch * cols : (ch + 1) * cols
                ]
        return u_rel, w_rel, c_a, c_b, c_c, opac, inv_det, coef_a, coef_b, coef_c

    wait_all(rec_in[0], RECORDS, 2)
    shapes = [prepare(0)]

    sub8 = lax.broadcasted_iota(jnp.int32, (8, cols), 0).astype(F32)
    parts_n = rows // 8
    row_local = [sub8 + (8.0 * part + 0.5 - 0.5 * TILE) for part in range(parts_n)]

    def spread_row(kind, j):
        return coef[kind, pl.ds(j, 8, stride=0), :]

    def blend(group, carry):
        trans, image = carry
        trans, image = list(trans), list(image)
        for k in range(8):
            j = group * 8 + k
            q0, q1, q2 = spread_row(0, j), spread_row(1, j), spread_row(2, j)
            low = spread_row(6, j)
            tint = [spread_row(3 + ch, j) for ch in range(3)]
            for part in range(parts_n):
                e_y = row_local[part] - low
                alpha = jnp.exp2(q0 + e_y * (q1 + e_y * q2))
                weight = alpha * trans[part]
                alpha_s[j, part] = alpha
                weight_s[j, part] = weight
                trans[part] = trans[part] * (1.0 - alpha)
                for ch in range(3):
                    at = ch * parts_n + part
                    image[at] = image[at] + weight * tint[ch]
        return tuple(trans), tuple(image)

    zero = jnp.zeros((8, cols), F32)
    state = (tuple([zero + 1.0] * parts_n), tuple([zero] * (3 * parts_n)))
    state = lax.fori_loop(0, 128 // 8, blend, state, unroll=UNROLL)
    for h in range(1, halves):
        wait_all(rec_in[h], RECORDS, 2 + h)
        shapes.append(prepare(h))
    _, image = lax.fori_loop(128 // 8, window // 8, blend, state, unroll=UNROLL)
    pred = [
        jnp.concatenate([image[ch * parts_n + part] for part in range(parts_n)], axis=0)
        for ch in range(3)
    ]
    for ch in range(3):
        halo_out[0, ch] = pred[ch][0:REACH]
        halo_out[1, ch] = pred[ch][rows - REACH : rows]
    edges_start(halo_out, halo_in, 1)
    edges_wait(halo_out, halo_in, 1)

    ext_x = jnp.concatenate(
        [v for ch in range(3) for v in (halo_in[0, ch], pred[ch], halo_in[1, ch], fill)], axis=0
    )
    mean_x, square_x, cross = smooth([ext_x, ext_x * ext_x, ext_x * ext_y])
    n_mean = 2.0 * mean_x * mean_y + STAB_MEAN
    n_var = 2.0 * (cross - mean_x * mean_y) + STAB_VAR
    d_mean = mean_x * mean_x + mean_y * mean_y + STAB_MEAN
    d_var = (square_x - mean_x * mean_x) + (square_y - mean_y * mean_y) + STAB_VAR
    inv_mean = 1.0 / d_mean
    inv_var = 1.0 / d_var
    inverse = inv_mean * inv_var
    ssim = n_mean * n_var * inverse
    ext_row = lax.broadcasted_iota(jnp.int32, (high_rows, cols), 0) % mid_rows
    image_row = ext_row + (band * rows - HALO)
    inside = (image_row >= 0) & (image_row < bands_n * rows) & (ext_row < rows + REACH)
    scale = -SSIM_WEIGHT / 3.0
    part_mean = 2.0 * mean_y * (n_var - n_mean) * inverse - 2.0 * mean_x * ssim * (
        inv_mean - inv_var
    )
    adjoint = jnp.concatenate(
        [
            jnp.where(inside, scale * part_mean, 0.0),
            jnp.where(inside, -scale * ssim * inv_var, 0.0),
            jnp.where(inside, (2.0 * scale) * n_mean * inverse, 0.0),
        ],
        axis=1,
    )
    high, low = split2(adjoint)
    down2 = mx(second_k[...], jnp.concatenate([high, low, high], axis=0))
    stacked2 = jnp.concatenate([down2[:, f * cols : (f + 1) * cols] for f in range(3)], axis=0)
    high, low = split2(stacked2)
    spread = mx(jnp.concatenate([high, low, high], axis=1), across_k[...])
    deep = 3 * rows
    pred_all = jnp.concatenate(pred, axis=0)
    mine_all = jnp.concatenate([mine[ch] for ch in range(3)], axis=0)
    error = pred_all - mine_all
    sign = jnp.where(error > 0.0, 1.0, jnp.where(error < 0.0, -1.0, 0.0))
    grad_pred = (
        ABS_WEIGHT / 3.0 * sign
        + spread[0:deep]
        + 2.0 * pred_all * spread[deep : 2 * deep]
        + mine_all * spread[2 * deep : 3 * deep]
    )
    own = (ext_row >= HALO) & (ext_row < HALO + rows)
    loss = jnp.sum(ABS_WEIGHT / 3.0 * jnp.abs(error), keepdims=True) + jnp.sum(
        jnp.where(own, SSIM_WEIGHT / 3.0 * (1.0 - ssim), 0.0), keepdims=True
    )

    pull = [
        [grad_pred[ch * rows + 8 * part : ch * rows + 8 * part + 8] for part in range(parts_n)]
        for ch in range(3)
    ]

    upper = lax.broadcasted_iota(jnp.int32, (8, cols), 0) < 4

    def keep_pair(held, kind, group, k, total):
        other = held.pop((kind, k // 2), None)
        if other is None:
            held[kind, k // 2] = total
            return
        a, b = (other, total) if k % 2 else (total, other)
        joined = jnp.where(upper, a, b) + pltpu.roll(jnp.where(upper, b, a), 4, 0)
        at = pl.multiple_of(group * 32 + k // 2 * 8, 8)
        moment_s[kind, pl.ds(at, 8), :] = joined

    def shades(group, carry):
        held = {}
        for k in range(8):
            j = group * 8 + k
            weight = [weight_s[j, part] for part in range(parts_n)]
            for ch in range(3):
                total = weight[0] * pull[ch][0]
                for part in range(1, parts_n):
                    total = total + weight[part] * pull[ch][part]
                keep_pair(held, ch, group, k, total)
        return carry

    def summed(kind, start, count):
        folded = moment_s.at[kind]
        quarter = [folded[pl.ds(start * 4 + sub, count, stride=4), :] for sub in range(4)]
        return (quarter[0] + quarter[1]) + (quarter[2] + quarter[3])

    lax.fori_loop(0, window // 8, shades, 0, unroll=UNROLL)

    def route(value, length):
        stack = jnp.concatenate(
            [value[:, k * length : (k + 1) * length] for k in range(TILE_MOST)], axis=0
        )
        return mx(put, stack2(stack))

    shade_flat = shade_out.reshape(devices * shade_out.shape[1], 128)
    folded = [piece for ch in range(3) for piece in split2(summed(ch, 0, window))]
    by_tile = jnp.transpose(mx(jnp.concatenate(folded, axis=1), shade_ref[...]))
    for ch in range(3):
        routed = route(by_tile[ch * tiles : (ch + 1) * tiles], block_len)
        for h in range(halves):
            shade_flat[pl.ds(ch * halves + h, devices, stride=shade_out.shape[1]), :] = routed[
                :, h * 128 : (h + 1) * 128
            ]
    shade_flat[pl.ds(tint_rows, devices, stride=shade_out.shape[1]), :] = jnp.broadcast_to(
        loss, (devices, 128)
    )
    to_all(shade_out, shade_in, tint_rows + 1, 2 + halves)
    shade_in[me] = shade_out[me]

    def unblend(step, behind):
        group = window // 8 - 1 - step
        behind = list(behind)
        held = {}
        for k in reversed(range(8)):
            j = group * 8 + k
            tint = [spread_row(3 + ch, j) for ch in range(3)]
            totals = [None] * 3
            for part in range(parts_n):
                alpha = alpha_s[j, part]
                shade = (
                    tint[0] * pull[0][part] + tint[1] * pull[1][part] + tint[2] * pull[2][part]
                )
                gap = shade - behind[part]
                behind[part] = behind[part] + alpha * gap
                lean = weight_s[j, part] * gap
                lean_r = lean * row_local[part]
                terms = [lean, lean_r, lean_r * row_local[part]]
                totals = [
                    value if total is None else total + value
                    for value, total in zip(terms, totals)
                ]
            for kind in range(3):
                keep_pair(held, kind, group, k, totals[kind])
        return tuple(behind)

    def derive(h):
        u_rel, w_rel, c_a, c_b, c_c, opac, inv_det, coef_a, coef_b, coef_c = shapes[h]
        moments = [
            jnp.concatenate(
                [summed(n, k * block_len + h * 128, 128) for k in range(TILE_MOST)],
                axis=0,
            )
            for n in range(3)
        ]
        power = power_ref[...]
        by_x = exact_dot(power, moments[0], NT)
        m_00, m_10, m_20 = by_x[0:tiles], by_x[tiles : 2 * tiles], by_x[2 * tiles : 3 * tiles]
        by_xr = exact_dot(power[0 : 2 * tiles], moments[1], NT)
        m_01, m_11 = by_xr[0:tiles], by_xr[tiles : 2 * tiles]
        m_02 = exact_dot(power[0:tiles], moments[2], NT)
        s_x = m_10 - u_rel * m_00
        s_y = m_01 - w_rel * m_00
        s_xx = m_20 - 2.0 * u_rel * m_10 + u_rel * u_rel * m_00
        s_xy = m_11 - u_rel * m_01 - w_rel * m_10 + u_rel * w_rel * m_00
        s_yy = m_02 - 2.0 * w_rel * m_01 + w_rel * w_rel * m_00
        by_det = -(coef_a * s_xx + coef_b * s_xy + coef_c * s_yy) * inv_det
        derivs = [
            -(2.0 * coef_a * s_x + coef_b * s_y),
            -(2.0 * coef_c * s_y + coef_b * s_x),
            -0.5 * inv_det * s_yy + by_det * c_c,
            inv_det * s_xy - 2.0 * c_b * by_det,
            -0.5 * inv_det * s_xx + by_det * c_a,
            m_00 / opac,
        ]
        flat_out = grad_out[h].reshape(devices * grad_out[h].shape[1], 128)
        for p in range(GEO_REC):
            flat_out[pl.ds(p, devices, stride=grad_out[h].shape[1]), :] = route(derivs[p], 128)
        to_all(grad_out[h], grad_in[h], GEO_REC, 2 + halves + 1 + h)
        grad_in[h][me] = grad_out[h][me]

    groups = window // 8
    last = groups - 128 // 8
    behind = lax.fori_loop(0, last, unblend, tuple([zero] * parts_n), unroll=UNROLL)
    for h in range(halves - 1, 0, -1):
        derive(h)
    lax.fori_loop(last, groups, unblend, behind, unroll=UNROLL)
    derive(0)
    wait_all(shade_in, tint_rows + 1, 2 + halves)
    shade_back = shade_in.reshape(devices * shade_in.shape[1], 128)

    def arrived(landed, stride, p):
        return jnp.concatenate(
            [landed[pl.ds(p * halves + h, devices, stride=stride), :] for h in range(halves)],
            axis=1,
        )

    def spread_back(table, values):
        high, low = split2(jnp.concatenate(values, axis=0))
        return mx(table[...], jnp.concatenate([high, high, low], axis=0), TN)

    for ch in range(3):
        colour = spread_back(tint_back, [arrived(shade_back, shade_in.shape[1], ch)])
        for q in range(BASIS):
            grad_ref[14 + 3 * q + ch] = colour[q * blocks : (q + 1) * blocks]
    losses = shade_back[pl.ds(tint_rows, devices, stride=shade_in.shape[1]), :]
    loss_v[...] = jnp.sum(losses, axis=0, keepdims=True)[:, 0:1] * (
        1.0 / (devices * rows * cols)
    )
    loss_copy = pltpu.make_async_copy(loss_v, loss_ref, fetch_sem.at[len(sources)])
    loss_copy.start()
    fetches[13].wait()
    fetches[14].wait()

    def update(c, carry):
        adam_step(c, grad_ref, (gauss_ref, one_ref, two_ref), (gauss_ref, one_ref, two_ref))
        return carry

    lax.fori_loop(SHAPE_COMPS, gauss_ref.shape[0], update, 0, unroll=4)

    for h in range(halves - 1, -1, -1):
        wait_all(grad_in[h], GEO_REC, 2 + halves + 1 + h)
    grad_back = [
        grad_in[h].reshape(devices * grad_in[h].shape[1], 128) for h in range(halves)
    ]
    geos = [
        jnp.concatenate(
            [back[pl.ds(p, devices, stride=grad_in[0].shape[1]), :] for back in grad_back], axis=1
        )
        for p in range(GEO_REC)
    ]
    line = spread_back(line_back, [geos[0], geos[1], geos[5]])
    shape = spread_back(shape_back, geos[2:5])

    def comp(value, n):
        return value[n * blocks : (n + 1) * blocks]

    d_logs, d_quats, d_logit = pullback(
        ([comp(shape, n) for n in range(TERM_ROWS)], comp(line, TERM_ROWS))
    )
    columns = [comp(line, n) for n in range(TERM_ROWS)] + list(d_logs) + list(d_quats) + [d_logit]
    for c, value in enumerate(columns):
        grad_ref[c] = value
    loss_copy.wait()


def adam_kernel(
    grad_ref,
    gauss_ref,
    one_ref,
    two_ref,
    loss_in,
    out_gauss,
    out_one,
    out_two,
    out_grad,
    loss_out,
    gauss_v,
    one_v,
    two_v,
    write_sem,
):
    comps = gauss_ref.shape[0]
    held = [(grad_ref, out_grad), (gauss_ref, out_gauss), (one_ref, out_one), (two_ref, out_two)]
    fresh = [(gauss_v, out_gauss), (one_v, out_one), (two_v, out_two)]
    total = pltpu.make_async_copy(loss_in, loss_out, write_sem.at[4])
    total.start()

    def send(group, low, high, first):
        part = pl.ds(low, high - low)
        for n, (source, landing) in enumerate(group, first):
            copy = pltpu.make_async_copy(
                source.at[part], landing.at[part], write_sem.at[n]
            )
            copy.start()

    for piece in range(PIECES):
        low = SHAPE_COMPS + piece * (comps - SHAPE_COMPS) // PIECES
        high = SHAPE_COMPS + (piece + 1) * (comps - SHAPE_COMPS) // PIECES
        send(held, low, high, 0)
    send(held[0:1], 0, SHAPE_COMPS, 0)
    for c in range(SHAPE_COMPS):
        adam_step(c, grad_ref, (gauss_ref, one_ref, two_ref), (gauss_v, one_v, two_v))
    send(fresh, 0, SHAPE_COMPS, 1)
    total.wait()
    for n, (source, landing) in enumerate(held):
        pltpu.make_async_copy(source, landing, write_sem.at[n]).wait()


def power_table(tiles, cols):
    lane = np.arange(cols)
    local = lane % TILE + 0.5 - TILE / 2
    belongs = (lane[None, :] // TILE == np.arange(tiles)[:, None]).astype(np.float32)
    return np.concatenate([belongs, belongs * local, belongs * local * local]).astype(np.float32)


def shade_table(tiles, cols):
    belongs = (np.arange(cols)[:, None] // TILE == np.arange(tiles)[None, :]).astype(np.float32)
    table = np.zeros((3, 2, cols, cols), np.float32)
    for ch in range(3):
        table[ch, :, :, ch * tiles : (ch + 1) * tiles] = belongs
    return table.reshape(6 * cols, cols)


def wide_table(tiles, cols, kinds):
    belongs = (np.arange(cols)[None, :] // TILE == np.arange(tiles)[:, None]).astype(np.float32)
    return np.tile(np.kron(np.eye(kinds, dtype=np.float32), belongs), (3, 1))


def per_device(
    gaussians,
    first_moment,
    second_moment,
    camera,
    target,
    block_list,
    block_count,
    tile_start,
    tile_end,
):
    views_n = lax.axis_size("view")
    bands_n = lax.axis_size("band")
    devices = views_n * bands_n
    blocks, comps, block_len = gaussians.shape
    list_len = block_list.shape[2]
    rows, cols = target.shape[2:]
    tiles = cols // TILE
    halves = block_len // 128
    geometry = (views_n, bands_n, blocks, list_len, rows, cols, block_len)

    across, first, second = smoothing_tables(rows, cols, 3)
    power = power_table(tiles, cols)
    shade = shade_table(tiles, cols).astype(BF16)
    quad = wide_table(tiles, cols, 6).astype(BF16)
    tone = wide_table(tiles, cols, 3).astype(BF16)
    vmem = pl.BlockSpec(memory_space=pltpu.VMEM)
    hbm = pl.BlockSpec(memory_space=pltpu.HBM)

    def by_comp(array):
        return jnp.transpose(array, (1, 0, 2))

    window = TILE_MOST * block_len
    tint_pad = up8(3 * halves + 1)
    basis_lanes = BASIS * blocks
    shape = jax.ShapeDtypeStruct((comps, blocks, block_len), F32)
    scalar = jax.ShapeDtypeStruct((1, 1), F32)
    kept = pltpu.VMEM(shape.shape, F32)
    gradient, params, one, two, mean_loss = pl.pallas_call(
        functools.partial(step_kernel, geometry),
        out_shape=(kept, kept, kept, kept, pltpu.HBM((1, 1), F32)),
        in_specs=[hbm] * 15,
        out_specs=(vmem,) * 4 + (hbm,),
        scratch_shapes=[
            pltpu.SMEM((1, 9), F32),
            pltpu.SMEM((1, 1, list_len), jnp.int32),
            pltpu.SMEM((1, 1, tiles), jnp.int32),
            pltpu.SMEM((1, 1, tiles), jnp.int32),
            pltpu.VMEM((1, 3, rows, cols), F32),
            pltpu.VMEM(across.shape, F32),
            pltpu.VMEM(first.shape, F32),
            pltpu.VMEM(second.shape, F32),
            pltpu.VMEM((second.shape[0], 3 * second.shape[1]), BF16),
            pltpu.VMEM((3 * cols, cols), BF16),
            pltpu.VMEM(power.shape, F32),
            pltpu.VMEM(shade.shape, BF16),
            pltpu.VMEM(quad.shape, BF16),
            pltpu.VMEM(tone.shape, BF16),
            pltpu.VMEM((views_n, 1, 128), F32),
            pltpu.VMEM((devices, 1, 128), F32),
            pltpu.VMEM((devices, 128), F32),
            pltpu.VMEM((1, 1), F32),
            pltpu.VMEM((128, 128), BF16),
            pltpu.VMEM((128, basis_lanes + 5 * 128), BF16),
            pltpu.VMEM((halves, GEO_COMPS, 3 * blocks, 128), BF16),
            pltpu.VMEM((halves, 3, basis_lanes, 3 * 128), BF16),
            pltpu.VMEM((3 * devices, basis_lanes), BF16),
            pltpu.VMEM((9 * devices, 128), BF16),
            pltpu.VMEM((9 * devices, 128), BF16),
            (pltpu.VMEM((devices, up8(RECORDS), 128), F32),) * halves,
            (pltpu.VMEM((devices, up8(RECORDS), 128), F32),) * halves,
            pltpu.VMEM((halves, TILE_MOST, RECORDS * tiles, 128), F32),
            pltpu.VMEM((devices, tint_pad, 128), F32),
            pltpu.VMEM((devices, tint_pad, 128), F32),
            (pltpu.VMEM((devices, up8(GEO_REC), 128), F32),) * halves,
            (pltpu.VMEM((devices, up8(GEO_REC), 128), F32),) * halves,
            pltpu.VMEM((2, 3, REACH, cols), F32),
            pltpu.VMEM((2, 3, REACH, cols), F32),
            pltpu.VMEM((2, 3, REACH, cols), F32),
            pltpu.VMEM((2, 3, REACH, cols), F32),
            pltpu.VMEM((7, window, cols), F32),
            pltpu.VMEM((window, rows // 8, 8, cols), F32),
            pltpu.VMEM((window, rows // 8, 8, cols), F32),
            pltpu.VMEM((3, window * 4, cols), F32),
            pltpu.SemaphoreType.DMA((3 + 2 * halves,)),
            pltpu.SemaphoreType.DMA((3 + 2 * halves,)),
            pltpu.SemaphoreType.DMA((2, 2)),
            pltpu.SemaphoreType.DMA((2, 2)),
            pltpu.SemaphoreType.DMA((16,)),
        ],
        compiler_params=pltpu.CompilerParams(
            collective_id=0, has_side_effects=True, vmem_limit_bytes=40 * 1024 * 1024
        ),
        name="render_step",
    )(
        *[
            pltpu.with_memory_space_constraint(array, pltpu.HBM)
            for array in (
                camera,
                block_list,
                tile_start,
                tile_end,
                target,
                by_comp(gaussians),
                by_comp(first_moment),
                by_comp(second_moment),
                across,
                first,
                second,
                power,
                shade,
                quad,
                tone,
            )
        ]
    )

    new_params, new_one, new_two, out_gradient, out_loss = pl.pallas_call(
        adam_kernel,
        out_shape=(shape, shape, shape, shape, scalar),
        in_specs=[vmem] * 4 + [hbm],
        out_specs=(hbm, hbm, hbm, hbm, hbm),
        scratch_shapes=[pltpu.VMEM((SHAPE_COMPS, blocks, block_len), F32)] * 3
        + [pltpu.SemaphoreType.DMA((5,))],
        compiler_params=pltpu.CompilerParams(vmem_limit_bytes=16 * 1024 * 1024),
        name="adam_step",
    )(gradient, params, one, two, pltpu.with_memory_space_constraint(mean_loss, pltpu.HBM))
    return (
        by_comp(new_params),
        by_comp(new_one),
        by_comp(new_two),
        out_loss.reshape(()),
        by_comp(out_gradient),
    )


def solution(mesh):
    return jax.shard_map(
        per_device,
        mesh=mesh,
        in_specs=(
            P(("view", "band"), None, None),
            P(("view", "band"), None, None),
            P(("view", "band"), None, None),
            P("view", None),
            P("view", None, "band", None),
            P("view", "band", None),
            P("view", "band"),
            P("view", "band", None),
            P("view", "band", None),
        ),
        out_specs=(
            P(("view", "band"), None, None),
            P(("view", "band"), None, None),
            P(("view", "band"), None, None),
            P(),
            P(("view", "band"), None, None),
        ),
        check_vma=False,
    )
```
